128 devices in a mesh: ctx: 32 (over y, x, core), head: 4 (over z).
Axes of the slice: x: 4, y: 4, z: 4, core: 2. Of those that a mesh axis runs over, the one named last changes fastest.
Arguments:
- prompt_values: bfloat16 [16384, 8192], P('ctx', 'head'), may hold values from -6 to 6
- prompt_gate: bfloat16 [16384, 8192], P('ctx', 'head'), may hold values from -6 to 6
- prompt_inject: bfloat16 [16384, 4, 256], P('ctx', 'head'), may hold values from -6 to 6
- prompt_read: bfloat16 [16384, 4, 256], P('ctx', 'head'), may hold values from -0.375 to 0.375
- prompt_step: float32 [128, 16384], P('head', 'ctx'), may hold values from -8 to 256
- decay_log: float32 [128], P('head'), may hold values from -10 to 0
- skip_gain: float32 [128], P('head'), may hold values from 0.5 to 1.5
- norm_weight: float32 [8192], P('head'), may hold values from 0.1 to 1.9
- out_weight: bfloat16 [8192, 4096], P('head'), may hold values from -0.0625 to 0.0625
- sample_values: bfloat16 [64, 16, 8192], P('ctx', None, 'head'), may hold values from -6 to 6
- sample_gate: bfloat16 [64, 16, 8192], P('ctx', None, 'head'), may hold values from -6 to 6
- sample_inject: bfloat16 [64, 16, 4, 256], P('ctx', None, 'head'), may hold values from -6 to 6
- sample_read: bfloat16 [64, 16, 4, 256], P('ctx', None, 'head'), may hold values from -0.375 to 0.375
- sample_step: float32 [128, 64, 16], P('head', 'ctx'), may hold values from -8 to 256
- sample_length: int32 [64], P('ctx'), may hold values from 1 to 16
Outputs:
- prompt_mixed: bfloat16 [4096, 16384], P('head', 'ctx')
- sample_mixed: bfloat16 [4096, 64], P('head', 'ctx')
The draws below stay inside these ranges and needn't reach their ends.
All inputs are finite; a program needn't handle non-finite values.
Results may differ from the reference program's by a relative error of at most 0.02.
Values may be sent and summed in bfloat16 or wider, within the bound.
No kernel may reach another device: no remote copies, remote signals or barrier semaphores. Data moves between devices by JAX's collectives and lax.ppermute only.
A program may use at most 192 MiB of HBM per device.

```python
import jax
import jax.numpy as jnp
from jax import lax

LOCAL_HEAD_COUNT = 128
HEAD_DIM = 64
STATE = 256
HEAD_GROUPS = 4
OUT_COLS = 4096
BLOCK = 128
SLEN = 16
TOK_DEV = 512
NTOK = 16384
SAMPLES = 64


def head_memory(key):
    base_key = jax.random.fold_in(key, 11)
    sorter, spreader = jax.random.split(base_key, 2)
    chooser = jax.random.uniform(sorter, (LOCAL_HEAD_COUNT,), jnp.float32)
    fast_share = 0.3
    middle_share = 0.5
    position = jax.random.uniform(spreader, (LOCAL_HEAD_COUNT,), jnp.float32)
    fast_memory = 30.0 * (5.0 / 3.0) ** position
    middle_memory = 50.0 * (2.5 * NTOK / 50.0) ** position
    slow_memory = 2.5 * NTOK * 2.4 ** position
    return jnp.where(chooser < fast_share, fast_memory, jnp.where(chooser < middle_share, middle_memory, slow_memory))


def spike_mask(key):
    places = jax.random.randint(jax.random.fold_in(key, 23), (HEAD_GROUPS, 2), 0, NTOK)
    positions = jnp.arange(NTOK)
    return jnp.any(positions[:, None, None] == places[None], axis=2)


def draw_decay_log(key, part):
    return (-0.5 * jnp.log(head_memory(key))).astype(jnp.float32)


def draw_prompt_step(key, part):
    memory = head_memory(key)
    decay_velocity = memory ** (-0.5)
    token_key, device_key, keeper_key = jax.random.split(jax.random.fold_in(key, 37), 3)
    token_factor = jnp.exp(jax.random.uniform(token_key, (LOCAL_HEAD_COUNT, NTOK), jnp.float32, -0.7, 0.7))
    device_factor = jnp.exp(jax.random.uniform(device_key, (LOCAL_HEAD_COUNT, NTOK // TOK_DEV), jnp.float32, -0.7, 0.7))
    stable_state = decay_velocity[:, None] * token_factor * jnp.repeat(device_factor, TOK_DEV, axis=1)
    retained_fraction = jax.random.uniform(keeper_key, (LOCAL_HEAD_COUNT, NTOK), jnp.float32, 0.5, 0.8)
    spike_steps = jnp.minimum(-jnp.log(retained_fraction) / decay_velocity[:, None], 250.0)
    inside_spike = jnp.repeat(spike_mask(key).T, LOCAL_HEAD_COUNT // HEAD_GROUPS, axis=0)
    selected_rows = jnp.where(inside_spike, spike_steps, stable_state)
    return (selected_rows + jnp.log(-jnp.expm1(-selected_rows))).astype(jnp.float32)


def draw_sample_step(key, part):
    memory = head_memory(key)
    token_factor = jnp.exp(jax.random.uniform(jax.random.fold_in(key, 53), (LOCAL_HEAD_COUNT, SAMPLES, SLEN), jnp.float32, -0.7, 0.7))
    stable_state = (memory ** (-0.5))[:, None, None] * token_factor
    return (stable_state + jnp.log(-jnp.expm1(-stable_state))).astype(jnp.float32)


def draw_prompt_inject(key, part):
    noise_key = jax.random.fold_in(key, 41)
    raw_noise = jnp.clip(jax.random.normal(noise_key, (NTOK, HEAD_GROUPS, STATE), jnp.float32), -6.0, 6.0)
    attenuation = jnp.where(spike_mask(key)[:, :, None], 0.02, 1.0)
    return (raw_noise * attenuation).astype(jnp.bfloat16)


def touch_ends(array, stream_key, smallest, high):
    spot = [jax.random.randint(jax.random.fold_in(stream_key, axis), (), 0, length) for axis, length in enumerate(array.shape)]
    main_axis = array.shape.index(max(array.shape))
    next_to = spot[:main_axis] + [(spot[main_axis] + 1) % array.shape[main_axis]] + spot[main_axis + 1:]
    return array.at[tuple(spot)].set(smallest).at[tuple(next_to)].set(high)


def steps_of(stream_key, extent, pieces, low, high):
    factor_of, own = 1.0, jax.random.fold_in(stream_key, 6)
    for dim, parts in pieces:
        steps = jnp.exp(jax.random.uniform(jax.random.fold_in(own, dim), (parts,), jnp.float32, low / len(pieces), high / len(pieces)))
        factor_of = factor_of * jnp.repeat(steps, extent[dim] // parts).reshape([-1 if axis == dim else 1 for axis in range(len(extent))])
    return factor_of


def gaussian(stream_key, shape, deviation, reach, pieces=(), dtype=jnp.bfloat16):
    gain = steps_of(stream_key, shape, pieces, -0.22, 0.18) if pieces else 1.0
    array = jax.random.normal(stream_key, shape, jnp.float32) * deviation * gain
    return jnp.minimum(jnp.maximum(array, -reach), reach).astype(dtype)


def setup_inputs(seed: int = 0) -> dict:
    splits = jax.random.split(jax.random.key(seed), 16)
    return {
        "prompt_values": gaussian(splits[0], (NTOK, LOCAL_HEAD_COUNT * HEAD_DIM), 1.0, 6.0, ((0, 32), (1, 4))),
        "prompt_gate": gaussian(splits[1], (NTOK, LOCAL_HEAD_COUNT * HEAD_DIM), 1.0, 6.0, ((0, 32), (1, 4))),
        "prompt_inject": draw_prompt_inject(jax.random.fold_in(splits[15], 71), 0),
        "prompt_read": gaussian(splits[3], (NTOK, HEAD_GROUPS, STATE), STATE ** -0.5, 0.375, ((0, 32), (1, 4))),
        "prompt_step": draw_prompt_step(jax.random.fold_in(splits[15], 71), 0),
        "decay_log": draw_decay_log(jax.random.fold_in(splits[15], 71), 0),
        "skip_gain": jnp.clip(0.5 + 1.0 * jax.random.uniform(splits[6], (LOCAL_HEAD_COUNT,), jnp.float32) ** steps_of(splits[6], (LOCAL_HEAD_COUNT,), ((0, 4),), -0.2, 0.2), 0.5, 1.5),
        "norm_weight": jnp.clip(1.0 + 0.18 * jax.random.normal(splits[7], (LOCAL_HEAD_COUNT * HEAD_DIM,), jnp.float32), 0.1, 1.9),
        "out_weight": gaussian(splits[8], (LOCAL_HEAD_COUNT * HEAD_DIM, OUT_COLS), (LOCAL_HEAD_COUNT * HEAD_DIM) ** -0.5, 0.0625, ((0, 4),)),
        "sample_values": gaussian(splits[9], (SAMPLES, SLEN, LOCAL_HEAD_COUNT * HEAD_DIM), 1.0, 6.0, ((0, 32), (2, 4))),
        "sample_gate": gaussian(splits[10], (SAMPLES, SLEN, LOCAL_HEAD_COUNT * HEAD_DIM), 1.0, 6.0, ((0, 32), (2, 4))),
        "sample_inject": gaussian(splits[11], (SAMPLES, SLEN, HEAD_GROUPS, STATE), 1.0, 6.0, ((0, 32), (2, 4))),
        "sample_read": gaussian(splits[12], (SAMPLES, SLEN, HEAD_GROUPS, STATE), STATE ** -0.5, 0.375, ((0, 32), (2, 4))),
        "sample_step": draw_sample_step(jax.random.fold_in(splits[15], 71), 0),
        "sample_length": touch_ends(jax.random.randint(splits[14], (SAMPLES,), 1, SLEN + 1), jax.random.fold_in(splits[14], 1), 1, SLEN).astype(jnp.int32),
    }


full_precision = lax.Precision.HIGHEST

def block_terms(values, inject, readout, steps, decay_rate):
    length = values.shape[0]
    log_decay = steps * decay_rate[:, None]
    running = jnp.cumsum(log_decay, axis=1)
    scores = jnp.dot(readout.astype(jnp.float32), inject.astype(jnp.float32).T, precision=full_precision)
    causal = jnp.arange(length)[:, None] >= jnp.arange(length)[None, :]
    gap_logs = jnp.where(causal[None], running[:, :, None] - running[:, None, :], 0.0)
    mixing = jnp.where(causal[None], scores[None] * jnp.exp(gap_logs) * steps[:, None, :], 0.0).astype(jnp.bfloat16)
    local_out = jnp.einsum('hts,shp->thp', mixing.astype(jnp.float32), values.astype(jnp.float32), precision=full_precision)
    to_end = jnp.exp(running[:, -1:] - running) * steps
    weighted = (to_end[:, :, None] * inject.astype(jnp.float32)[None]).astype(jnp.bfloat16)
    local_state = jnp.einsum('shp,hsn->hpn', values.astype(jnp.float32), weighted.astype(jnp.float32), precision=full_precision)
    return (local_out, local_state, running)

def group_block(values, inject, readout, steps, decay_rate, carry_state):
    local_out, local_state, running = block_terms(values, inject, readout, steps, decay_rate)
    carried = jnp.einsum('tn,hpn->thp', readout.astype(jnp.float32), carry_state, precision=full_precision)
    carried = carried * jnp.exp(running).T[:, :, None]
    next_state = jnp.exp(running[:, -1])[:, None, None] * carry_state + local_state
    return (local_out + carried, next_state, running)

def finish(outputs, values, gate, skip_gain, norm_weight, groups):
    row_count = values.shape[0]
    with_skip = outputs + skip_gain[None, :, None] * values.reshape(row_count, skip_gain.shape[0], -1).astype(jnp.float32)
    gated_out = with_skip.reshape(row_count, -1) * jax.nn.silu(gate.astype(jnp.float32))
    grouped = gated_out.reshape(row_count, groups, -1)
    inverse_rms = lax.rsqrt(lax.optimization_barrier(jnp.mean(grouped * grouped, axis=2, keepdims=True)) + 1e-05)
    return ((grouped * inverse_rms).reshape(row_count, -1) * norm_weight[None]).astype(jnp.bfloat16)

def reference(prompt_values, prompt_gate, prompt_inject, prompt_read, prompt_step, decay_log, skip_gain, norm_weight, out_weight, sample_values, sample_gate, sample_inject, sample_read, sample_step, sample_length):
    per_group = LOCAL_HEAD_COUNT // HEAD_GROUPS
    blocks = NTOK // BLOCK
    decay_rate = (-jnp.exp(decay_log)).reshape(HEAD_GROUPS, per_group)
    steps = jax.nn.softplus(prompt_step).reshape(HEAD_GROUPS, per_group, blocks, BLOCK).transpose(2, 0, 1, 3)
    values = prompt_values.reshape(blocks, BLOCK, HEAD_GROUPS, per_group, HEAD_DIM)
    inject = prompt_inject.reshape(blocks, BLOCK, HEAD_GROUPS, STATE)
    readout = prompt_read.reshape(blocks, BLOCK, HEAD_GROUPS, STATE)
    grouped_block = jax.vmap(group_block, in_axes=(1, 1, 1, 0, 0, 0), out_axes=(1, 0, 0))

    def advance(carry_state, block_data):
        block_values, block_inject, block_readout, block_steps = block_data
        block_out, next_state, running = grouped_block(block_values, block_inject, block_readout, block_steps, decay_rate, carry_state)
        return (next_state, block_out)
    start_state = jnp.zeros((HEAD_GROUPS, per_group, HEAD_DIM, STATE), jnp.float32)
    final_state, outputs = lax.scan(advance, start_state, (values, inject, readout, steps))
    outputs = outputs.reshape(NTOK, LOCAL_HEAD_COUNT, HEAD_DIM)
    normed = finish(outputs, prompt_values, prompt_gate, skip_gain, norm_weight, HEAD_GROUPS)
    weight_full = out_weight.astype(jnp.float32)
    prompt_mixed = jnp.dot(normed.astype(jnp.float32), weight_full, precision=full_precision).T.astype(jnp.bfloat16)
    sample_steps = jax.nn.softplus(sample_step).reshape(HEAD_GROUPS, per_group, SAMPLES, SLEN).transpose(2, 0, 1, 3)
    sample_vals = sample_values.reshape(SAMPLES, SLEN, HEAD_GROUPS, per_group, HEAD_DIM)
    per_sample = jax.vmap(grouped_block, in_axes=(0, 0, 0, 0, None, None), out_axes=(0, 0, 0))
    sample_out = per_sample(sample_vals, sample_inject, sample_read, sample_steps, decay_rate, final_state)[0]
    sample_out = sample_out.reshape(SAMPLES * SLEN, LOCAL_HEAD_COUNT, HEAD_DIM)
    sample_normed = finish(sample_out, sample_values.reshape(SAMPLES * SLEN, -1), sample_gate.reshape(SAMPLES * SLEN, -1), skip_gain, norm_weight, HEAD_GROUPS)
    onehot = (jnp.arange(SLEN)[None, :] == (sample_length - 1)[:, None]).astype(jnp.float32)
    picked = lax.optimization_barrier(jnp.sum(onehot[:, :, None] * sample_normed.reshape(SAMPLES, SLEN, -1).astype(jnp.float32), axis=1)).astype(jnp.bfloat16)
    sample_mixed = jnp.dot(picked.astype(jnp.float32), weight_full, precision=full_precision).T.astype(jnp.bfloat16)
    return (prompt_mixed, sample_mixed)
```

```python
import jax
import jax.numpy as jnp
from jax import lax
from jax.experimental import pallas as pl
from jax.experimental.pallas import tpu as pltpu
from jax.sharding import Mesh
from jax.sharding import PartitionSpec as P

HEADS = 32
HEAD_DIM = 64
STATE = 256
BLOCK = 128
SLEN = 16
TOK = 512
CH = HEADS * HEAD_DIM
COLS = 4096
PIECE = 512
ROWS = 144
CTX = ("y", "x", "core")
F32 = jnp.float32
BF16 = jnp.bfloat16
EXACT = lax.Precision.HIGHEST
CHUNK = 256
MB = 1 << 20


def softplus(v):
    return jnp.maximum(v, 0.0) + jnp.log1p(jnp.exp(-jnp.abs(v)))


def iota(shape, dim):
    return lax.broadcasted_iota(jnp.int32, shape, dim)


def column(row):
    n = row.shape[1]
    square = jnp.broadcast_to(row, (n, n))
    return jnp.sum(jnp.where(iota((n, n), 0) == iota((n, n), 1), square, 0.0), axis=1, keepdims=True)


def tokens_first(x):
    pad = jnp.zeros((128 - x.shape[0], x.shape[1]), F32)
    return jnp.transpose(jnp.concatenate([x, pad], axis=0))


def per_pair(columns, pair, shape, low):
    first = jnp.broadcast_to(columns[:, 2 * pair : 2 * pair + 1], shape)
    second = jnp.broadcast_to(columns[:, 2 * pair + 1 : 2 * pair + 2], shape)
    return jnp.where(low, first, second)


def three_parts(x):
    hi = x.astype(BF16).astype(F32)
    mid = (x - hi).astype(BF16).astype(F32)
    lo = (x - hi - mid).astype(BF16).astype(F32)
    return hi, mid, lo


def decay_of(tail):
    return tail[8:9] + tail[9:10] + tail[10:11]


def with_decay(tail, decay):
    row = iota((16, 128), 0)
    hi, mid, lo = three_parts(decay)
    tail = jnp.where(row == 8, hi, tail)
    tail = jnp.where(row == 9, mid, tail)
    return jnp.where(row == 10, lo, tail)


def end_state_kernel(meta, step_ref, decay_ref, values_ref, inject_ref, read_ref, keep_ref, send_ref, scaled):
    core = meta[0]
    step = softplus(step_ref[...])
    logs = step * -jnp.exp(column(decay_ref[...]))
    later = (iota((BLOCK, BLOCK), 0) > iota((BLOCK, BLOCK), 1)).astype(F32)
    after = jnp.zeros((HEADS, 1), F32)
    parts = []
    for b in reversed(range(TOK // BLOCK)):
        here = logs[:, b * BLOCK : (b + 1) * BLOCK]
        parts.append(jnp.dot(here, later, precision=EXACT, preferred_element_type=F32) + after)
        after = after + jnp.sum(here, axis=1, keepdims=True)
    weight = tokens_first(jnp.exp(jnp.concatenate(parts[::-1], axis=1)) * step)
    total = tokens_first(jnp.broadcast_to(jnp.exp(after), (HEADS, 128)))[0:8]
    inject_t = jnp.transpose(inject_ref[...].astype(F32)).astype(BF16)
    low = iota((TOK, 128), 1) < HEAD_DIM
    low_row = iota((8, 128), 1) < HEAD_DIM
    row = iota((16, 128), 0)
    tails = []
    for half in range(2):
        lanes = slice(half * 128, (half + 1) * 128)
        tail = jnp.zeros((16, 128), F32)
        for s in range(2):
            last = iota((SLEN, 128), 0) == meta[1 + s] - 1
            picked = jnp.sum(jnp.where(last, read_ref[s, :, lanes].astype(F32), 0.0), axis=0, keepdims=True)
            tail = jnp.where(row == 2 * core + s, picked, tail)
        tails.append(tail)
    for half in range(2):
        for q in range(8):
            pair = half * 8 + q
            lanes = slice(pair * 128, (pair + 1) * 128)
            w = per_pair(weight, pair, (TOK, 128), low)
            scaled[:, q * 128 : (q + 1) * 128] = (values_ref[:, lanes].astype(F32) * w).astype(BF16)
        state = jnp.dot(inject_t, scaled[...], preferred_element_type=F32).astype(BF16)

        def put(out_ref, half=half, state=state):
            for q in range(8):
                decay = per_pair(total, half * 8 + q, (8, 128), low_row)[0:1]
                for n in range(2):
                    out_ref[2 * q + n, 0:128, :] = state[n * 128 : (n + 1) * 128, q * 128 : (q + 1) * 128]
                    out_ref[2 * q + n, 128:ROWS, :] = with_decay(tails[n], decay).astype(BF16)

        @pl.when(core == half)
        def _(put=put):
            put(keep_ref)

        @pl.when(core != half)
        def _(put=put):
            put(send_ref)


def join_cores_kernel(meta, own_ref, sib_ref, out_ref):
    first = meta[0] == 0
    row = iota((16, 128), 0)
    for k in range(16):
        own_tail = own_ref[k, 128:ROWS, :].astype(F32)
        sib_tail = sib_ref[k, 128:ROWS, :].astype(F32)
        own_decay, sib_decay = decay_of(own_tail), decay_of(sib_tail)
        own_weight = jnp.where(first, sib_decay, 1.0)
        sib_weight = jnp.where(first, 1.0, own_decay)
        out_ref[k, 0:128, :] = (
            own_ref[k, 0:128, :].astype(F32) * own_weight + sib_ref[k, 0:128, :].astype(F32) * sib_weight
        ).astype(BF16)
        tail = jnp.where(row < 8, own_tail + sib_tail, 0.0)
        out_ref[k, 128:ROWS, :] = with_decay(tail, own_decay * sib_decay).astype(BF16)


def prefix_kernel(in_ref, out_ref):
    state = jnp.zeros((128, 128), F32)
    for i in range(16):
        out_ref[i, 0:128, :] = state.astype(BF16)
        decay = decay_of(in_ref[i, 128:ROWS, :].astype(F32))
        state = state * decay + in_ref[i, 0:128, :].astype(F32)
    final = state.astype(BF16)
    for i in range(16):
        out_ref[i, 128:ROWS, :] = jnp.dot(
            in_ref[i, 128:ROWS, :], final, preferred_element_type=F32
        ).astype(BF16)


def split_cores_kernel(meta, back_ref, own_ref, sib_ref, mine_ref, send_ref):
    first = meta[0] == 0
    for k in range(16):
        q, n = k // 2, k % 2
        arrived = back_ref[k, 0:128, :].astype(F32)
        own_decay = decay_of(own_ref[k, 128:ROWS, :].astype(F32))
        sib_decay = decay_of(sib_ref[k, 128:ROWS, :].astype(F32))
        decay = jnp.where(first, own_decay, sib_decay)
        state = jnp.where(first, own_ref[k, 0:128, :].astype(F32), sib_ref[k, 0:128, :].astype(F32))
        second = arrived * decay + state
        mine_ref[n * 128 : (n + 1) * 128, q * 128 : (q + 1) * 128] = jnp.where(first, arrived, second).astype(BF16)
        send_ref[k, 0:128, :] = jnp.where(first, second, arrived).astype(BF16)
        send_ref[k, 128:ROWS, :] = back_ref[k, 128:ROWS, :]
    for q in range(8):
        mine_ref[256:272, q * 128 : (q + 1) * 128] = (
            back_ref[2 * q, 128:ROWS, :].astype(F32) + back_ref[2 * q + 1, 128:ROWS, :].astype(F32)
        ).astype(BF16)


def local_kernel(
    step_ref, decay_ref, skip_ref, values_ref, gate_ref, inject_ref, read_ref,
    scaled_ref, gain_ref, state, before, ends, weighted, carried,
):
    first = pl.program_id(0) == 0

    @pl.when(first)
    def _():
        state[...] = jnp.zeros_like(state)
        before[...] = jnp.ones_like(before)

    step = softplus(step_ref[...])
    logs = step * -jnp.exp(column(decay_ref[...]))
    upto = (iota((BLOCK, BLOCK), 0) <= iota((BLOCK, BLOCK), 1)).astype(F32)
    running = jnp.dot(logs, upto, precision=EXACT, preferred_element_type=F32)
    running_t = tokens_first(running)
    step_t = tokens_first(step)
    read = read_ref[...]
    inject = inject_ref[...]
    inject_t = jnp.transpose(inject.astype(F32)).astype(BF16)
    scores = jnp.dot(read, inject_t, preferred_element_type=F32)
    carried[...] = jnp.dot(read, state[...].astype(BF16), preferred_element_type=F32)
    causal = iota((BLOCK, BLOCK), 0) >= iota((BLOCK, BLOCK), 1)
    low = iota((BLOCK, 128), 1) < HEAD_DIM
    for pair in range(16):
        lanes = slice(pair * 128, (pair + 1) * 128)
        mixing = []
        spread = []
        for h in (2 * pair, 2 * pair + 1):
            mine = jnp.broadcast_to(running_t[:, h : h + 1], (BLOCK, BLOCK))
            gap = jnp.where(causal, mine - running[h : h + 1, :], -1e30)
            mixing.append((scores * jnp.exp(gap)).astype(BF16))
            spread.append(mine)
        now = jnp.where(low, spread[0], spread[1])
        grown = jnp.exp(now)
        values = values_ref[:, lanes].astype(F32)
        stepped = values * per_pair(step_t, pair, (BLOCK, 128), low)
        diagonal = jnp.concatenate([jnp.where(low, stepped, 0.0), jnp.where(low, 0.0, stepped)], axis=0)
        local = jnp.dot(
            jnp.concatenate(mixing, axis=1), diagonal.astype(BF16), preferred_element_type=F32
        )
        out = local + carried[:, lanes] * grown + skip_ref[:, lanes] * values
        gate = gate_ref[:, lanes].astype(F32)
        gate = gate / (1.0 + jnp.exp(-gate))
        scaled_ref[:, lanes] = (out * gate).astype(BF16)
        gain_ref[:, lanes] = (gate * grown * before[0:1, lanes]).astype(BF16)
        end = now[BLOCK - 1 : BLOCK, :]
        weighted[:, lanes] = (stepped * jnp.exp(end - now)).astype(BF16)
        ends[0:1, lanes] = jnp.exp(end)
    state[...] = state[...] * ends[0:1, :] + jnp.dot(inject_t, weighted[...], preferred_element_type=F32)
    before[0:1, :] = before[0:1, :] * ends[0:1, :]


def sample_kernel(
    meta, step_ref, decay_ref, skip_ref, values_ref, gate_ref, inject_ref, read_ref, local_ref, grown_ref, gate_out_ref
):
    rate = -jnp.exp(column(decay_ref[...]))
    row = iota((16, CH), 0)
    spread = (iota((128, CH), 1) // HEAD_DIM == iota((128, CH), 0)).astype(F32)
    local_all = jnp.zeros((16, CH), F32)
    grown_all = jnp.zeros((16, CH), F32)
    gate_all = jnp.zeros((16, CH), F32)
    for s in range(2):
        last = meta[1 + s] - 1
        step = softplus(step_ref[s])
        logs = step * rate
        pad = jnp.zeros((HEADS, 128 - SLEN), F32)
        step_t = tokens_first(jnp.concatenate([step, pad], axis=1))[0:SLEN]
        logs_t = tokens_first(jnp.concatenate([logs, pad], axis=1))[0:SLEN]
        place = iota((SLEN, 128), 0)
        logs_t = jnp.where(place <= last, logs_t, 0.0)
        gap = jnp.zeros((SLEN, 128), F32)
        for k in range(SLEN):
            gap = gap + jnp.where(place < k, logs_t[k : k + 1], 0.0)
        whole = jnp.sum(logs_t, axis=0, keepdims=True)
        place_wide = iota((SLEN, STATE), 0)
        read = jnp.sum(jnp.where(place_wide == last, read_ref[s].astype(F32), 0.0), axis=0, keepdims=True)
        scores = jnp.sum(inject_ref[s].astype(F32) * read, axis=1, keepdims=True)
        weight = jnp.where(place <= last, scores * jnp.exp(gap) * step_t, 0.0)
        both = jnp.concatenate([weight, jnp.broadcast_to(jnp.exp(whole), (8, 128))], axis=0)
        wide = jnp.dot(both, spread, precision=EXACT, preferred_element_type=F32)
        values = values_ref[s].astype(F32)
        at_last = iota((SLEN, CH), 0) == last
        picked = jnp.sum(jnp.where(at_last, values, 0.0), axis=0, keepdims=True)
        gate = jnp.sum(jnp.where(at_last, gate_ref[s].astype(F32), 0.0), axis=0, keepdims=True)
        local = jnp.sum(wide[0:SLEN] * values, axis=0, keepdims=True) + skip_ref[...] * picked
        local_all = jnp.where(row == s, local, local_all)
        grown_all = jnp.where(row == s, wide[SLEN : SLEN + 1], grown_all)
        gate_all = jnp.where(row == s, gate / (1.0 + jnp.exp(-gate)), gate_all)
    local_ref[...] = local_all
    grown_ref[...] = grown_all
    gate_out_ref[...] = gate_all


def normalize(gated, weight):
    mean = jnp.sum(gated * gated, axis=1, keepdims=True) * (1.0 / CH)
    return (gated * lax.rsqrt(mean + 1e-05) * weight).astype(BF16)


def project(j, normed, weight_ref, first_ref, second_ref):
    out = jnp.dot(normed, weight_ref[...], preferred_element_type=F32).astype(BF16)

    @pl.when(j < 2)
    def _():
        first_ref[0] = out

    @pl.when(j >= 2)
    def _():
        second_ref[0] = out


def chunk_one_kernel(
    meta, mine_ref, theirs_ref, read_ref, scaled_ref, gain_ref, norm_ref, weight_ref,
    first_ref, second_ref, normed_ref, state_ref,
):
    j = pl.program_id(0)

    @pl.when(j == 0)
    def _():
        core = meta[0]
        own = pl.multiple_of(core * 1024, 1024)
        state_ref[:, pl.ds(own, 1024)] = mine_ref[...]
        for q in range(8):
            at = pl.multiple_of((1 - core) * 1024 + q * 128, 128)
            for n in range(2):
                state_ref[n * 128 : (n + 1) * 128, pl.ds(at, 128)] = theirs_ref[2 * q + n, 0:128, :]
            state_ref[256:272, pl.ds(at, 128)] = (
                theirs_ref[2 * q, 128:ROWS, :].astype(F32) + theirs_ref[2 * q + 1, 128:ROWS, :].astype(F32)
            ).astype(BF16)
        arrived = jnp.dot(read_ref[...], state_ref[0:256, :], preferred_element_type=F32)
        gated = scaled_ref[...].astype(F32) + arrived * gain_ref[...].astype(F32)
        normed_ref[...] = normalize(gated, norm_ref[...])

    project(j, normed_ref[...], weight_ref, first_ref, second_ref)


def chunk_two_kernel(
    meta, state_ref, read_ref, scaled_ref, gain_ref, norm_ref, local_ref, grown_ref, gate_ref, weight_ref,
    first_ref, second_ref, normed_ref,
):
    j = pl.program_id(0)

    @pl.when(j == 0)
    def _():
        arrived = jnp.dot(read_ref[...], state_ref[0:256, :], preferred_element_type=F32)
        gated = scaled_ref[...].astype(F32) + arrived * gain_ref[...].astype(F32)
        normed_ref[0:CHUNK, :] = normalize(gated, norm_ref[...])
        readings = state_ref[256:272, :].astype(F32)
        moved = jnp.concatenate([readings[2:16], readings[0:2]], axis=0)
        readings = jnp.where(meta[0] == 0, readings, moved)
        sampled = (local_ref[...] + readings * grown_ref[...]) * gate_ref[...]
        normed_ref[CHUNK : CHUNK + 16, :] = normalize(sampled, norm_ref[...])

    project(j, normed_ref[...], weight_ref, first_ref, second_ref)


def rest_kernel(meta, normed_ref, weight_ref, out_ref):
    out_ref[0] = jnp.dot(normed_ref[...], weight_ref[...], preferred_element_type=F32).astype(BF16)


def finish_kernel(*refs):
    ins, out_ref, sample_ref = refs[:-2], refs[-2], refs[-1]
    for c in range(2):
        rest, ra, rb, sa, sb = ins[5 * c : 5 * c + 5]
        for half, (own, near, far) in enumerate(((0, ra, sa), (2, rb, sb))):
            total = rest[own].astype(F32) + near[0].astype(F32) + far[...].astype(F32)
            rows = slice(half * PIECE, (half + 1) * PIECE)
            out_ref[rows, c * CHUNK : (c + 1) * CHUNK] = jnp.transpose(total[0:CHUNK]).astype(BF16)
            if c == 1:
                extra = jnp.concatenate([total[CHUNK : CHUNK + 16], jnp.zeros((112, PIECE), F32)], axis=0)
                sample_ref[rows, :] = jnp.transpose(extra)[:, 0:2].astype(BF16)


def params(limit=56):
    return pltpu.CompilerParams(vmem_limit_bytes=limit * MB)


SMEM = pl.BlockSpec(memory_space=pltpu.SMEM)
VMEM = pl.BlockSpec(memory_space=pltpu.VMEM)


def shape(dims, dtype=BF16):
    return jax.ShapeDtypeStruct(dims, dtype)


def swap(x, step):
    return lax.ppermute(x, "head", [(i, i ^ step) for i in range(4)])


def per_device(
    prompt_values, prompt_gate, prompt_inject, prompt_read, prompt_step, decay_log, skip_gain, norm_weight, out_weight,
    sample_values, sample_gate, sample_inject, sample_read, sample_step, sample_length,
):
    core = lax.axis_index("core")
    z = lax.axis_index("head")
    flip = [(z ^ k) * 2 for k in range(4)]
    order = [flip[1], flip[2], flip[3] + 1, flip[2] + 1, flip[0], flip[3], flip[0] + 1, flip[1] + 1]
    meta = jnp.concatenate([core[None], sample_length, jnp.stack(order)]).astype(jnp.int32)
    inject = prompt_inject.reshape(TOK, STATE)
    read = prompt_read.reshape(TOK, STATE)
    decay = decay_log.reshape(1, HEADS)
    skip = jnp.repeat(skip_gain, HEAD_DIM).reshape(1, CH)
    norm = norm_weight.reshape(1, CH)
    s_read = sample_read.reshape(2, SLEN, STATE)
    s_inject = sample_inject.reshape(2, SLEN, STATE)

    keep, send = pl.pallas_call(
        end_state_kernel,
        out_shape=(shape((16, ROWS, 128)),) * 2,
        in_specs=[SMEM] + [VMEM] * 5,
        out_specs=(VMEM, VMEM),
        scratch_shapes=[pltpu.VMEM((TOK, 1024), BF16)],
        compiler_params=params(),
        name="end_state",
    )(meta, prompt_step, decay, prompt_values, inject, s_read)
    sibling = lax.ppermute(send, "core", [(0, 1), (1, 0)])
    joined = pl.pallas_call(
        join_cores_kernel,
        out_shape=shape((16, ROWS, 128)),
        in_specs=[SMEM, VMEM, VMEM],
        out_specs=VMEM,
        compiler_params=params(16),
        name="join_cores",
    )(meta, keep, sibling)
    joined, step_b = lax.optimization_barrier((joined, prompt_step))
    slices = lax.all_to_all(joined, ("y", "x"), 0, 0, tiled=True)

    row = lambda width: pl.BlockSpec((1, width), lambda b: (0, 0))
    tokens = lambda width: pl.BlockSpec((BLOCK, width), lambda b: (b, 0))
    scaled, gain = pl.pallas_call(
        local_kernel,
        grid=(TOK // BLOCK,),
        out_shape=(shape((TOK, CH)),) * 2,
        in_specs=[
            pl.BlockSpec((HEADS, BLOCK), lambda b: (0, b)), row(HEADS), row(CH),
            tokens(CH), tokens(CH), tokens(STATE), tokens(STATE),
        ],
        out_specs=(tokens(CH), tokens(CH)),
        scratch_shapes=[
            pltpu.VMEM((STATE, CH), F32), pltpu.VMEM((8, CH), F32), pltpu.VMEM((8, CH), F32),
            pltpu.VMEM((BLOCK, CH), BF16), pltpu.VMEM((BLOCK, CH), F32),
        ],
        compiler_params=params(),
        name="local_outputs",
    )(step_b, decay, skip, prompt_values, prompt_gate, inject, read)
    s_local, s_grown, s_gate = pl.pallas_call(
        sample_kernel,
        out_shape=(shape((16, CH), F32),) * 3,
        in_specs=[SMEM] + [VMEM] * 7,
        out_specs=(VMEM,) * 3,
        compiler_params=params(16),
        name="sample_outputs",
    )(meta, sample_step.transpose(1, 0, 2), decay, skip, sample_values, sample_gate, s_inject, s_read)

    prefix = pl.pallas_call(
        prefix_kernel,
        out_shape=shape((16, ROWS, 128)),
        in_specs=[VMEM],
        out_specs=VMEM,
        compiler_params=params(16),
        name="prefix",
    )(slices)
    back = lax.all_to_all(prefix, ("y", "x"), 0, 0, tiled=True)
    mine, send = pl.pallas_call(
        split_cores_kernel,
        out_shape=(shape((272, 1024)), shape((16, ROWS, 128))),
        in_specs=[SMEM] + [VMEM] * 3,
        out_specs=(VMEM, VMEM),
        compiler_params=params(16),
        name="split_cores",
    )(meta, back, keep, sibling)
    theirs = lax.ppermute(send, "core", [(0, 1), (1, 0)])

    def whole(*dims):
        return pl.BlockSpec(dims, lambda j, m: (0,) * len(dims))

    def chunk(width, c):
        return pl.BlockSpec((CHUNK, width), lambda j, m: (c, 0))

    def weight(base):
        return pl.BlockSpec((CH, PIECE), lambda j, m: (0, m[3 + base + j]))

    def sent(rows):
        return (
            pl.BlockSpec((1, rows, PIECE), lambda j, m: (jnp.minimum(j, 1), 0, 0)),
            pl.BlockSpec((1, rows, PIECE), lambda j, m: (jnp.maximum(j - 2, 0), 0, 0)),
        )

    first_1, second_1, normed_1, state = pl.pallas_call(
        chunk_one_kernel,
        grid_spec=pltpu.PrefetchScalarGridSpec(
            num_scalar_prefetch=1,
            grid=(4,),
            in_specs=[
                whole(272, 1024), whole(16, ROWS, 128), chunk(STATE, 0), chunk(CH, 0), chunk(CH, 0), whole(1, CH), weight(0),
            ],
            out_specs=(*sent(CHUNK), whole(CHUNK, CH), whole(272, CH)),
        ),
        out_shape=(
            shape((2, CHUNK, PIECE)), shape((2, CHUNK, PIECE)), shape((CHUNK, CH)), shape((272, CH)),
        ),
        compiler_params=params(),
        name="chunk_one",
    )(meta, mine, theirs, read, scaled, gain, norm, out_weight)
    near_1 = lax.optimization_barrier((swap(first_1, 1), swap(second_1, 3)))

    def rest(normed, name):
        rows = normed.shape[0]
        return pl.pallas_call(
            rest_kernel,
            grid_spec=pltpu.PrefetchScalarGridSpec(
                num_scalar_prefetch=1,
                grid=(4,),
                in_specs=[whole(rows, CH), weight(4)],
                out_specs=pl.BlockSpec((1, rows, PIECE), lambda j, m: (j, 0, 0)),
            ),
            out_shape=shape((4, rows, PIECE)),
            compiler_params=params(),
            name=name,
        )(meta, normed, out_weight)

    rows = CHUNK + 16
    first_2, second_2, normed_2 = pl.pallas_call(
        chunk_two_kernel,
        grid_spec=pltpu.PrefetchScalarGridSpec(
            num_scalar_prefetch=1,
            grid=(4,),
            in_specs=[
                whole(272, CH), chunk(STATE, 1), chunk(CH, 1), chunk(CH, 1), whole(1, CH),
                whole(16, CH), whole(16, CH), whole(16, CH), weight(0),
            ],
            out_specs=(*sent(rows), whole(rows, CH)),
        ),
        out_shape=(shape((2, rows, PIECE)), shape((2, rows, PIECE)), shape((rows, CH))),
        compiler_params=params(),
        name="chunk_two",
    )(meta, state, read, scaled, gain, norm, s_local, s_grown, s_gate, out_weight)
    near_2 = lax.optimization_barrier((swap(first_2, 1), swap(second_2, 3)))
    rest_1 = rest(normed_1, "rest_one")
    rest_2 = rest(normed_2, "rest_two")

    def onward(rest, near):
        a = (rest[1].astype(F32) + near[0][1].astype(F32)).astype(BF16)
        b = (rest[3].astype(F32) + near[1][1].astype(F32)).astype(BF16)
        a, b = lax.optimization_barrier((a, b))
        return lax.optimization_barrier((swap(a, 3), swap(b, 1)))

    far_1 = onward(rest_1, near_1)
    far_2 = onward(rest_2, near_2)
    return pl.pallas_call(
        finish_kernel,
        out_shape=(shape((1024, TOK)), shape((1024, 2))),
        in_specs=[VMEM] * 10,
        out_specs=(VMEM, VMEM),
        compiler_params=params(),
        name="finish",
    )(rest_1, *near_1, *far_1, rest_2, *near_2, *far_2)


def solution(mesh):
    split = Mesh(mesh.devices.reshape(4, 4, 2, mesh.shape["head"]), ("y", "x", "core", "head"))
    return jax.shard_map(
        per_device,
        mesh=split,
        in_specs=(
            P(CTX, "head"), P(CTX, "head"), P(CTX, "head", None), P(CTX, "head", None), P("head", CTX),
            P("head"), P("head"), P("head"), P("head", None),
            P(CTX, None, "head"), P(CTX, None, "head"), P(CTX, None, "head", None), P(CTX, None, "head", None),
            P("head", CTX, None), P(CTX),
        ),
        out_specs=(P("head", CTX), P("head", CTX)),
        check_vma=False,
    )
```

```python
import functools

import jax
import jax.numpy as jnp
from jax import lax
from jax.experimental import pallas as pl
from jax.experimental.pallas import tpu as pltpu
from jax.sharding import Mesh
from jax.sharding import PartitionSpec as P

HEADS = 32
HEAD_DIM = 64
STATE = 256
BLOCK = 128
SLEN = 16
TOK = 512
CH = HEADS * HEAD_DIM
PIECE = 512
ROWS = 144
CTX = ("y", "x", "core")
F32 = jnp.float32
BF16 = jnp.bfloat16
EXACT = lax.Precision.HIGHEST
CHUNKS = (256, 256)


def softplus(v):
    return jnp.maximum(v, 0.0) + jnp.log1p(jnp.exp(-jnp.abs(v)))


def iota(shape, dim):
    return lax.broadcasted_iota(jnp.int32, shape, dim)


def column(row):
    n = row.shape[1]
    square = jnp.broadcast_to(row, (n, n))
    return jnp.sum(jnp.where(iota((n, n), 0) == iota((n, n), 1), square, 0.0), axis=1, keepdims=True)


def tokens_first(x):
    pad = jnp.zeros((128 - x.shape[0], x.shape[1]), F32)
    return jnp.transpose(jnp.concatenate([x, pad], axis=0))


def per_pair(columns, pair, shape, low):
    first = jnp.broadcast_to(columns[:, 2 * pair : 2 * pair + 1], shape)
    second = jnp.broadcast_to(columns[:, 2 * pair + 1 : 2 * pair + 2], shape)
    return jnp.where(low, first, second)


def three_parts(x):
    hi = x.astype(BF16).astype(F32)
    mid = (x - hi).astype(BF16).astype(F32)
    lo = (x - hi - mid).astype(BF16).astype(F32)
    return hi, mid, lo


def decay_of(tail):
    return tail[8:9] + tail[9:10] + tail[10:11]


def with_decay(tail, decay):
    row = iota((16, 128), 0)
    hi, mid, lo = three_parts(decay)
    tail = jnp.where(row == 8, hi, tail)
    tail = jnp.where(row == 9, mid, tail)
    return jnp.where(row == 10, lo, tail)


def end_state_kernel(length, step_ref, decay_ref, values_ref, inject_ref, read_ref, keep_ref, send_ref, scaled):
    core = lax.axis_index("core")
    step = softplus(step_ref[...])
    logs = step * -jnp.exp(column(decay_ref[...]))
    later = (iota((BLOCK, BLOCK), 0) > iota((BLOCK, BLOCK), 1)).astype(F32)
    after = jnp.zeros((HEADS, 1), F32)
    parts = []
    for b in reversed(range(TOK // BLOCK)):
        here = logs[:, b * BLOCK : (b + 1) * BLOCK]
        parts.append(jnp.dot(here, later, precision=EXACT, preferred_element_type=F32) + after)
        after = after + jnp.sum(here, axis=1, keepdims=True)
    weight = tokens_first(jnp.exp(jnp.concatenate(parts[::-1], axis=1)) * step)
    total = tokens_first(jnp.broadcast_to(jnp.exp(after), (HEADS, 128)))[0:8]
    inject_t = jnp.transpose(inject_ref[...].astype(F32)).astype(BF16)
    low = iota((TOK, 128), 1) < HEAD_DIM
    low_row = iota((8, 128), 1) < HEAD_DIM
    row = iota((16, 128), 0)
    tails = []
    for half in range(2):
        lanes = slice(half * 128, (half + 1) * 128)
        tail = jnp.zeros((16, 128), F32)
        for s in range(2):
            last = iota((SLEN, 128), 0) == length[s] - 1
            picked = jnp.sum(jnp.where(last, read_ref[s, :, lanes].astype(F32), 0.0), axis=0, keepdims=True)
            tail = jnp.where(row == 2 * core + s, picked, tail)
        tails.append(tail)
    for half in range(2):
        for q in range(8):
            pair = half * 8 + q
            lanes = slice(pair * 128, (pair + 1) * 128)
            w = per_pair(weight, pair, (TOK, 128), low)
            scaled[:, q * 128 : (q + 1) * 128] = (values_ref[:, lanes].astype(F32) * w).astype(BF16)
        state = jnp.dot(inject_t, scaled[...], preferred_element_type=F32).astype(BF16)

        def put(out_ref, half=half, state=state):
            for q in range(8):
                decay = per_pair(total, half * 8 + q, (8, 128), low_row)[0:1]
                for n in range(2):
                    out_ref[2 * q + n, 0:128, :] = state[n * 128 : (n + 1) * 128, q * 128 : (q + 1) * 128]
                    out_ref[2 * q + n, 128:ROWS, :] = with_decay(tails[n], decay).astype(BF16)

        @pl.when(core == half)
        def _(put=put):
            put(keep_ref)

        @pl.when(core != half)
        def _(put=put):
            put(send_ref)


def join_cores_kernel(own_ref, sib_ref, out_ref):
    first = lax.axis_index("core") == 0
    row = iota((16, 128), 0)
    for k in range(16):
        own_tail = own_ref[k, 128:ROWS, :].astype(F32)
        sib_tail = sib_ref[k, 128:ROWS, :].astype(F32)
        own_decay, sib_decay = decay_of(own_tail), decay_of(sib_tail)
        own_weight = jnp.where(first, sib_decay, 1.0)
        sib_weight = jnp.where(first, 1.0, own_decay)
        out_ref[k, 0:128, :] = (
            own_ref[k, 0:128, :].astype(F32) * own_weight + sib_ref[k, 0:128, :].astype(F32) * sib_weight
        ).astype(BF16)
        tail = jnp.where(row < 8, own_tail + sib_tail, 0.0)
        out_ref[k, 128:ROWS, :] = with_decay(tail, own_decay * sib_decay).astype(BF16)


def prefix_kernel(in_ref, out_ref):
    state = jnp.zeros((128, 128), F32)
    for i in range(16):
        out_ref[i, 0:128, :] = state.astype(BF16)
        decay = decay_of(in_ref[i, 128:ROWS, :].astype(F32))
        state = state * decay + in_ref[i, 0:128, :].astype(F32)
    final = state.astype(BF16)
    for i in range(16):
        out_ref[i, 128:ROWS, :] = jnp.dot(
            in_ref[i, 128:ROWS, :], final, preferred_element_type=F32
        ).astype(BF16)


def split_cores_kernel(back_ref, own_ref, sib_ref, mine_ref, send_ref):
    first = lax.axis_index("core") == 0
    for k in range(16):
        q, n = k // 2, k % 2
        arrived = back_ref[k, 0:128, :].astype(F32)
        own_decay = decay_of(own_ref[k, 128:ROWS, :].astype(F32))
        sib_decay = decay_of(sib_ref[k, 128:ROWS, :].astype(F32))
        decay = jnp.where(first, own_decay, sib_decay)
        state = jnp.where(first, own_ref[k, 0:128, :].astype(F32), sib_ref[k, 0:128, :].astype(F32))
        second = arrived * decay + state
        mine_ref[n * 128 : (n + 1) * 128, q * 128 : (q + 1) * 128] = jnp.where(first, arrived, second).astype(BF16)
        send_ref[k, 0:128, :] = jnp.where(first, second, arrived).astype(BF16)
        send_ref[k, 128:ROWS, :] = back_ref[k, 128:ROWS, :]
    for q in range(8):
        mine_ref[256:272, q * 128 : (q + 1) * 128] = (
            back_ref[2 * q, 128:ROWS, :].astype(F32) + back_ref[2 * q + 1, 128:ROWS, :].astype(F32)
        ).astype(BF16)


def local_kernel(
    step_ref, decay_ref, skip_ref, values_ref, gate_ref, inject_ref, read_ref, *refs
):
    if len(refs) == 7:
        scaled_ref, gain_ref, state, before, ends, weighted, carried = refs
    else:
        start, start_before, scaled_ref, gain_ref, ends, weighted, carried, state, before = refs

    @pl.when(pl.program_id(0) == 0)
    def _():
        if len(refs) == 7:
            state[...] = jnp.zeros_like(state)
            before[...] = jnp.ones_like(before)
        else:
            state[...] = start[...]
            before[...] = start_before[...]

    step = softplus(step_ref[...])
    logs = step * -jnp.exp(column(decay_ref[...]))
    upto = (iota((BLOCK, BLOCK), 0) <= iota((BLOCK, BLOCK), 1)).astype(F32)
    running = jnp.dot(logs, upto, precision=EXACT, preferred_element_type=F32)
    running_t = tokens_first(running)
    step_t = tokens_first(step)
    read = read_ref[...]
    inject = inject_ref[...]
    inject_t = jnp.transpose(inject.astype(F32)).astype(BF16)
    scores = jnp.dot(read, inject_t, preferred_element_type=F32)
    carried[...] = jnp.dot(read, state[...].astype(BF16), preferred_element_type=F32)
    causal = iota((BLOCK, BLOCK), 0) >= iota((BLOCK, BLOCK), 1)
    low = iota((BLOCK, 128), 1) < HEAD_DIM
    for pair in range(16):
        lanes = slice(pair * 128, (pair + 1) * 128)
        mixing = []
        spread = []
        for h in (2 * pair, 2 * pair + 1):
            mine = jnp.broadcast_to(running_t[:, h : h + 1], (BLOCK, BLOCK))
            gap = jnp.where(causal, mine - running[h : h + 1, :], -1e30)
            mixing.append((scores * jnp.exp(gap)).astype(BF16))
            spread.append(mine)
        now = jnp.where(low, spread[0], spread[1])
        grown = jnp.exp(now)
        values = values_ref[:, lanes].astype(F32)
        stepped = values * per_pair(step_t, pair, (BLOCK, 128), low)
        diagonal = jnp.concatenate([jnp.where(low, stepped, 0.0), jnp.where(low, 0.0, stepped)], axis=0)
        local = jnp.dot(
            jnp.concatenate(mixing, axis=1), diagonal.astype(BF16), preferred_element_type=F32
        )
        out = local + carried[:, lanes] * grown + skip_ref[:, lanes] * values
        gate = gate_ref[:, lanes].astype(F32)
        gate = gate / (1.0 + jnp.exp(-gate))
        scaled_ref[:, lanes] = (out * gate).astype(BF16)
        gain_ref[:, lanes] = (gate * grown * before[0:1, lanes]).astype(BF16)
        end = now[BLOCK - 1 : BLOCK, :]
        weighted[:, lanes] = (stepped * jnp.exp(end - now)).astype(BF16)
        ends[0:1, lanes] = jnp.exp(end)
    state[...] = state[...] * ends[0:1, :] + jnp.dot(inject_t, weighted[...], preferred_element_type=F32)
    before[0:1, :] = before[0:1, :] * ends[0:1, :]


def sample_kernel(
    length, step_ref, decay_ref, skip_ref, values_ref, gate_ref, inject_ref, read_ref, local_ref, grown_ref, gate_out_ref
):
    rate = -jnp.exp(column(decay_ref[...]))
    row = iota((16, CH), 0)
    spread = (iota((128, CH), 1) // HEAD_DIM == iota((128, CH), 0)).astype(F32)
    local_all = jnp.zeros((16, CH), F32)
    grown_all = jnp.zeros((16, CH), F32)
    gate_all = jnp.zeros((16, CH), F32)
    for s in range(2):
        last = length[s] - 1
        step = softplus(step_ref[s])
        logs = step * rate
        pad = jnp.zeros((HEADS, 128 - SLEN), F32)
        step_t = tokens_first(jnp.concatenate([step, pad], axis=1))[0:SLEN]
        logs_t = tokens_first(jnp.concatenate([logs, pad], axis=1))[0:SLEN]
        place = iota((SLEN, 128), 0)
        logs_t = jnp.where(place <= last, logs_t, 0.0)
        gap = jnp.zeros((SLEN, 128), F32)
        for k in range(SLEN):
            gap = gap + jnp.where(place < k, logs_t[k : k + 1], 0.0)
        whole = jnp.sum(logs_t, axis=0, keepdims=True)
        place_wide = iota((SLEN, STATE), 0)
        read = jnp.sum(jnp.where(place_wide == last, read_ref[s].astype(F32), 0.0), axis=0, keepdims=True)
        scores = jnp.sum(inject_ref[s].astype(F32) * read, axis=1, keepdims=True)
        weight = jnp.where(place <= last, scores * jnp.exp(gap) * step_t, 0.0)
        both = jnp.concatenate([weight, jnp.broadcast_to(jnp.exp(whole), (8, 128))], axis=0)
        wide = jnp.dot(both, spread, precision=EXACT, preferred_element_type=F32)
        values = values_ref[s].astype(F32)
        at_last = iota((SLEN, CH), 0) == last
        picked = jnp.sum(jnp.where(at_last, values, 0.0), axis=0, keepdims=True)
        gate = jnp.sum(jnp.where(at_last, gate_ref[s].astype(F32), 0.0), axis=0, keepdims=True)
        local = jnp.sum(wide[0:SLEN] * values, axis=0, keepdims=True) + skip_ref[...] * picked
        local_all = jnp.where(row == s, local, local_all)
        grown_all = jnp.where(row == s, wide[SLEN : SLEN + 1], grown_all)
        gate_all = jnp.where(row == s, gate / (1.0 + jnp.exp(-gate)), gate_all)
    local_ref[...] = local_all
    grown_ref[...] = grown_all
    gate_out_ref[...] = gate_all


def normalize(gated, weight):
    mean = jnp.sum(gated * gated, axis=1, keepdims=True) * (1.0 / CH)
    return (gated * lax.rsqrt(mean + 1e-05) * weight).astype(BF16)


FIRST = ((1, 0), (2, 0), (3, 1), (2, 1))
REST = ((3, 0), (1, 1), (0, 0), (0, 1))


class Columns:
    def __init__(self, pieces, weight_ref, held, sems, base=0):
        z = lax.axis_index("head")
        self.held, self.base, self.copies = held, base, []
        for i, (flip, half) in enumerate(pieces):
            at = pl.multiple_of(((z ^ flip) * 2 + half) * PIECE, PIECE)
            self.copies.append(
                pltpu.make_async_copy(weight_ref.at[:, pl.ds(at, PIECE)], held.at[base + i], sems.at[base + i])
            )
        for copy in self.copies:
            copy.start()

    def project(self, normed, outs):
        for i, (copy, (ref, k)) in enumerate(zip(self.copies, outs)):
            copy.wait()
            out = jnp.dot(normed[...], self.held[self.base + i], preferred_element_type=F32)
            ref[k] = out.astype(BF16)


def gate_and_normalize(place, state_ref, read_ref, scaled_ref, gain_ref, norm_ref, normed):
    rows = CHUNKS[place]
    read = read_ref[place * rows : (place + 1) * rows, :]
    arrived = jnp.dot(read, state_ref[0:STATE, :], preferred_element_type=F32)
    gated = scaled_ref[...].astype(F32) + arrived * gain_ref[...].astype(F32)
    normed[0:rows, :] = normalize(gated, norm_ref[...])


def first_chunk_kernel(
    mine_ref, theirs_ref, read_ref, scaled_ref, gain_ref, norm_ref, weight_ref,
    first_ref, second_ref, normed_ref, state_ref, held, sems,
):
    columns = Columns(FIRST, weight_ref, held, sems)
    core = lax.axis_index("core")
    state_ref[:, pl.ds(pl.multiple_of(core * 1024, 1024), 1024)] = mine_ref[...]
    for q in range(8):
        lanes = pl.ds(pl.multiple_of((1 - core) * 1024 + q * 128, 128), 128)
        for n in range(2):
            state_ref[n * 128 : (n + 1) * 128, lanes] = theirs_ref[2 * q + n, 0:128, :]
        state_ref[256:272, lanes] = (
            theirs_ref[2 * q, 128:ROWS, :].astype(F32) + theirs_ref[2 * q + 1, 128:ROWS, :].astype(F32)
        ).astype(BF16)
    gate_and_normalize(0, state_ref, read_ref, scaled_ref, gain_ref, norm_ref, normed_ref)
    columns.project(normed_ref, ((first_ref, 0), (first_ref, 1), (second_ref, 0), (second_ref, 1)))


def next_chunk_kernel(
    place, before_ref, state_ref, read_ref, scaled_ref, gain_ref, norm_ref, weight_ref, *refs
):
    sample, (rest_ref, first_ref, second_ref, normed_ref, held, sems) = refs[:-6], refs[-6:]
    columns = Columns(FIRST, weight_ref, held, sems)
    rest = Columns(REST, weight_ref, held, sems, 4)
    gate_and_normalize(place, state_ref, read_ref, scaled_ref, gain_ref, norm_ref, normed_ref)
    if sample:
        local_ref, grown_ref, gate_ref = sample
        readings = state_ref[256:272, :].astype(F32)
        moved = jnp.concatenate([readings[2:16], readings[0:2]], axis=0)
        readings = jnp.where(lax.axis_index("core") == 0, readings, moved)
        sampled = (local_ref[...] + readings * grown_ref[...]) * gate_ref[...]
        rows = CHUNKS[place]
        normed_ref[rows : rows + 16, :] = normalize(sampled, norm_ref[...])
    columns.project(normed_ref, ((first_ref, 0), (first_ref, 1), (second_ref, 0), (second_ref, 1)))
    rest.project(before_ref, ((rest_ref, 1), (rest_ref, 3), (rest_ref, 0), (rest_ref, 2)))


def rest_kernel(normed_ref, weight_ref, rest_ref, held, sems):
    rest = Columns(REST, weight_ref, held, sems)
    rest.project(normed_ref, ((rest_ref, 1), (rest_ref, 3), (rest_ref, 0), (rest_ref, 2)))


def onward_kernel(a_ref, b_ref, rest_ref, a_out, b_out):
    a_out[...] = (rest_ref[1].astype(F32) + a_ref[1].astype(F32)).astype(BF16)
    b_out[...] = (rest_ref[3].astype(F32) + b_ref[1].astype(F32)).astype(BF16)


def finish_kernel(*refs):
    ins, out_ref, sample_ref = refs[:-2], refs[-2], refs[-1]
    start = 0
    for c, rows in enumerate(CHUNKS):
        ra, rb, rest, sa, sb = ins[5 * c : 5 * c + 5]
        for half, (own, near, far) in enumerate(((0, ra, sa), (2, rb, sb))):
            total = rest[own].astype(F32) + near[0].astype(F32) + far[...].astype(F32)
            columns = slice(half * PIECE, (half + 1) * PIECE)
            out_ref[columns, start : start + rows] = jnp.transpose(total[0:rows]).astype(BF16)
            if c == len(CHUNKS) - 1:
                sample_ref[:, columns] = total[rows : rows + 2].astype(BF16)
        start += rows


def call(kernel, name, out_shape, inputs, limit, scalars=0, streamed=None, **more):
    return pl.pallas_call(
        kernel,
        out_shape=out_shape,
        in_specs=[
            SMEM if i < scalars else pl.BlockSpec(memory_space=pl.ANY) if i == streamed else VMEM for i in range(len(inputs))
        ],
        out_specs=jax.tree.map(lambda _: VMEM, out_shape),
        compiler_params=pltpu.CompilerParams(vmem_limit_bytes=limit << 20),
        cost_estimate=pl.CostEstimate(flops=1, bytes_accessed=1, transcendentals=0),
        name=name,
        **more,
    )(*inputs)


SMEM = pl.BlockSpec(memory_space=pltpu.SMEM)
VMEM = pl.BlockSpec(memory_space=pltpu.VMEM)


def shape(dims, dtype=BF16):
    return jax.ShapeDtypeStruct(dims, dtype)


def held(pieces):
    return [pltpu.VMEM((pieces, CH, PIECE), BF16), pltpu.SemaphoreType.DMA((pieces,))]


def swap(x, step):
    return lax.ppermute(x, "head", [(i, i ^ step) for i in range(4)])


def other_core(x):
    return lax.ppermute(x, "core", [(0, 1), (1, 0)])


def local_outputs(part, step, decay, skip, values, gate, inject, read, start=()):
    blocks = TOK // BLOCK // 2
    row = lambda width: pl.BlockSpec((1, width), lambda b: (0, 0))
    tokens = lambda width: pl.BlockSpec((BLOCK, width), lambda b: (b + part * blocks, 0))
    out = pl.BlockSpec((BLOCK, CH), lambda b: (b, 0))
    whole = lambda rows: pl.BlockSpec((rows, CH), lambda b: (0, 0))
    carry = (shape((STATE, CH), F32), shape((8, CH), F32))
    results = (shape((TOK // 2, CH)), shape((TOK // 2, CH)))
    scratch = [pltpu.VMEM((8, CH), F32), pltpu.VMEM((BLOCK, CH), BF16), pltpu.VMEM((BLOCK, CH), F32)]
    if start:
        start_specs = [whole(STATE), whole(8)]
        out_specs = (out, out)
        scratch += [pltpu.VMEM((STATE, CH), F32), pltpu.VMEM((8, CH), F32)]
    else:
        start_specs = []
        results += carry
        out_specs = (out, out, whole(STATE), whole(8))
    values, gate = (pltpu.with_memory_space_constraint(x, pltpu.HBM) for x in (values, gate))
    return pl.pallas_call(
        local_kernel,
        grid=(blocks,),
        out_shape=results,
        in_specs=[
            pl.BlockSpec((HEADS, BLOCK), lambda b: (0, b + part * blocks)), row(HEADS), row(CH),
            tokens(CH), tokens(CH), tokens(STATE), tokens(STATE), *start_specs,
        ],
        out_specs=out_specs,
        scratch_shapes=scratch,
        compiler_params=pltpu.CompilerParams(vmem_limit_bytes=20 << 20),
        cost_estimate=pl.CostEstimate(flops=3 << 30, bytes_accessed=20 << 20, transcendentals=2 << 20),
        name="local_outputs",
    )(step, decay, skip, values, gate, inject, read, *start)


def per_device(
    prompt_values, prompt_gate, prompt_inject, prompt_read, prompt_step, decay_log, skip_gain, norm_weight, out_weight,
    sample_values, sample_gate, sample_inject, sample_read, sample_step, sample_length,
):
    inject = prompt_inject.reshape(TOK, STATE)
    read = prompt_read.reshape(TOK, STATE)
    decay = decay_log.reshape(1, HEADS)
    skip = jnp.repeat(skip_gain, HEAD_DIM).reshape(1, CH)
    norm = norm_weight.reshape(1, CH)
    s_read = sample_read.reshape(2, SLEN, STATE)
    s_inject = sample_inject.reshape(2, SLEN, STATE)
    slices_shape = shape((16, ROWS, 128))

    keep, send = call(
        end_state_kernel, "end_state", (slices_shape,) * 2,
        (sample_length, prompt_step, decay, prompt_values, inject, s_read), 24, 1,
        scratch_shapes=[pltpu.VMEM((TOK, 1024), BF16)],
    )
    sibling = other_core(send)
    joined = call(join_cores_kernel, "join_cores", slices_shape, (keep, sibling), 16)
    joined, step_1 = lax.optimization_barrier((joined, prompt_step))
    slices = lax.all_to_all(joined, ("y", "x"), 0, 0, tiled=True)
    scaled_1, gain_1, *carry = local_outputs(
        0, step_1, decay, skip, prompt_values, prompt_gate, inject, read
    )
    slices, scaled_1 = lax.optimization_barrier((slices, scaled_1))
    prefix = call(prefix_kernel, "prefix", slices_shape, (slices,), 16)
    prefix, step_2, s_step = lax.optimization_barrier((prefix, prompt_step, sample_step))
    back = lax.all_to_all(prefix, ("y", "x"), 0, 0, tiled=True)
    scaled_2, gain_2 = local_outputs(
        1, step_2, decay, skip, prompt_values, prompt_gate, inject, read, carry
    )
    sample = call(
        sample_kernel, "sample_outputs", (shape((16, CH), F32),) * 3,
        (sample_length, s_step.transpose(1, 0, 2), decay, skip, sample_values, sample_gate, s_inject, s_read), 16, 1,
    )
    back, scaled_2, sample = lax.optimization_barrier((back, scaled_2, sample))
    mine, send = call(
        split_cores_kernel, "split_cores", (shape((272, 1024)), slices_shape), (back, keep, sibling), 16
    )
    theirs = other_core(send)

    weight = pltpu.with_memory_space_constraint(out_weight, pltpu.HBM)
    scaled = (scaled_1, scaled_2)
    gain = (gain_1, gain_2)
    near, rests = [], []
    normed = state = None
    for c, rows in enumerate(CHUNKS):
        parts = (read, scaled[c], gain[c], norm, weight)
        last = c == len(CHUNKS) - 1
        size = rows + (16 if last else 0)
        sent = (shape((2, size, PIECE)),) * 2 + (shape((size, CH)),)
        if c == 0:
            *now, normed, state = call(
                first_chunk_kernel, "first_chunk", (*sent, shape((272, CH))), (mine, theirs, *parts), 40,
                streamed=6, scratch_shapes=held(4),
            )
        else:
            rest, *now, normed = call(
                functools.partial(next_chunk_kernel, c), "next_chunk", (shape((4, normed.shape[0], PIECE)), *sent),
                (normed, state, *parts, *(sample if last else ())), 40, streamed=6, scratch_shapes=held(8),
            )
            rests.append(rest)
        near.append(lax.optimization_barrier((swap(now[0], 1), swap(now[1], 3))))
    rests.append(
        call(
            rest_kernel, "rest", shape((4, normed.shape[0], PIECE)), (normed, weight), 40, streamed=1, scratch_shapes=held(4)
        )
    )

    ends = []
    a_on = None
    for rest, (a, b) in zip(rests, near):
        if a_on is not None:
            a, b, a_on = lax.optimization_barrier((a, b, a_on))
            ends += lax.optimization_barrier((swap(a_on, 3), swap(b_on, 1)))
        a_on, b_on = call(onward_kernel, "onward", (shape(a.shape[1:]),) * 2, (a, b, rest), 8)
        ends += [a, b, rest]
    ends += lax.optimization_barrier((swap(a_on, 3), swap(b_on, 1)))
    prompt_mixed, sample_mixed = call(
        finish_kernel, "finish", (shape((1024, TOK)), shape((2, 1024))), tuple(ends), 24
    )
    return prompt_mixed, sample_mixed.T


def solution(mesh):
    split = Mesh(mesh.devices.reshape(4, 4, 2, mesh.shape["head"]), ("y", "x", "core", "head"))
    return jax.shard_map(
        per_device,
        mesh=split,
        in_specs=(
            P(CTX, "head"), P(CTX, "head"), P(CTX, "head", None), P(CTX, "head", None), P("head", CTX),
            P("head"), P("head"), P("head"), P("head", None),
            P(CTX, None, "head"), P(CTX, None, "head"), P(CTX, None, "head", None), P(CTX, None, "head", None),
            P("head", CTX, None), P(CTX),
        ),
        out_specs=(P("head", CTX), P("head", CTX)),
        check_vma=False,
    )
```

```python
import functools

import jax
import jax.numpy as jnp
from jax import lax
from jax.experimental import pallas as pl
from jax.experimental.pallas import tpu as pltpu
from jax.sharding import Mesh
from jax.sharding import PartitionSpec as P

HEADS = 32
HEAD_DIM = 64
STATE = 256
BLOCK = 128
SLEN = 16
TOK = 512
CH = HEADS * HEAD_DIM
PIECE = 512
ROWS = 144
CTX = ("y", "x", "core")
F32 = jnp.float32
BF16 = jnp.bfloat16
EXACT = lax.Precision.HIGHEST
CHUNKS = (256, 256)


def softplus(v):
    return jnp.maximum(v, 0.0) + jnp.log1p(jnp.exp(-jnp.abs(v)))


def iota(shape, dim):
    return lax.broadcasted_iota(jnp.int32, shape, dim)


def column(row):
    n = row.shape[1]
    square = jnp.broadcast_to(row, (n, n))
    return jnp.sum(jnp.where(iota((n, n), 0) == iota((n, n), 1), square, 0.0), axis=1, keepdims=True)


def tokens_first(x):
    pad = jnp.zeros((128 - x.shape[0], x.shape[1]), F32)
    return jnp.transpose(jnp.concatenate([x, pad], axis=0))


def per_pair(columns, pair, shape, low):
    first = jnp.broadcast_to(columns[:, 2 * pair : 2 * pair + 1], shape)
    second = jnp.broadcast_to(columns[:, 2 * pair + 1 : 2 * pair + 2], shape)
    return jnp.where(low, first, second)


def three_parts(x):
    hi = x.astype(BF16).astype(F32)
    mid = (x - hi).astype(BF16).astype(F32)
    lo = (x - hi - mid).astype(BF16).astype(F32)
    return hi, mid, lo


def decay_of(tail):
    return tail[8:9] + tail[9:10] + tail[10:11]


def with_decay(tail, decay):
    row = iota((16, 128), 0)
    hi, mid, lo = three_parts(decay)
    tail = jnp.where(row == 8, hi, tail)
    tail = jnp.where(row == 9, mid, tail)
    return jnp.where(row == 10, lo, tail)


def end_state_kernel(length, step_ref, decay_ref, values_ref, inject_ref, read_ref, keep_ref, send_ref, scaled):
    core = lax.axis_index("core")
    step = softplus(step_ref[...])
    logs = step * -jnp.exp(column(decay_ref[...]))
    later = (iota((BLOCK, BLOCK), 0) > iota((BLOCK, BLOCK), 1)).astype(F32)
    after = jnp.zeros((HEADS, 1), F32)
    parts = []
    for b in reversed(range(TOK // BLOCK)):
        here = logs[:, b * BLOCK : (b + 1) * BLOCK]
        parts.append(jnp.dot(here, later, precision=EXACT, preferred_element_type=F32) + after)
        after = after + jnp.sum(here, axis=1, keepdims=True)
    weight = tokens_first(jnp.exp(jnp.concatenate(parts[::-1], axis=1)) * step)
    total = tokens_first(jnp.broadcast_to(jnp.exp(after), (HEADS, 128)))[0:8]
    inject_t = jnp.transpose(inject_ref[...].astype(F32)).astype(BF16)
    low = iota((TOK, 128), 1) < HEAD_DIM
    low_row = iota((8, 128), 1) < HEAD_DIM
    row = iota((16, 128), 0)
    tails = []
    for half in range(2):
        lanes = slice(half * 128, (half + 1) * 128)
        tail = jnp.zeros((16, 128), F32)
        for s in range(2):
            last = iota((SLEN, 128), 0) == length[s] - 1
            picked = jnp.sum(jnp.where(last, read_ref[s, :, lanes].astype(F32), 0.0), axis=0, keepdims=True)
            tail = jnp.where(row == 2 * core + s, picked, tail)
        tails.append(tail)
    for half in range(2):
        for q in range(8):
            pair = half * 8 + q
            lanes = slice(pair * 128, (pair + 1) * 128)
            w = per_pair(weight, pair, (TOK, 128), low)
            scaled[:, q * 128 : (q + 1) * 128] = (values_ref[:, lanes].astype(F32) * w).astype(BF16)
        state = jnp.dot(inject_t, scaled[...], preferred_element_type=F32).astype(BF16)

        def put(out_ref, half=half, state=state):
            for q in range(8):
                decay = per_pair(total, half * 8 + q, (8, 128), low_row)[0:1]
                for n in range(2):
                    out_ref[2 * q + n, 0:128, :] = state[n * 128 : (n + 1) * 128, q * 128 : (q + 1) * 128]
                    out_ref[2 * q + n, 128:ROWS, :] = with_decay(tails[n], decay).astype(BF16)

        @pl.when(core == half)
        def _(put=put):
            put(keep_ref)

        @pl.when(core != half)
        def _(put=put):
            put(send_ref)


def join_cores_kernel(own_ref, sib_ref, out_ref):
    first = lax.axis_index("core") == 0
    row = iota((16, 128), 0)
    for k in range(16):
        own_tail = own_ref[k, 128:ROWS, :].astype(F32)
        sib_tail = sib_ref[k, 128:ROWS, :].astype(F32)
        own_decay, sib_decay = decay_of(own_tail), decay_of(sib_tail)
        own_weight = jnp.where(first, sib_decay, 1.0)
        sib_weight = jnp.where(first, 1.0, own_decay)
        out_ref[k, 0:128, :] = (
            own_ref[k, 0:128, :].astype(F32) * own_weight + sib_ref[k, 0:128, :].astype(F32) * sib_weight
        ).astype(BF16)
        tail = jnp.where(row < 8, own_tail + sib_tail, 0.0)
        out_ref[k, 128:ROWS, :] = with_decay(tail, own_decay * sib_decay).astype(BF16)


def prefix_kernel(in_ref, out_ref):
    state = jnp.zeros((128, 128), F32)
    for i in range(16):
        out_ref[i, 0:128, :] = state.astype(BF16)
        decay = decay_of(in_ref[i, 128:ROWS, :].astype(F32))
        state = state * decay + in_ref[i, 0:128, :].astype(F32)
    final = state.astype(BF16)
    for i in range(16):
        out_ref[i, 128:ROWS, :] = jnp.dot(
            in_ref[i, 128:ROWS, :], final, preferred_element_type=F32
        ).astype(BF16)


def split_cores_kernel(back_ref, own_ref, sib_ref, mine_ref, send_ref):
    first = lax.axis_index("core") == 0
    for k in range(16):
        q, n = k // 2, k % 2
        arrived = back_ref[k, 0:128, :].astype(F32)
        own_decay = decay_of(own_ref[k, 128:ROWS, :].astype(F32))
        sib_decay = decay_of(sib_ref[k, 128:ROWS, :].astype(F32))
        decay = jnp.where(first, own_decay, sib_decay)
        state = jnp.where(first, own_ref[k, 0:128, :].astype(F32), sib_ref[k, 0:128, :].astype(F32))
        second = arrived * decay + state
        mine_ref[n * 128 : (n + 1) * 128, q * 128 : (q + 1) * 128] = jnp.where(first, arrived, second).astype(BF16)
        send_ref[k, 0:128, :] = jnp.where(first, second, arrived).astype(BF16)
        send_ref[k, 128:ROWS, :] = back_ref[k, 128:ROWS, :]
    for q in range(8):
        mine_ref[256:272, q * 128 : (q + 1) * 128] = (
            back_ref[2 * q, 128:ROWS, :].astype(F32) + back_ref[2 * q + 1, 128:ROWS, :].astype(F32)
        ).astype(BF16)


def local_kernel(
    step_ref, decay_ref, skip_ref, values_ref, gate_ref, inject_ref, read_ref, *refs
):
    if len(refs) == 7:
        scaled_ref, gain_ref, state, before, ends, weighted, carried = refs
    else:
        start, start_before, scaled_ref, gain_ref, ends, weighted, carried, state, before = refs

    @pl.when(pl.program_id(0) == 0)
    def _():
        if len(refs) == 7:
            state[...] = jnp.zeros_like(state)
            before[...] = jnp.ones_like(before)
        else:
            state[...] = start[...]
            before[...] = start_before[...]

    step = softplus(step_ref[...])
    logs = step * -jnp.exp(column(decay_ref[...]))
    upto = (iota((BLOCK, BLOCK), 0) <= iota((BLOCK, BLOCK), 1)).astype(F32)
    running = jnp.dot(logs, upto, precision=EXACT, preferred_element_type=F32)
    running_t = tokens_first(running)
    step_t = tokens_first(step)
    read = read_ref[...]
    inject = inject_ref[...]
    inject_t = jnp.transpose(inject.astype(F32)).astype(BF16)
    scores = jnp.dot(read, inject_t, preferred_element_type=F32)
    carried[...] = jnp.dot(read, state[...].astype(BF16), preferred_element_type=F32)
    causal = iota((BLOCK, BLOCK), 0) >= iota((BLOCK, BLOCK), 1)
    low = iota((BLOCK, 128), 1) < HEAD_DIM
    for pair in range(16):
        lanes = slice(pair * 128, (pair + 1) * 128)
        mixing = []
        spread = []
        for h in (2 * pair, 2 * pair + 1):
            mine = jnp.broadcast_to(running_t[:, h : h + 1], (BLOCK, BLOCK))
            gap = jnp.where(causal, mine - running[h : h + 1, :], -1e30)
            mixing.append((scores * jnp.exp(gap)).astype(BF16))
            spread.append(mine)
        now = jnp.where(low, spread[0], spread[1])
        grown = jnp.exp(now)
        values = values_ref[:, lanes].astype(F32)
        stepped = values * per_pair(step_t, pair, (BLOCK, 128), low)
        diagonal = jnp.concatenate([jnp.where(low, stepped, 0.0), jnp.where(low, 0.0, stepped)], axis=0)
        local = jnp.dot(
            jnp.concatenate(mixing, axis=1), diagonal.astype(BF16), preferred_element_type=F32
        )
        out = local + carried[:, lanes] * grown + skip_ref[:, lanes] * values
        gate = gate_ref[:, lanes].astype(F32)
        gate = gate / (1.0 + jnp.exp(-gate))
        scaled_ref[:, lanes] = (out * gate).astype(BF16)
        gain_ref[:, lanes] = (gate * grown * before[0:1, lanes]).astype(BF16)
        end = now[BLOCK - 1 : BLOCK, :]
        weighted[:, lanes] = (stepped * jnp.exp(end - now)).astype(BF16)
        ends[0:1, lanes] = jnp.exp(end)
    state[...] = state[...] * ends[0:1, :] + jnp.dot(inject_t, weighted[...], preferred_element_type=F32)
    before[0:1, :] = before[0:1, :] * ends[0:1, :]


def sample_kernel(
    length, step_ref, decay_ref, skip_ref, values_ref, gate_ref, inject_ref, read_ref, local_ref, grown_ref, gate_out_ref
):
    rate = -jnp.exp(column(decay_ref[...]))
    row = iota((16, CH), 0)
    spread = (iota((128, CH), 1) // HEAD_DIM == iota((128, CH), 0)).astype(F32)
    local_all = jnp.zeros((16, CH), F32)
    grown_all = jnp.zeros((16, CH), F32)
    gate_all = jnp.zeros((16, CH), F32)
    for s in range(2):
        last = length[s] - 1
        step = softplus(step_ref[s])
        logs = step * rate
        pad = jnp.zeros((HEADS, 128 - SLEN), F32)
        step_t = tokens_first(jnp.concatenate([step, pad], axis=1))[0:SLEN]
        logs_t = tokens_first(jnp.concatenate([logs, pad], axis=1))[0:SLEN]
        place = iota((SLEN, 128), 0)
        logs_t = jnp.where(place <= last, logs_t, 0.0)
        gap = jnp.zeros((SLEN, 128), F32)
        for k in range(SLEN):
            gap = gap + jnp.where(place < k, logs_t[k : k + 1], 0.0)
        whole = jnp.sum(logs_t, axis=0, keepdims=True)
        place_wide = iota((SLEN, STATE), 0)
        read = jnp.sum(jnp.where(place_wide == last, read_ref[s].astype(F32), 0.0), axis=0, keepdims=True)
        scores = jnp.sum(inject_ref[s].astype(F32) * read, axis=1, keepdims=True)
        weight = jnp.where(place <= last, scores * jnp.exp(gap) * step_t, 0.0)
        both = jnp.concatenate([weight, jnp.broadcast_to(jnp.exp(whole), (8, 128))], axis=0)
        wide = jnp.dot(both, spread, precision=EXACT, preferred_element_type=F32)
        values = values_ref[s].astype(F32)
        at_last = iota((SLEN, CH), 0) == last
        picked = jnp.sum(jnp.where(at_last, values, 0.0), axis=0, keepdims=True)
        gate = jnp.sum(jnp.where(at_last, gate_ref[s].astype(F32), 0.0), axis=0, keepdims=True)
        local = jnp.sum(wide[0:SLEN] * values, axis=0, keepdims=True) + skip_ref[...] * picked
        local_all = jnp.where(row == s, local, local_all)
        grown_all = jnp.where(row == s, wide[SLEN : SLEN + 1], grown_all)
        gate_all = jnp.where(row == s, gate / (1.0 + jnp.exp(-gate)), gate_all)
    local_ref[...] = local_all
    grown_ref[...] = grown_all
    gate_out_ref[...] = gate_all


def normalize(gated, weight):
    mean = jnp.sum(gated * gated, axis=1, keepdims=True) * (1.0 / CH)
    return (gated * lax.rsqrt(mean + 1e-05) * weight).astype(BF16)


FIRST = ((1, 0), (2, 0), (3, 1), (2, 1))
REST = ((3, 0), (1, 1), (0, 0), (0, 1))


class Columns:
    def __init__(self, pieces, weight_ref, held, sems, base=0):
        z = lax.axis_index("head")
        self.held, self.base, self.copies = held, base, []
        for i, (flip, half) in enumerate(pieces):
            at = pl.multiple_of(((z ^ flip) * 2 + half) * PIECE, PIECE)
            self.copies.append(
                pltpu.make_async_copy(weight_ref.at[:, pl.ds(at, PIECE)], held.at[base + i], sems.at[base + i])
            )
        for copy in self.copies:
            copy.start()

    def project(self, normed, outs):
        for i, (copy, (ref, k)) in enumerate(zip(self.copies, outs)):
            copy.wait()
            out = jnp.dot(normed[...], self.held[self.base + i], preferred_element_type=F32)
            ref[k] = out.astype(BF16)


def gate_and_normalize(place, state_ref, read_ref, scaled_ref, gain_ref, norm_ref, normed):
    rows = CHUNKS[place]
    read = read_ref[place * rows : (place + 1) * rows, :]
    arrived = jnp.dot(read, state_ref[0:STATE, :], preferred_element_type=F32)
    gated = scaled_ref[...].astype(F32) + arrived * gain_ref[...].astype(F32)
    normed[0:rows, :] = normalize(gated, norm_ref[...])


def join_halves_kernel(mine_ref, theirs_ref, state_ref):
    core = lax.axis_index("core")
    state_ref[:, pl.ds(pl.multiple_of(core * 1024, 1024), 1024)] = mine_ref[...]
    for q in range(8):
        lanes = pl.ds(pl.multiple_of((1 - core) * 1024 + q * 128, 128), 128)
        for n in range(2):
            state_ref[n * 128 : (n + 1) * 128, lanes] = theirs_ref[2 * q + n, 0:128, :]
        state_ref[256:272, lanes] = (
            theirs_ref[2 * q, 128:ROWS, :].astype(F32) + theirs_ref[2 * q + 1, 128:ROWS, :].astype(F32)
        ).astype(BF16)


def chunk_kernel(place, state_ref, read_ref, scaled_ref, gain_ref, norm_ref, weight_ref, *refs):
    sample, (first_ref, second_ref, normed_ref, held, sems) = refs[:-5], refs[-5:]
    columns = Columns(FIRST, weight_ref, held, sems)
    gate_and_normalize(place, state_ref, read_ref, scaled_ref, gain_ref, norm_ref, normed_ref)
    if sample:
        local_ref, grown_ref, gate_ref = sample
        readings = state_ref[256:272, :].astype(F32)
        moved = jnp.concatenate([readings[2:16], readings[0:2]], axis=0)
        readings = jnp.where(lax.axis_index("core") == 0, readings, moved)
        sampled = (local_ref[...] + readings * grown_ref[...]) * gate_ref[...]
        rows = CHUNKS[place]
        normed_ref[rows : rows + 16, :] = normalize(sampled, norm_ref[...])
    columns.project(normed_ref, ((first_ref, 0), (first_ref, 1), (second_ref, 0), (second_ref, 1)))


def rest_kernel(normed_ref, weight_ref, rest_ref, held, sems):
    rest = Columns(REST, weight_ref, held, sems)
    rest.project(normed_ref, ((rest_ref, 1), (rest_ref, 3), (rest_ref, 0), (rest_ref, 2)))


def onward_kernel(a_ref, b_ref, rest_ref, a_out, b_out):
    a_out[...] = (rest_ref[1].astype(F32) + a_ref[1].astype(F32)).astype(BF16)
    b_out[...] = (rest_ref[3].astype(F32) + b_ref[1].astype(F32)).astype(BF16)


def finish_kernel(*refs):
    ins, out_ref, sample_ref = refs[:-2], refs[-2], refs[-1]
    start = 0
    for c, rows in enumerate(CHUNKS):
        ra, rb, rest, sa, sb = ins[5 * c : 5 * c + 5]
        for half, (own, near, far) in enumerate(((0, ra, sa), (2, rb, sb))):
            total = rest[own].astype(F32) + near[0].astype(F32) + far[...].astype(F32)
            columns = slice(half * PIECE, (half + 1) * PIECE)
            out_ref[columns, start : start + rows] = jnp.transpose(total[0:rows]).astype(BF16)
            if c == len(CHUNKS) - 1:
                sample_ref[:, columns] = total[rows : rows + 2].astype(BF16)
        start += rows


def in_hbm(*arrays):
    return tuple(pltpu.with_memory_space_constraint(x, pltpu.HBM) for x in arrays)


def call(kernel, name, out_shape, inputs, limit, scalars=0, streamed=None, **more):
    return pl.pallas_call(
        kernel,
        out_shape=out_shape,
        in_specs=[
            SMEM if i < scalars else pl.BlockSpec(memory_space=pl.ANY) if i == streamed else VMEM for i in range(len(inputs))
        ],
        out_specs=jax.tree.map(lambda _: VMEM, out_shape, is_leaf=lambda x: not isinstance(x, tuple)),
        compiler_params=pltpu.CompilerParams(vmem_limit_bytes=limit << 20),
        cost_estimate=pl.CostEstimate(flops=1, bytes_accessed=1, transcendentals=0),
        name=name,
        **more,
    )(*inputs)


SMEM = pl.BlockSpec(memory_space=pltpu.SMEM)
VMEM = pl.BlockSpec(memory_space=pltpu.VMEM)


def shape(dims, dtype=BF16):
    return jax.ShapeDtypeStruct(dims, dtype)


def held(pieces):
    return [pltpu.VMEM((pieces, CH, PIECE), BF16), pltpu.SemaphoreType.DMA((pieces,))]


def swap(x, step):
    return lax.ppermute(x, "head", [(i, i ^ step) for i in range(4)])


def other_core(x):
    return lax.ppermute(x, "core", [(0, 1), (1, 0)])


def local_outputs(part, step, decay, skip, values, gate, inject, read, start=()):
    blocks = TOK // BLOCK // 2
    row = lambda width: pl.BlockSpec((1, width), lambda b: (0, 0))
    tokens = lambda width: pl.BlockSpec((BLOCK, width), lambda b: (b + part * blocks, 0))
    out = pl.BlockSpec((BLOCK, CH), lambda b: (b, 0))
    whole = lambda rows: pl.BlockSpec((rows, CH), lambda b: (0, 0))
    carry = (pltpu.HBM((STATE, CH), F32), pltpu.HBM((8, CH), F32))
    results = (pltpu.HBM((TOK // 2, CH), BF16),) * 2
    scratch = [pltpu.VMEM((8, CH), F32), pltpu.VMEM((BLOCK, CH), BF16), pltpu.VMEM((BLOCK, CH), F32)]
    if start:
        start_specs = [whole(STATE), whole(8)]
        out_specs = (out, out)
        scratch += [pltpu.VMEM((STATE, CH), F32), pltpu.VMEM((8, CH), F32)]
    else:
        start_specs = []
        results += carry
        out_specs = (out, out, whole(STATE), whole(8))
    step, values, gate, inject, read = in_hbm(step, values, gate, inject, read)
    return pl.pallas_call(
        local_kernel,
        grid=(blocks,),
        out_shape=results,
        in_specs=[
            pl.BlockSpec((HEADS, BLOCK), lambda b: (0, b + part * blocks)), row(HEADS), row(CH),
            tokens(CH), tokens(CH), tokens(STATE), tokens(STATE), *start_specs,
        ],
        out_specs=out_specs,
        scratch_shapes=scratch,
        compiler_params=pltpu.CompilerParams(vmem_limit_bytes=20 << 20),
        cost_estimate=pl.CostEstimate(flops=3 << 30, bytes_accessed=20 << 20, transcendentals=2 << 20),
        name="local_outputs",
    )(step, decay, skip, values, gate, inject, read, *start)


def per_device(
    prompt_values, prompt_gate, prompt_inject, prompt_read, prompt_step, decay_log, skip_gain, norm_weight, out_weight,
    sample_values, sample_gate, sample_inject, sample_read, sample_step, sample_length,
):
    inject = prompt_inject.reshape(TOK, STATE)
    read = prompt_read.reshape(TOK, STATE)
    decay = decay_log.reshape(1, HEADS)
    skip = jnp.repeat(skip_gain, HEAD_DIM).reshape(1, CH)
    norm = norm_weight.reshape(1, CH)
    s_read = sample_read.reshape(2, SLEN, STATE)
    s_inject = sample_inject.reshape(2, SLEN, STATE)
    slices_shape = shape((16, ROWS, 128))

    keep, send = call(
        end_state_kernel, "end_state", (slices_shape,) * 2,
        (sample_length, *in_hbm(prompt_step, decay, prompt_values, inject, s_read)), 24, 1,
        scratch_shapes=[pltpu.VMEM((TOK, 1024), BF16)],
    )
    sibling = other_core(send)
    joined = call(join_cores_kernel, "join_cores", slices_shape, (keep, sibling), 16)
    joined, step_1, s_step = lax.optimization_barrier((joined, prompt_step, sample_step.transpose(1, 0, 2)))
    slices = lax.all_to_all(joined, ("y", "x"), 0, 0, tiled=True)
    scaled_1, gain_1, *carry = local_outputs(
        0, step_1, decay, skip, prompt_values, prompt_gate, inject, read
    )
    sample = call(
        sample_kernel, "sample_outputs", (pltpu.HBM((16, CH), F32),) * 3,
        (sample_length, *in_hbm(s_step, decay, skip, sample_values, sample_gate, s_inject, s_read)), 16, 1,
    )
    slices, scaled_1, sample = lax.optimization_barrier((slices, scaled_1, sample))
    prefix = call(prefix_kernel, "prefix", slices_shape, (slices,), 16)
    prefix, step_2 = lax.optimization_barrier((prefix, prompt_step))
    back = lax.all_to_all(prefix, ("y", "x"), 0, 0, tiled=True)
    scaled_2, gain_2 = local_outputs(
        1, step_2, decay, skip, prompt_values, prompt_gate, inject, read, carry
    )
    back, scaled_2 = lax.optimization_barrier((back, scaled_2))
    mine, send = call(
        split_cores_kernel, "split_cores", (shape((272, 1024)), slices_shape), (back, keep, sibling), 16
    )
    theirs = other_core(send)

    weight = pltpu.with_memory_space_constraint(out_weight, pltpu.HBM)
    scaled = (scaled_1, scaled_2)
    gain = (gain_1, gain_2)
    state = call(join_halves_kernel, "join_halves", shape((272, CH)), (mine, theirs), 8)
    near, rests = [], []
    for c, rows in enumerate(CHUNKS):
        last = c == len(CHUNKS) - 1
        size = rows + (16 if last else 0)
        *now, normed = call(
            functools.partial(chunk_kernel, c), "chunk", (shape((2, size, PIECE)),) * 2 + (shape((size, CH)),),
            (state, read, scaled[c], gain[c], norm, weight, *(sample if last else ())), 40, streamed=5, scratch_shapes=held(4),
        )
        near.append(lax.optimization_barrier((swap(now[0], 1), swap(now[1], 3))))
        rests.append(
            call(rest_kernel, "rest", shape((4, size, PIECE)), (normed, weight), 40, streamed=1, scratch_shapes=held(4))
        )

    ends = []
    for rest, (a, b) in zip(rests, near):
        a_on, b_on = call(onward_kernel, "onward", (shape(a.shape[1:]),) * 2, (a, b, rest), 8)
        ends += [a, b, rest, *lax.optimization_barrier((swap(a_on, 3), swap(b_on, 1)))]
    prompt_mixed, sample_mixed = call(
        finish_kernel, "finish", (shape((1024, TOK)), shape((2, 1024))), tuple(ends), 24
    )
    return prompt_mixed, sample_mixed.T


def solution(mesh):
    split = Mesh(mesh.devices.reshape(4, 4, 2, mesh.shape["head"]), ("y", "x", "core", "head"))
    return jax.shard_map(
        per_device,
        mesh=split,
        in_specs=(
            P(CTX, "head"), P(CTX, "head"), P(CTX, "head", None), P(CTX, "head", None), P("head", CTX),
            P("head"), P("head"), P("head"), P("head", None),
            P(CTX, None, "head"), P(CTX, None, "head"), P(CTX, None, "head", None), P(CTX, None, "head", None),
            P("head", CTX, None), P(CTX),
        ),
        out_specs=(P("head", CTX), P("head", CTX)),
        check_vma=False,
    )
```

```python
import functools

import jax
import jax.numpy as jnp
from jax import lax
from jax.experimental import pallas as pl
from jax.experimental.pallas import tpu as pltpu
from jax.sharding import Mesh
from jax.sharding import PartitionSpec as P

HEADS = 32
HEAD_DIM = 64
STATE = 256
BLOCK = 128
SLEN = 16
TOK = 512
CH = HEADS * HEAD_DIM
PIECE = 512
HALF = TOK // 2
ROWS = 144
CTX = ("y", "x", "core")
F32 = jnp.float32
BF16 = jnp.bfloat16
EXACT = lax.Precision.HIGHEST
CHUNKS = ((256, 256), (0, 256))


def softplus(v):
    return jnp.maximum(v, 0.0) + jnp.log1p(jnp.exp(-jnp.abs(v)))


def iota(shape, dim):
    return lax.broadcasted_iota(jnp.int32, shape, dim)


def column(row):
    n = row.shape[1]
    square = jnp.broadcast_to(row, (n, n))
    return jnp.sum(jnp.where(iota((n, n), 0) == iota((n, n), 1), square, 0.0), axis=1, keepdims=True)


def tokens_first(x):
    pad = jnp.zeros((128 - x.shape[0], x.shape[1]), F32)
    return jnp.transpose(jnp.concatenate([x, pad], axis=0))


def per_pair(columns, pair, shape, low):
    first = jnp.broadcast_to(columns[:, 2 * pair : 2 * pair + 1], shape)
    second = jnp.broadcast_to(columns[:, 2 * pair + 1 : 2 * pair + 2], shape)
    return jnp.where(low, first, second)


def three_parts(x):
    hi = x.astype(BF16).astype(F32)
    mid = (x - hi).astype(BF16).astype(F32)
    lo = (x - hi - mid).astype(BF16).astype(F32)
    return hi, mid, lo


def decay_of(tail):
    return tail[8:9] + tail[9:10] + tail[10:11]


def with_decay(tail, decay):
    row = iota((16, 128), 0)
    hi, mid, lo = three_parts(decay)
    tail = jnp.where(row == 8, hi, tail)
    tail = jnp.where(row == 9, mid, tail)
    return jnp.where(row == 10, lo, tail)


def end_state_kernel(length, step_ref, decay_ref, values_ref, inject_ref, read_ref, keep_ref, send_ref, scaled):
    core = lax.axis_index("core")
    step = softplus(step_ref[...])
    logs = step * -jnp.exp(column(decay_ref[...]))
    later = (iota((BLOCK, BLOCK), 0) > iota((BLOCK, BLOCK), 1)).astype(F32)
    after = jnp.zeros((HEADS, 1), F32)
    parts = []
    for b in reversed(range(TOK // BLOCK)):
        here = logs[:, b * BLOCK : (b + 1) * BLOCK]
        parts.append(jnp.dot(here, later, precision=EXACT, preferred_element_type=F32) + after)
        after = after + jnp.sum(here, axis=1, keepdims=True)
    weight = tokens_first(jnp.exp(jnp.concatenate(parts[::-1], axis=1)) * step)
    total = tokens_first(jnp.broadcast_to(jnp.exp(after), (HEADS, 128)))[0:8]
    inject_t = jnp.transpose(inject_ref[...].astype(F32)).astype(BF16)
    low = iota((TOK, 128), 1) < HEAD_DIM
    low_row = iota((8, 128), 1) < HEAD_DIM
    row = iota((16, 128), 0)
    tails = []
    for half in range(2):
        lanes = slice(half * 128, (half + 1) * 128)
        tail = jnp.zeros((16, 128), F32)
        for s in range(2):
            last = iota((SLEN, 128), 0) == length[s] - 1
            picked = jnp.sum(jnp.where(last, read_ref[s, :, lanes].astype(F32), 0.0), axis=0, keepdims=True)
            tail = jnp.where(row == 2 * core + s, picked, tail)
        tails.append(tail)
    for half in range(2):
        for q in range(8):
            pair = half * 8 + q
            lanes = slice(pair * 128, (pair + 1) * 128)
            w = per_pair(weight, pair, (TOK, 128), low)
            scaled[:, q * 128 : (q + 1) * 128] = (values_ref[:, lanes].astype(F32) * w).astype(BF16)
        state = jnp.dot(inject_t, scaled[...], preferred_element_type=F32).astype(BF16)

        def put(out_ref, half=half, state=state):
            for q in range(8):
                decay = per_pair(total, half * 8 + q, (8, 128), low_row)[0:1]
                for n in range(2):
                    out_ref[2 * q + n, 0:128, :] = state[n * 128 : (n + 1) * 128, q * 128 : (q + 1) * 128]
                    out_ref[2 * q + n, 128:ROWS, :] = with_decay(tails[n], decay).astype(BF16)

        @pl.when(core == half)
        def _(put=put):
            put(keep_ref)

        @pl.when(core != half)
        def _(put=put):
            put(send_ref)


def join_cores_kernel(own_ref, sib_ref, out_ref):
    first = lax.axis_index("core") == 0
    row = iota((16, 128), 0)
    for k in range(16):
        own_tail = own_ref[k, 128:ROWS, :].astype(F32)
        sib_tail = sib_ref[k, 128:ROWS, :].astype(F32)
        own_decay, sib_decay = decay_of(own_tail), decay_of(sib_tail)
        own_weight = jnp.where(first, sib_decay, 1.0)
        sib_weight = jnp.where(first, 1.0, own_decay)
        out_ref[k, 0:128, :] = (
            own_ref[k, 0:128, :].astype(F32) * own_weight + sib_ref[k, 0:128, :].astype(F32) * sib_weight
        ).astype(BF16)
        tail = jnp.where(row < 8, own_tail + sib_tail, 0.0)
        out_ref[k, 128:ROWS, :] = with_decay(tail, own_decay * sib_decay).astype(BF16)


def prefix_kernel(in_ref, out_ref):
    state = jnp.zeros((128, 128), F32)
    for i in range(16):
        out_ref[i, 0:128, :] = state.astype(BF16)
        decay = decay_of(in_ref[i, 128:ROWS, :].astype(F32))
        state = state * decay + in_ref[i, 0:128, :].astype(F32)
    final = state.astype(BF16)
    for i in range(16):
        out_ref[i, 128:ROWS, :] = jnp.dot(
            in_ref[i, 128:ROWS, :], final, preferred_element_type=F32
        ).astype(BF16)


def split_cores_kernel(back_ref, own_ref, sib_ref, mine_ref, send_ref):
    first = lax.axis_index("core") == 0
    for k in range(16):
        q, n = k // 2, k % 2
        arrived = back_ref[k, 0:128, :].astype(F32)
        own_decay = decay_of(own_ref[k, 128:ROWS, :].astype(F32))
        sib_decay = decay_of(sib_ref[k, 128:ROWS, :].astype(F32))
        decay = jnp.where(first, own_decay, sib_decay)
        state = jnp.where(first, own_ref[k, 0:128, :].astype(F32), sib_ref[k, 0:128, :].astype(F32))
        second = arrived * decay + state
        mine_ref[n * 128 : (n + 1) * 128, q * 128 : (q + 1) * 128] = jnp.where(first, arrived, second).astype(BF16)
        send_ref[k, 0:128, :] = jnp.where(first, second, arrived).astype(BF16)
        send_ref[k, 128:ROWS, :] = back_ref[k, 128:ROWS, :]
    for q in range(8):
        mine_ref[256:272, q * 128 : (q + 1) * 128] = (
            back_ref[2 * q, 128:ROWS, :].astype(F32) + back_ref[2 * q + 1, 128:ROWS, :].astype(F32)
        ).astype(BF16)


def local_kernel(
    part, step_ref, decay_ref, skip_ref, values_ref, gate_ref, inject_ref, read_ref, *refs
):
    if part == 0:
        scaled_ref, gain_ref, carry, carry_before, ends, weighted, carried, state, before = refs
    else:
        start, start_before, scaled_ref, gain_ref, ends, weighted, carried, state, before = refs

    @pl.when(pl.program_id(0) == 0)
    def _():
        if part == 0:
            state[...] = jnp.zeros_like(state)
            before[...] = jnp.ones_like(before)
        else:
            state[...] = start[...].astype(F32)
            before[...] = start_before[...]

    step = softplus(step_ref[...])
    logs = step * -jnp.exp(column(decay_ref[...]))
    upto = (iota((BLOCK, BLOCK), 0) <= iota((BLOCK, BLOCK), 1)).astype(F32)
    running = jnp.dot(logs, upto, precision=EXACT, preferred_element_type=F32)
    running_t = tokens_first(running)
    step_t = tokens_first(step)
    read = read_ref[...]
    inject = inject_ref[...]
    inject_t = jnp.transpose(inject.astype(F32)).astype(BF16)
    scores = jnp.dot(read, inject_t, preferred_element_type=F32)
    carried[...] = jnp.dot(read, state[...].astype(BF16), preferred_element_type=F32)
    causal = iota((BLOCK, BLOCK), 0) >= iota((BLOCK, BLOCK), 1)
    low = iota((BLOCK, 128), 1) < HEAD_DIM
    for pair in range(16):
        lanes = slice(pair * 128, (pair + 1) * 128)
        mixing = []
        spread = []
        for h in (2 * pair, 2 * pair + 1):
            mine = jnp.broadcast_to(running_t[:, h : h + 1], (BLOCK, BLOCK))
            gap = jnp.where(causal, mine - running[h : h + 1, :], -1e30)
            mixing.append((scores * jnp.exp(gap)).astype(BF16))
            spread.append(mine)
        now = jnp.where(low, spread[0], spread[1])
        grown = jnp.exp(now)
        values = values_ref[:, lanes].astype(F32)
        stepped = values * per_pair(step_t, pair, (BLOCK, 128), low)
        diagonal = jnp.concatenate([jnp.where(low, stepped, 0.0), jnp.where(low, 0.0, stepped)], axis=0)
        local = jnp.dot(
            jnp.concatenate(mixing, axis=1), diagonal.astype(BF16), preferred_element_type=F32
        )
        out = local + carried[:, lanes] * grown + skip_ref[:, lanes] * values
        gate = gate_ref[:, lanes].astype(F32)
        gate = gate / (1.0 + jnp.exp(-gate))
        scaled_ref[:, lanes] = (out * gate).astype(BF16)
        gain_ref[:, lanes] = (gate * grown * before[0:1, lanes]).astype(BF16)
        end = now[BLOCK - 1 : BLOCK, :]
        weighted[:, lanes] = (stepped * jnp.exp(end - now)).astype(BF16)
        ends[0:1, lanes] = jnp.exp(end)
    state[...] = state[...] * ends[0:1, :] + jnp.dot(inject_t, weighted[...], preferred_element_type=F32)
    before[0:1, :] = before[0:1, :] * ends[0:1, :]
    if part == 0:

        @pl.when(pl.program_id(0) == pl.num_programs(0) - 1)
        def _():
            carry[...] = state[...].astype(BF16)
            carry_before[...] = before[...]


def sample_kernel(
    length, step_ref, decay_ref, skip_ref, values_ref, gate_ref, inject_ref, read_ref, local_ref, grown_ref, gate_out_ref
):
    rate = -jnp.exp(column(decay_ref[...]))
    row = iota((16, CH), 0)
    place = iota((SLEN, 128), 0)
    place_wide = iota((SLEN, STATE), 0)
    narrow = []
    for s in range(2):
        last = length[s] - 1
        step = softplus(step_ref[s])
        logs = step * rate
        pad = jnp.zeros((HEADS, 128 - SLEN), F32)
        step_t = tokens_first(jnp.concatenate([step, pad], axis=1))[0:SLEN]
        logs_t = tokens_first(jnp.concatenate([logs, pad], axis=1))[0:SLEN]
        logs_t = jnp.where(place <= last, logs_t, 0.0)
        gap = jnp.zeros((SLEN, 128), F32)
        for k in range(SLEN):
            gap = gap + jnp.where(place < k, logs_t[k : k + 1], 0.0)
        whole = jnp.sum(logs_t, axis=0, keepdims=True)
        read = jnp.sum(jnp.where(place_wide == last, read_ref[s].astype(F32), 0.0), axis=0, keepdims=True)
        scores = jnp.sum(inject_ref[s].astype(F32) * read, axis=1, keepdims=True)
        narrow.append(jnp.where(place <= last, scores * jnp.exp(gap) * step_t, 0.0))
        narrow.append(jnp.broadcast_to(jnp.exp(whole), (SLEN, 128)))
    spread = (iota((128, CH), 1) // HEAD_DIM == iota((128, CH), 0)).astype(BF16)
    parts = jnp.concatenate(three_parts(jnp.concatenate(narrow, axis=0)), axis=0).astype(BF16)
    wide = jnp.dot(parts, spread, preferred_element_type=F32)
    wide = wide[0:64] + wide[64:128] + wide[128:192]
    local_all = jnp.zeros((16, CH), F32)
    grown_all = jnp.zeros((16, CH), F32)
    gate_all = jnp.zeros((16, CH), F32)
    for s in range(2):
        values = values_ref[s].astype(F32)
        at_last = iota((SLEN, CH), 0) == length[s] - 1
        picked = jnp.sum(jnp.where(at_last, values, 0.0), axis=0, keepdims=True)
        gate = jnp.sum(jnp.where(at_last, gate_ref[s].astype(F32), 0.0), axis=0, keepdims=True)
        local = jnp.sum(wide[32 * s : 32 * s + SLEN] * values, axis=0, keepdims=True) + skip_ref[...] * picked
        local_all = jnp.where(row == s, local, local_all)
        grown_all = jnp.where(row == s, wide[32 * s + SLEN : 32 * s + SLEN + 1], grown_all)
        gate_all = jnp.where(row == s, gate / (1.0 + jnp.exp(-gate)), gate_all)
    local_ref[...] = local_all
    grown_ref[...] = grown_all
    gate_out_ref[...] = gate_all


def normalize(gated, weight):
    mean = jnp.sum(gated * gated, axis=1, keepdims=True) * (1.0 / CH)
    return (gated * lax.rsqrt(mean + 1e-05) * weight).astype(BF16)


FIRST = ((1, 0), (2, 0), (3, 1), (2, 1))
REST = ((3, 0), (1, 1), (0, 0), (0, 1))


def fetch_kernel(pieces, weight_ref, out_ref, sems):
    z = lax.axis_index("head")
    copies = []
    for i, (flip, half) in enumerate(pieces):
        at = pl.multiple_of(((z ^ flip) * 2 + half) * PIECE, PIECE)
        copies.append(pltpu.make_async_copy(weight_ref.at[:, pl.ds(at, PIECE)], out_ref.at[i], sems.at[i]))
    for copy in copies:
        copy.start()
    for copy in copies:
        copy.wait()


def fetch(pieces, weight):
    out = pl.pallas_call(
        functools.partial(fetch_kernel, pieces),
        out_shape=pltpu.VMEM((4, CH, PIECE), BF16),
        in_specs=[pl.BlockSpec(memory_space=pl.ANY)],
        out_specs=VMEM,
        scratch_shapes=[pltpu.SemaphoreType.DMA((4,))],
        compiler_params=pltpu.CompilerParams(vmem_limit_bytes=12 << 20),
        name="fetch_weight",
    )(*in_hbm(weight))
    return pltpu.with_memory_space_constraint(out, pltpu.VMEM)


def project(normed, weight_ref, outs):
    for i, (ref, k) in enumerate(outs):
        ref[k] = jnp.dot(normed[...], weight_ref[i], preferred_element_type=F32).astype(BF16)


def gate_and_normalize(place, state_ref, read_ref, scaled_ref, gain_ref, norm_ref, normed):
    start, rows = CHUNKS[place]
    arrived = jnp.dot(read_ref[start : start + rows, :], state_ref[0:STATE, :], preferred_element_type=F32)
    here = slice(start % HALF, start % HALF + rows)
    gated = scaled_ref[here, :].astype(F32) + arrived * gain_ref[here, :].astype(F32)
    normed[0:rows, :] = normalize(gated, norm_ref[...])


def join_halves_kernel(mine_ref, theirs_ref, state_ref):
    core = lax.axis_index("core")
    state_ref[:, pl.ds(pl.multiple_of(core * 1024, 1024), 1024)] = mine_ref[...]
    for q in range(8):
        lanes = pl.ds(pl.multiple_of((1 - core) * 1024 + q * 128, 128), 128)
        for n in range(2):
            state_ref[n * 128 : (n + 1) * 128, lanes] = theirs_ref[2 * q + n, 0:128, :]
        state_ref[256:272, lanes] = (
            theirs_ref[2 * q, 128:ROWS, :].astype(F32) + theirs_ref[2 * q + 1, 128:ROWS, :].astype(F32)
        ).astype(BF16)


def chunk_kernel(place, state_ref, read_ref, scaled_ref, gain_ref, norm_ref, weight_ref, *refs):
    sample, (first_ref, second_ref, normed_ref) = refs[:-3], refs[-3:]
    gate_and_normalize(place, state_ref, read_ref, scaled_ref, gain_ref, norm_ref, normed_ref)
    if sample:
        local_ref, grown_ref, gate_ref = sample
        readings = state_ref[256:272, :].astype(F32)
        moved = jnp.concatenate([readings[2:16], readings[0:2]], axis=0)
        readings = jnp.where(lax.axis_index("core") == 0, readings, moved)
        sampled = (local_ref[...] + readings * grown_ref[...]) * gate_ref[...]
        rows = CHUNKS[place][1]
        normed_ref[rows : rows + 16, :] = normalize(sampled, norm_ref[...])
    project(normed_ref, weight_ref, ((first_ref, 0), (first_ref, 1), (second_ref, 0), (second_ref, 1)))


def rest_kernel(normed_ref, weight_ref, rest_ref):
    project(normed_ref, weight_ref, ((rest_ref, 1), (rest_ref, 3), (rest_ref, 0), (rest_ref, 2)))


def onward_kernel(a_ref, b_ref, rest_ref, a_out, b_out):
    a_out[...] = (rest_ref[1].astype(F32) + a_ref[1].astype(F32)).astype(BF16)
    b_out[...] = (rest_ref[3].astype(F32) + b_ref[1].astype(F32)).astype(BF16)


def finish_kernel(*refs):
    ins, out_ref, sample_ref = refs[:-2], refs[-2], refs[-1]
    for place, (start, rows) in enumerate(CHUNKS):
        ra, rb, rest, sa, sb = ins[5 * place : 5 * place + 5]
        for half, (own, near, far) in enumerate(((0, ra, sa), (2, rb, sb))):
            total = rest[own].astype(F32) + near[0].astype(F32) + far[...].astype(F32)
            columns = slice(half * PIECE, (half + 1) * PIECE)
            out_ref[columns, start : start + rows] = jnp.transpose(total[0:rows]).astype(BF16)
            if place == 0:
                sample_ref[:, columns] = total[rows : rows + 2].astype(BF16)


def in_hbm(*arrays):
    return tuple(pltpu.with_memory_space_constraint(x, pltpu.HBM) for x in arrays)


def call(kernel, name, out_shape, inputs, limit, scalars=0, **more):
    return pl.pallas_call(
        kernel,
        out_shape=out_shape,
        in_specs=[SMEM] * scalars + [VMEM] * (len(inputs) - scalars),
        out_specs=jax.tree.map(lambda _: VMEM, out_shape, is_leaf=lambda x: not isinstance(x, tuple)),
        compiler_params=pltpu.CompilerParams(vmem_limit_bytes=limit << 20),
        cost_estimate=pl.CostEstimate(flops=1, bytes_accessed=1, transcendentals=0),
        name=name,
        **more,
    )(*inputs)


SMEM = pl.BlockSpec(memory_space=pltpu.SMEM)
VMEM = pl.BlockSpec(memory_space=pltpu.VMEM)


def shape(dims, dtype=BF16):
    return jax.ShapeDtypeStruct(dims, dtype)


def swap(x, step):
    return lax.ppermute(x, "head", [(i, i ^ step) for i in range(4)])


def other_core(x):
    return lax.ppermute(x, "core", [(0, 1), (1, 0)])


def local_outputs(part, step, decay, skip, values, gate, inject, read, start=()):
    blocks = TOK // BLOCK // 2
    row = lambda width: pl.BlockSpec((1, width), lambda b: (0, 0))
    tokens = lambda width: pl.BlockSpec((BLOCK, width), lambda b: (b + part * blocks, 0))
    out = pl.BlockSpec((BLOCK, CH), lambda b: (b, 0))
    whole = lambda rows: pl.BlockSpec((rows, CH), lambda b: (0, 0))
    carry = (pltpu.HBM((STATE, CH), BF16), pltpu.HBM((8, CH), F32))
    results = (pltpu.HBM((TOK // 2, CH), BF16),) * 2
    scratch = [
        pltpu.VMEM((8, CH), F32), pltpu.VMEM((BLOCK, CH), BF16), pltpu.VMEM((BLOCK, CH), F32),
        pltpu.VMEM((STATE, CH), F32), pltpu.VMEM((8, CH), F32),
    ]
    if start:
        start_specs = [whole(STATE), whole(8)]
        out_specs = (out, out)
    else:
        start_specs = []
        results += carry
        out_specs = (out, out, whole(STATE), whole(8))
    step, values, gate, inject, read, *start = in_hbm(step, values, gate, inject, read, *start)
    return pl.pallas_call(
        functools.partial(local_kernel, part),
        grid=(blocks,),
        out_shape=results,
        in_specs=[
            pl.BlockSpec((HEADS, BLOCK), lambda b: (0, b + part * blocks)), row(HEADS), row(CH),
            tokens(CH), tokens(CH), tokens(STATE), tokens(STATE), *start_specs,
        ],
        out_specs=out_specs,
        scratch_shapes=scratch,
        compiler_params=pltpu.CompilerParams(vmem_limit_bytes=20 << 20),
        cost_estimate=pl.CostEstimate(flops=3 << 30, bytes_accessed=20 << 20, transcendentals=2 << 20),
        name="local_outputs",
    )(step, decay, skip, values, gate, inject, read, *start)


def per_device(
    prompt_values, prompt_gate, prompt_inject, prompt_read, prompt_step, decay_log, skip_gain, norm_weight, out_weight,
    sample_values, sample_gate, sample_inject, sample_read, sample_step, sample_length,
):
    inject = prompt_inject.reshape(TOK, STATE)
    read = prompt_read.reshape(TOK, STATE)
    decay = decay_log.reshape(1, HEADS)
    skip = jnp.repeat(skip_gain, HEAD_DIM).reshape(1, CH)
    norm = norm_weight.reshape(1, CH)
    s_read = sample_read.reshape(2, SLEN, STATE)
    s_inject = sample_inject.reshape(2, SLEN, STATE)
    slices_shape = shape((16, ROWS, 128))

    keep, send = call(
        end_state_kernel, "end_state", (slices_shape,) * 2,
        (sample_length, *in_hbm(prompt_step, decay, prompt_values, inject, s_read)), 24, 1,
        scratch_shapes=[pltpu.VMEM((TOK, 1024), BF16)],
    )
    sibling = other_core(send)
    joined = call(join_cores_kernel, "join_cores", slices_shape, (keep, sibling), 16)
    joined, step_1, s_step = lax.optimization_barrier((joined, prompt_step, sample_step.transpose(1, 0, 2)))
    slices = lax.all_to_all(joined, ("y", "x"), 0, 0, tiled=True)
    scaled_1, gain_1, *carry = local_outputs(
        0, step_1, decay, skip, prompt_values, prompt_gate, inject, read
    )
    sample = call(
        sample_kernel, "sample_outputs", (pltpu.HBM((16, CH), F32),) * 3,
        (sample_length, *in_hbm(s_step, decay, skip, sample_values, sample_gate, s_inject, s_read)), 16, 1,
    )
    slices, scaled_1, sample = lax.optimization_barrier((slices, scaled_1, sample))
    prefix = call(prefix_kernel, "prefix", slices_shape, (slices,), 16)
    prefix, step_2 = lax.optimization_barrier((prefix, prompt_step))
    back = lax.all_to_all(prefix, ("y", "x"), 0, 0, tiled=True)
    scaled_2, gain_2 = local_outputs(
        1, step_2, decay, skip, prompt_values, prompt_gate, inject, read, carry
    )
    back, scaled_2, weight = lax.optimization_barrier((back, scaled_2, out_weight))
    mine, send = call(
        split_cores_kernel, "split_cores", (shape((272, 1024)), slices_shape), (back, keep, sibling), 16
    )
    theirs = other_core(send)

    first_columns = fetch(FIRST, weight)
    scaled = (scaled_1, scaled_2)
    gain = (gain_1, gain_2)
    state = call(join_halves_kernel, "join_halves", shape((272, CH)), (mine, theirs), 8)

    def chunk(place, *sample):
        start, rows = CHUNKS[place]
        size = rows + (16 if sample else 0)
        *sent, normed = call(
            functools.partial(chunk_kernel, place), "chunk", (shape((2, size, PIECE)),) * 2 + (shape((size, CH)),),
            (state, read, scaled[start // HALF], gain[start // HALF], norm, first_columns, *sample), 24,
        )
        near = lax.optimization_barrier((swap(sent[0], 1), swap(sent[1], 3)))
        return normed, near

    def exchange(normed, near, rest_columns):
        rest = call(rest_kernel, "rest", shape((4, normed.shape[0], PIECE)), (normed, rest_columns), 24)
        a, b = near
        a_on, b_on = call(onward_kernel, "onward", (shape(a.shape[1:]),) * 2, (a, b, rest), 8)
        return (a, b, rest, *lax.optimization_barrier((swap(a_on, 3), swap(b_on, 1))))

    normed_1, near_1 = chunk(1)
    rest_columns = fetch(REST, weight)
    normed_0, near_0 = chunk(0, *sample)
    parts = [
        exchange(normed, near, rest_columns)
        for normed, near in ((normed_0, near_0), (normed_1, near_1))
    ]
    prompt_mixed, sample_mixed = call(
        finish_kernel, "finish", (shape((1024, TOK)), shape((2, 1024))), tuple(sum(parts, ())), 16
    )
    return prompt_mixed, sample_mixed.T


def solution(mesh):
    split = Mesh(mesh.devices.reshape(4, 4, 2, mesh.shape["head"]), ("y", "x", "core", "head"))
    return jax.shard_map(
        per_device,
        mesh=split,
        in_specs=(
            P(CTX, "head"), P(CTX, "head"), P(CTX, "head", None), P(CTX, "head", None), P("head", CTX),
            P("head"), P("head"), P("head"), P("head", None),
            P(CTX, None, "head"), P(CTX, None, "head"), P(CTX, None, "head", None), P(CTX, None, "head", None),
            P("head", CTX, None), P(CTX),
        ),
        out_specs=(P("head", CTX), P("head", CTX)),
        check_vma=False,
    )
```

```python
import functools

import jax
import jax.numpy as jnp
from jax import lax
from jax.experimental import pallas as pl
from jax.experimental.pallas import tpu as pltpu
from jax.sharding import Mesh
from jax.sharding import PartitionSpec as P

HEADS = 32
HEAD_DIM = 64
STATE = 256
BLOCK = 128
SLEN = 16
TOK = 512
CH = HEADS * HEAD_DIM
PIECE = 512
HALF = TOK // 2
ROWS = 144
CTX = ("y", "x", "core")
F32 = jnp.float32
BF16 = jnp.bfloat16
EXACT = lax.Precision.HIGHEST
LOG2E = 1.4426950408889634
CHUNKS = ((256, 256), (0, 256))
LEADING = 0


def softplus(v):
    return jnp.maximum(v, 0.0) + jnp.log1p(jnp.exp(-jnp.abs(v)))


def iota(shape, dim):
    return lax.broadcasted_iota(jnp.int32, shape, dim)


def column(row):
    n = row.shape[1]
    square = jnp.broadcast_to(row, (n, n))
    return jnp.sum(jnp.where(iota((n, n), 0) == iota((n, n), 1), square, 0.0), axis=1, keepdims=True)


def tokens_first(x):
    pad = jnp.zeros((128 - x.shape[0], x.shape[1]), F32)
    return jnp.transpose(jnp.concatenate([x, pad], axis=0))


def per_pair(columns, pair, shape, low):
    first = jnp.broadcast_to(columns[:, 2 * pair : 2 * pair + 1], shape)
    second = jnp.broadcast_to(columns[:, 2 * pair + 1 : 2 * pair + 2], shape)
    return jnp.where(low, first, second)


def three_parts(x):
    hi = x.astype(BF16).astype(F32)
    mid = (x - hi).astype(BF16).astype(F32)
    lo = (x - hi - mid).astype(BF16).astype(F32)
    return hi, mid, lo


def decay_of(tail):
    return tail[8:9] + tail[9:10] + tail[10:11]


def with_decay(tail, decay):
    row = iota((16, 128), 0)
    hi, mid, lo = three_parts(decay)
    tail = jnp.where(row == 8, hi, tail)
    tail = jnp.where(row == 9, mid, tail)
    return jnp.where(row == 10, lo, tail)


def end_state_kernel(
    length, step_any, decay_ref, values_any, inject_any, read_ref, keep_ref, send_ref,
    scaled, step_ref, values_ref, inject_ref, sems,
):
    copies = [
        pltpu.make_async_copy(step_any, step_ref, sems.at[0]),
        pltpu.make_async_copy(inject_any, inject_ref, sems.at[1]),
    ]
    for half in range(2):
        lanes = slice(half * 1024, (half + 1) * 1024)
        copies.append(pltpu.make_async_copy(values_any.at[:, lanes], values_ref.at[:, lanes], sems.at[2 + half]))
    for copy in copies:
        copy.start()
    copies[0].wait()
    core = lax.axis_index("core")
    step = softplus(step_ref[...])
    logs = step * -jnp.exp(column(decay_ref[...]))
    later = (iota((BLOCK, BLOCK), 0) > iota((BLOCK, BLOCK), 1)).astype(F32)
    after = jnp.zeros((HEADS, 1), F32)
    parts = []
    for b in reversed(range(TOK // BLOCK)):
        here = logs[:, b * BLOCK : (b + 1) * BLOCK]
        parts.append(jnp.dot(here, later, precision=EXACT, preferred_element_type=F32) + after)
        after = after + jnp.sum(here, axis=1, keepdims=True)
    weight = tokens_first(jnp.exp(jnp.concatenate(parts[::-1], axis=1)) * step)
    total = tokens_first(jnp.broadcast_to(jnp.exp(after), (HEADS, 128)))[0:8]
    copies[1].wait()
    inject_t = jnp.transpose(inject_ref[...].astype(F32)).astype(BF16)
    low = iota((TOK, 128), 1) < HEAD_DIM
    low_row = iota((8, 128), 1) < HEAD_DIM
    row = iota((16, 128), 0)
    tails = []
    for half in range(2):
        lanes = slice(half * 128, (half + 1) * 128)
        tail = jnp.zeros((16, 128), F32)
        for s in range(2):
            last = iota((SLEN, 128), 0) == length[s] - 1
            picked = jnp.sum(jnp.where(last, read_ref[s, :, lanes].astype(F32), 0.0), axis=0, keepdims=True)
            tail = jnp.where(row == 2 * core + s, picked, tail)
        tails.append(tail)
    for half in range(2):
        copies[2 + half].wait()
        for q in range(8):
            pair = half * 8 + q
            lanes = slice(pair * 128, (pair + 1) * 128)
            w = per_pair(weight, pair, (TOK, 128), low)
            scaled[:, q * 128 : (q + 1) * 128] = (values_ref[:, lanes].astype(F32) * w).astype(BF16)
        state = jnp.dot(inject_t, scaled[...], preferred_element_type=F32).astype(BF16)

        def put(out_ref, half=half, state=state):
            for q in range(8):
                decay = per_pair(total, half * 8 + q, (8, 128), low_row)[0:1]
                for n in range(2):
                    out_ref[2 * q + n, 0:128, :] = state[n * 128 : (n + 1) * 128, q * 128 : (q + 1) * 128]
                    out_ref[2 * q + n, 128:ROWS, :] = with_decay(tails[n], decay).astype(BF16)

        @pl.when(core == half)
        def _(put=put):
            put(keep_ref)

        @pl.when(core != half)
        def _(put=put):
            put(send_ref)


def join_cores_kernel(own_ref, sib_ref, out_ref):
    first = lax.axis_index("core") == 0
    row = iota((16, 128), 0)
    for k in range(16):
        own_tail = own_ref[k, 128:ROWS, :].astype(F32)
        sib_tail = sib_ref[k, 128:ROWS, :].astype(F32)
        own_decay, sib_decay = decay_of(own_tail), decay_of(sib_tail)
        own_weight = jnp.where(first, sib_decay, 1.0)
        sib_weight = jnp.where(first, 1.0, own_decay)
        out_ref[k, 0:128, :] = (
            own_ref[k, 0:128, :].astype(F32) * own_weight + sib_ref[k, 0:128, :].astype(F32) * sib_weight
        ).astype(BF16)
        tail = jnp.where(row < 8, own_tail + sib_tail, 0.0)
        out_ref[k, 128:ROWS, :] = with_decay(tail, own_decay * sib_decay).astype(BF16)


def prefix_kernel(in_ref, out_ref):
    state = jnp.zeros((128, 128), F32)
    for i in range(16):
        out_ref[i, 0:128, :] = state.astype(BF16)
        decay = decay_of(in_ref[i, 128:ROWS, :].astype(F32))
        state = state * decay + in_ref[i, 0:128, :].astype(F32)
    final = state.astype(BF16)
    for i in range(16):
        out_ref[i, 128:ROWS, :] = jnp.dot(
            in_ref[i, 128:ROWS, :], final, preferred_element_type=F32
        ).astype(BF16)


def split_cores_kernel(back_ref, own_ref, sib_ref, mine_ref, send_ref):
    first = lax.axis_index("core") == 0
    for k in range(16):
        q, n = k // 2, k % 2
        arrived = back_ref[k, 0:128, :].astype(F32)
        own_decay = decay_of(own_ref[k, 128:ROWS, :].astype(F32))
        sib_decay = decay_of(sib_ref[k, 128:ROWS, :].astype(F32))
        decay = jnp.where(first, own_decay, sib_decay)
        state = jnp.where(first, own_ref[k, 0:128, :].astype(F32), sib_ref[k, 0:128, :].astype(F32))
        second = arrived * decay + state
        mine_ref[n * 128 : (n + 1) * 128, q * 128 : (q + 1) * 128] = jnp.where(first, arrived, second).astype(BF16)
        send_ref[k, 0:128, :] = jnp.where(first, second, arrived).astype(BF16)
        send_ref[k, 128:ROWS, :] = back_ref[k, 128:ROWS, :]
    for q in range(8):
        mine_ref[256:272, q * 128 : (q + 1) * 128] = (
            back_ref[2 * q, 128:ROWS, :].astype(F32) + back_ref[2 * q + 1, 128:ROWS, :].astype(F32)
        ).astype(BF16)


def local_kernel(
    part, step_ref, decay_ref, skip_ref, values_ref, gate_ref, inject_ref, read_ref, *refs
):
    if part == 0:
        scaled_ref, gain_ref, carry, carry_before, ends, weighted, carried, state, before = refs
    else:
        start, start_before, scaled_ref, gain_ref, ends, weighted, carried, state, before = refs

    @pl.when(pl.program_id(0) == 0)
    def _():
        if part == 0:
            state[...] = jnp.zeros_like(state)
            before[...] = jnp.ones_like(before)
        else:
            state[...] = start[...].astype(F32)
            before[...] = start_before[...]

    step = softplus(step_ref[...])
    logs = step * -jnp.exp(column(decay_ref[...]))
    upto = (iota((BLOCK, BLOCK), 0) <= iota((BLOCK, BLOCK), 1)).astype(F32)
    running = jnp.dot(logs, upto, precision=EXACT, preferred_element_type=F32) * LOG2E
    running_t = tokens_first(running)
    step_t = tokens_first(step)
    read = read_ref[...]
    inject = inject_ref[...]
    inject_t = jnp.transpose(inject.astype(F32)).astype(BF16)
    scores = jnp.dot(read, inject_t, preferred_element_type=F32)
    carried[...] = jnp.dot(read, state[...].astype(BF16), preferred_element_type=F32)
    causal = iota((BLOCK, BLOCK), 0) >= iota((BLOCK, BLOCK), 1)
    low = iota((BLOCK, 128), 1) < HEAD_DIM
    for pair in range(16):
        lanes = slice(pair * 128, (pair + 1) * 128)
        mixing = []
        spread = []
        for h in (2 * pair, 2 * pair + 1):
            mine = jnp.broadcast_to(running_t[:, h : h + 1], (BLOCK, BLOCK))
            gap = jnp.where(causal, mine - running[h : h + 1, :], -1e30)
            mixing.append((scores * jnp.exp2(gap)).astype(BF16))
            spread.append(mine)
        now = jnp.where(low, spread[0], spread[1])
        grown = jnp.exp2(now)
        values = values_ref[:, lanes].astype(F32)
        stepped = values * per_pair(step_t, pair, (BLOCK, 128), low)
        diagonal = jnp.concatenate([jnp.where(low, stepped, 0.0), jnp.where(low, 0.0, stepped)], axis=0)
        local = jnp.dot(
            jnp.concatenate(mixing, axis=1), diagonal.astype(BF16), preferred_element_type=F32
        )
        skip = per_pair(skip_ref[...], pair, (1, 128), low[0:1])
        out = local + carried[:, lanes] * grown + skip * values
        gate = gate_ref[:, lanes].astype(F32)
        gate = gate / (1.0 + jnp.exp(-gate))
        scaled_ref[:, lanes] = (out * gate).astype(BF16)
        gain_ref[:, lanes] = (gate * grown * before[0:1, lanes]).astype(BF16)
        end = now[BLOCK - 1 : BLOCK, :]
        weighted[:, lanes] = (stepped * jnp.exp2(end - now)).astype(BF16)
        ends[0:1, lanes] = jnp.exp2(end)
    state[...] = state[...] * ends[0:1, :] + jnp.dot(inject_t, weighted[...], preferred_element_type=F32)
    before[0:1, :] = before[0:1, :] * ends[0:1, :]
    if part == 0:

        @pl.when(pl.program_id(0) == pl.num_programs(0) - 1)
        def _():
            carry[...] = state[...].astype(BF16)
            carry_before[...] = before[...]


def sample_kernel(
    length, step_ref, decay_ref, skip_ref, values_ref, gate_ref, inject_ref, read_ref, local_ref, grown_ref, gate_out_ref
):
    rate = -jnp.exp(column(decay_ref[...]))
    row = iota((16, CH), 0)
    place = iota((SLEN, 128), 0)
    place_wide = iota((SLEN, STATE), 0)
    narrow = []
    for s in range(2):
        last = length[s] - 1
        step = softplus(step_ref[s])
        logs = step * rate
        pad = jnp.zeros((HEADS, 128 - SLEN), F32)
        step_t = tokens_first(jnp.concatenate([step, pad], axis=1))[0:SLEN]
        logs_t = tokens_first(jnp.concatenate([logs, pad], axis=1))[0:SLEN]
        logs_t = jnp.where(place <= last, logs_t, 0.0)
        gap = jnp.zeros((SLEN, 128), F32)
        for k in range(SLEN):
            gap = gap + jnp.where(place < k, logs_t[k : k + 1], 0.0)
        whole = jnp.sum(logs_t, axis=0, keepdims=True)
        read = jnp.sum(jnp.where(place_wide == last, read_ref[s].astype(F32), 0.0), axis=0, keepdims=True)
        scores = jnp.sum(inject_ref[s].astype(F32) * read, axis=1, keepdims=True)
        narrow.append(jnp.where(place <= last, scores * jnp.exp(gap) * step_t, 0.0))
        narrow.append(jnp.broadcast_to(jnp.exp(whole), (SLEN, 128)))
    skip = jnp.concatenate([skip_ref[...], jnp.zeros((1, 128 - HEADS), F32)], axis=1)
    narrow.append(jnp.broadcast_to(skip, (SLEN, 128)))
    spread = (iota((128, CH), 1) // HEAD_DIM == iota((128, CH), 0)).astype(BF16)
    parts = jnp.concatenate(three_parts(jnp.concatenate(narrow, axis=0)), axis=0).astype(BF16)
    wide = jnp.dot(parts, spread, preferred_element_type=F32)
    wide = wide[0:80] + wide[80:160] + wide[160:240]
    local_all = jnp.zeros((16, CH), F32)
    grown_all = jnp.zeros((16, CH), F32)
    gate_all = jnp.zeros((16, CH), F32)
    for s in range(2):
        values = values_ref[s].astype(F32)
        at_last = iota((SLEN, CH), 0) == length[s] - 1
        picked = jnp.sum(jnp.where(at_last, values, 0.0), axis=0, keepdims=True)
        gate = jnp.sum(jnp.where(at_last, gate_ref[s].astype(F32), 0.0), axis=0, keepdims=True)
        local = jnp.sum(wide[32 * s : 32 * s + SLEN] * values, axis=0, keepdims=True) + wide[64:65] * picked
        local_all = jnp.where(row == s, local, local_all)
        grown_all = jnp.where(row == s, wide[32 * s + SLEN : 32 * s + SLEN + 1], grown_all)
        gate_all = jnp.where(row == s, gate / (1.0 + jnp.exp(-gate)), gate_all)
    local_ref[...] = local_all
    grown_ref[...] = grown_all
    gate_out_ref[...] = gate_all


def normalize(gated, weight):
    mean = jnp.sum(gated * gated, axis=1, keepdims=True) * (1.0 / CH)
    return (gated * lax.rsqrt(mean + 1e-05) * weight).astype(BF16)


FIRST = ((1, 0), (2, 0), (3, 1), (2, 1))
REST = ((3, 0), (1, 1), (0, 0), (0, 1))


def column_copies(pieces, weight_ref, held, sems):
    z = lax.axis_index("head")
    copies = []
    for i, (flip, half) in enumerate(pieces):
        at = pl.multiple_of(((z ^ flip) * 2 + half) * PIECE, PIECE)
        copies.append(pltpu.make_async_copy(weight_ref.at[:, pl.ds(at, PIECE)], held.at[i], sems.at[i]))
    for copy in copies:
        copy.start()
    return copies


def fetch_kernel(pieces, weight_ref, out_ref, sems):
    for copy in column_copies(pieces, weight_ref, out_ref, sems):
        copy.wait()


def resident(x):
    return pltpu.with_memory_space_constraint(x, pltpu.VMEM)


def fetch(pieces, weight):
    out = pl.pallas_call(
        functools.partial(fetch_kernel, pieces),
        out_shape=pltpu.VMEM((len(pieces), CH, PIECE), BF16),
        in_specs=[pl.BlockSpec(memory_space=pl.ANY)],
        out_specs=VMEM,
        scratch_shapes=[pltpu.SemaphoreType.DMA((len(pieces),))],
        compiler_params=pltpu.CompilerParams(vmem_limit_bytes=12 << 20),
        name="fetch_weight",
    )(*in_hbm(weight))
    return resident(out)


def project(normed, columns, outs):
    for column, (ref, k) in zip(columns, outs):
        ref[k] = jnp.dot(normed[...], column[...], preferred_element_type=F32).astype(BF16)


def gate_and_normalize(place, state_ref, read_ref, scaled_ref, gain_ref, norm_ref, normed):
    start, rows = CHUNKS[place]
    arrived = jnp.dot(read_ref[start : start + rows, :], state_ref[0:STATE, :], preferred_element_type=F32)
    here = slice(start % HALF, start % HALF + rows)
    gated = scaled_ref[here, :].astype(F32) + arrived * gain_ref[here, :].astype(F32)
    normed[0:rows, :] = normalize(gated, norm_ref[...])


def join_halves_kernel(mine_ref, theirs_ref, state_ref):
    core = lax.axis_index("core")
    state_ref[:, pl.ds(pl.multiple_of(core * 1024, 1024), 1024)] = mine_ref[...]
    for q in range(8):
        lanes = pl.ds(pl.multiple_of((1 - core) * 1024 + q * 128, 128), 128)
        for n in range(2):
            state_ref[n * 128 : (n + 1) * 128, lanes] = theirs_ref[2 * q + n, 0:128, :]
        state_ref[256:272, lanes] = (
            theirs_ref[2 * q, 128:ROWS, :].astype(F32) + theirs_ref[2 * q + 1, 128:ROWS, :].astype(F32)
        ).astype(BF16)


def chunk_kernel(place, sampled, state_ref, read_ref, scaled_ref, gain_ref, norm_ref, near_ref, far_ref, *refs):
    if place == LEADING:
        *sample, first_ref, second_ref, normed_ref, held, sems = refs
        copies = column_copies(FIRST[2:], far_ref, held, sems)
    else:
        *sample, first_ref, second_ref, normed_ref = refs
        held = far_ref
    gate_and_normalize(place, state_ref, read_ref, scaled_ref, gain_ref, norm_ref, normed_ref)
    if sampled:
        local_ref, grown_ref, gate_ref = sample
        readings = state_ref[256:272, :].astype(F32)
        moved = jnp.concatenate([readings[2:16], readings[0:2]], axis=0)
        readings = jnp.where(lax.axis_index("core") == 0, readings, moved)
        sampled = (local_ref[...] + readings * grown_ref[...]) * gate_ref[...]
        rows = CHUNKS[place][1]
        normed_ref[rows : rows + 16, :] = normalize(sampled, norm_ref[...])
    project(normed_ref, (near_ref.at[0], near_ref.at[1]), ((first_ref, 0), (first_ref, 1)))
    for i in range(2):
        if place == LEADING:
            copies[i].wait()
        project(normed_ref, (held.at[i],), ((second_ref, i),))


def rest_kernel(normed_ref, weight_ref, rest_ref):
    project(normed_ref, [weight_ref.at[i] for i in range(4)], ((rest_ref, 1), (rest_ref, 3), (rest_ref, 0), (rest_ref, 2)))


def onward_kernel(a_ref, b_ref, rest_ref, a_out, b_out):
    a_out[...] = (rest_ref[1].astype(F32) + a_ref[1].astype(F32)).astype(BF16)
    b_out[...] = (rest_ref[3].astype(F32) + b_ref[1].astype(F32)).astype(BF16)


def finish_kernel(*refs):
    ins, (out_ref, sample_ref, turned, sems) = refs[:-4], refs[-4:]
    copies = []
    for place, (start, rows) in enumerate(CHUNKS):
        ra, rb, rest, sa, sb = ins[5 * place : 5 * place + 5]
        for half, (own, near, far) in enumerate(((0, ra, sa), (2, rb, sb))):
            total = rest[own].astype(F32) + near[0].astype(F32) + far[...].astype(F32)
            columns = slice(half * PIECE, (half + 1) * PIECE)
            here = (columns, slice(start, start + rows))
            turned[here] = jnp.transpose(total[0:rows]).astype(BF16)
            if place == LEADING:
                sample_ref[:, columns] = total[rows : rows + 2].astype(BF16)
            copies.append(pltpu.make_async_copy(turned.at[here], out_ref.at[here], sems.at[len(copies)]))
            copies[-1].start()
    for copy in copies:
        copy.wait()


def in_hbm(*arrays):
    return tuple(pltpu.with_memory_space_constraint(x, pltpu.HBM) for x in arrays)


def call(kernel, name, out_shape, inputs, limit, scalars=0, **more):
    return pl.pallas_call(
        kernel,
        out_shape=out_shape,
        in_specs=[SMEM] * scalars + [VMEM] * (len(inputs) - scalars),
        out_specs=jax.tree.map(lambda _: VMEM, out_shape, is_leaf=lambda x: not isinstance(x, tuple)),
        compiler_params=pltpu.CompilerParams(vmem_limit_bytes=limit << 20),
        cost_estimate=pl.CostEstimate(flops=1, bytes_accessed=1, transcendentals=0),
        name=name,
        **more,
    )(*inputs)


SMEM = pl.BlockSpec(memory_space=pltpu.SMEM)
VMEM = pl.BlockSpec(memory_space=pltpu.VMEM)


def shape(dims, dtype=BF16):
    return jax.ShapeDtypeStruct(dims, dtype)


def swap(x, step):
    return lax.ppermute(x, "head", [(i, i ^ step) for i in range(4)])


def other_core(x):
    return lax.ppermute(x, "core", [(0, 1), (1, 0)])


def local_outputs(part, step, decay, skip, values, gate, inject, read, start=()):
    blocks = TOK // BLOCK // 2
    row = lambda width: pl.BlockSpec((1, width), lambda b: (0, 0))
    tokens = lambda width: pl.BlockSpec((BLOCK, width), lambda b: (b + part * blocks, 0))
    out = pl.BlockSpec((BLOCK, CH), lambda b: (b, 0))
    whole = lambda rows: pl.BlockSpec((rows, CH), lambda b: (0, 0))
    carry = (pltpu.HBM((STATE, CH), BF16), pltpu.HBM((8, CH), F32))
    results = (pltpu.HBM((TOK // 2, CH), BF16),) * 2
    scratch = [
        pltpu.VMEM((8, CH), F32), pltpu.VMEM((BLOCK, CH), BF16), pltpu.VMEM((BLOCK, CH), F32),
        pltpu.VMEM((STATE, CH), F32), pltpu.VMEM((8, CH), F32),
    ]
    if start:
        start_specs = [whole(STATE), whole(8)]
        out_specs = (out, out)
    else:
        start_specs = []
        results += carry
        out_specs = (out, out, whole(STATE), whole(8))
    step, values, gate, inject, read, *start = in_hbm(step, values, gate, inject, read, *start)
    return pl.pallas_call(
        functools.partial(local_kernel, part),
        grid=(blocks,),
        out_shape=results,
        in_specs=[
            pl.BlockSpec((HEADS, BLOCK), lambda b: (0, b + part * blocks)), row(HEADS), row(HEADS),
            tokens(CH), tokens(CH), tokens(STATE), tokens(STATE), *start_specs,
        ],
        out_specs=out_specs,
        scratch_shapes=scratch,
        compiler_params=pltpu.CompilerParams(vmem_limit_bytes=20 << 20),
        cost_estimate=pl.CostEstimate(flops=3 << 30, bytes_accessed=20 << 20, transcendentals=2 << 20),
        name="local_outputs",
    )(step, decay, skip, values, gate, inject, read, *start)


def per_device(
    prompt_values, prompt_gate, prompt_inject, prompt_read, prompt_step, decay_log, skip_gain, norm_weight, out_weight,
    sample_values, sample_gate, sample_inject, sample_read, sample_step, sample_length,
):
    inject = prompt_inject.reshape(TOK, STATE)
    read = prompt_read.reshape(TOK, STATE)
    decay = decay_log.reshape(1, HEADS)
    skip = skip_gain.reshape(1, HEADS)
    norm = norm_weight.reshape(1, CH)
    s_read = sample_read.reshape(2, SLEN, STATE)
    s_inject = sample_inject.reshape(2, SLEN, STATE)
    slices_shape = shape((16, ROWS, 128))

    anywhere = pl.BlockSpec(memory_space=pl.ANY)
    keep, send = pl.pallas_call(
        end_state_kernel,
        out_shape=(slices_shape,) * 2,
        in_specs=[SMEM, anywhere, VMEM, anywhere, anywhere, VMEM],
        out_specs=(VMEM, VMEM),
        scratch_shapes=[
            pltpu.VMEM((TOK, 1024), BF16), pltpu.VMEM((HEADS, TOK), F32), pltpu.VMEM((TOK, CH), BF16),
            pltpu.VMEM((TOK, STATE), BF16), pltpu.SemaphoreType.DMA((4,)),
        ],
        compiler_params=pltpu.CompilerParams(vmem_limit_bytes=24 << 20),
        name="end_state",
    )(*in_hbm(sample_length, prompt_step, decay, prompt_values, inject, s_read))
    sibling = other_core(send)
    joined = call(join_cores_kernel, "join_cores", slices_shape, (keep, sibling), 16)
    joined, step_1, s_step = lax.optimization_barrier((joined, prompt_step, sample_step.transpose(1, 0, 2)))
    slices = lax.all_to_all(joined, ("y", "x"), 0, 0, tiled=True)
    scaled_1, gain_1, *carry = local_outputs(
        0, step_1, decay, skip, prompt_values, prompt_gate, inject, read
    )
    sample = call(
        sample_kernel, "sample_outputs", (pltpu.HBM((16, CH), F32),) * 3,
        (sample_length, *in_hbm(s_step, decay, skip, sample_values, sample_gate, s_inject, s_read)), 16, 1,
    )
    slices, scaled_1, sample = lax.optimization_barrier((slices, scaled_1, sample))
    prefix = call(prefix_kernel, "prefix", slices_shape, (slices,), 16)
    prefix, step_2 = lax.optimization_barrier((prefix, prompt_step))
    back = lax.all_to_all(prefix, ("y", "x"), 0, 0, tiled=True)
    scaled_2, gain_2 = local_outputs(
        1, step_2, decay, skip, prompt_values, prompt_gate, inject, read, carry
    )
    back, scaled_2, weight = lax.optimization_barrier((back, scaled_2, out_weight))
    mine, send = call(
        split_cores_kernel, "split_cores", (shape((272, 1024)), slices_shape), (back, keep, sibling), 16
    )
    theirs = other_core(send)

    near_columns = fetch(FIRST[:2], weight)
    scaled = (scaled_1, scaled_2)
    gain = (gain_1, gain_2)
    state = call(join_halves_kernel, "join_halves", shape((272, CH)), (mine, theirs), 8)

    def chunk(place, far_columns, *sample):
        start, rows = CHUNKS[place]
        size = rows + (16 if sample else 0)
        leading = place == LEADING
        piece = shape((2, size, PIECE))
        held = pltpu.VMEM((2, CH, PIECE), BF16)
        first, second, normed, *held = pl.pallas_call(
            functools.partial(chunk_kernel, place, bool(sample)),
            out_shape=(piece, piece, shape((size, CH)), *([held] if leading else [])),
            in_specs=[VMEM] * 6 + [anywhere if leading else VMEM] + [VMEM] * len(sample),
            out_specs=(VMEM,) * (4 if leading else 3),
            scratch_shapes=[pltpu.SemaphoreType.DMA((2,))] if leading else [],
            compiler_params=pltpu.CompilerParams(vmem_limit_bytes=24 << 20),
            name="chunk",
        )(state, read, scaled[start // HALF], gain[start // HALF], norm, near_columns, far_columns, *sample)
        near = lax.optimization_barrier((swap(first, 1), swap(second, 3)))
        return normed, near, *held

    def exchange(normed, near, rest_columns):
        rest = call(rest_kernel, "rest", shape((4, normed.shape[0], PIECE)), (normed, rest_columns), 24)
        a, b = near
        a_on, b_on = call(onward_kernel, "onward", (shape(a.shape[1:]),) * 2, (a, b, rest), 8)
        return (a, b, rest, *lax.optimization_barrier((swap(a_on, 3), swap(b_on, 1))))

    normed_0, near_0, far_columns = chunk(0, *in_hbm(weight), *sample)
    rest_columns = fetch(REST, weight)
    normed_1, near_1 = chunk(1, resident(far_columns))
    parts = exchange(normed_0, near_0, rest_columns) + exchange(normed_1, near_1, rest_columns)
    prompt_mixed, sample_mixed = pl.pallas_call(
        finish_kernel,
        out_shape=(shape((1024, TOK)), shape((2, 1024))),
        in_specs=[VMEM] * 10,
        out_specs=(anywhere, VMEM),
        scratch_shapes=[pltpu.VMEM((1024, TOK), BF16), pltpu.SemaphoreType.DMA((4,))],
        compiler_params=pltpu.CompilerParams(vmem_limit_bytes=16 << 20),
        name="finish",
    )(*parts)
    return prompt_mixed, sample_mixed.T


def solution(mesh):
    split = Mesh(mesh.devices.reshape(4, 4, 2, mesh.shape["head"]), ("y", "x", "core", "head"))
    return jax.shard_map(
        per_device,
        mesh=split,
        in_specs=(
            P(CTX, "head"), P(CTX, "head"), P(CTX, "head", None), P(CTX, "head", None), P("head", CTX),
            P("head"), P("head"), P("head"), P("head", None),
            P(CTX, None, "head"), P(CTX, None, "head"), P(CTX, None, "head", None), P(CTX, None, "head", None),
            P("head", CTX, None), P(CTX),
        ),
        out_specs=(P("head", CTX), P("head", CTX)),
        check_vma=False,
    )
```

```python
import functools

import jax
import jax.numpy as jnp
from jax import lax
from jax.experimental import pallas as pl
from jax.experimental.pallas import tpu as pltpu
from jax.sharding import Mesh
from jax.sharding import PartitionSpec as P

HEADS = 32
HEAD_DIM = 64
STATE = 256
BLOCK = 128
SLEN = 16
TOK = 512
CH = HEADS * HEAD_DIM
PIECE = 512
HALF = TOK // 2
ROWS = 144
CTX = ("y", "x", "core")
F32 = jnp.float32
BF16 = jnp.bfloat16
EXACT = lax.Precision.HIGHEST
LOG2E = 1.4426950408889634
CHUNKS = ((256, 256), (0, 128), (128, 128))
LEADING = 0


def softplus(v):
    return jnp.maximum(v, 0.0) + jnp.log1p(jnp.exp(-jnp.abs(v)))


def iota(shape, dim):
    return lax.broadcasted_iota(jnp.int32, shape, dim)


def column(row):
    n = row.shape[1]
    square = jnp.broadcast_to(row, (n, n))
    return jnp.sum(jnp.where(iota((n, n), 0) == iota((n, n), 1), square, 0.0), axis=1, keepdims=True)


def tokens_first(x):
    pad = jnp.zeros((128 - x.shape[0], x.shape[1]), F32)
    return jnp.transpose(jnp.concatenate([x, pad], axis=0))


def per_pair(columns, pair, shape, low):
    first = jnp.broadcast_to(columns[:, 2 * pair : 2 * pair + 1], shape)
    second = jnp.broadcast_to(columns[:, 2 * pair + 1 : 2 * pair + 2], shape)
    return jnp.where(low, first, second)


def three_parts(x):
    hi = x.astype(BF16).astype(F32)
    mid = (x - hi).astype(BF16).astype(F32)
    lo = (x - hi - mid).astype(BF16).astype(F32)
    return hi, mid, lo


def decay_of(tail):
    return tail[8:9] + tail[9:10] + tail[10:11]


def with_decay(tail, decay):
    row = iota((16, 128), 0)
    hi, mid, lo = three_parts(decay)
    tail = jnp.where(row == 8, hi, tail)
    tail = jnp.where(row == 9, mid, tail)
    return jnp.where(row == 10, lo, tail)


def end_state_kernel(
    length, step_any, decay_ref, values_any, inject_any, read_ref, keep_ref, send_ref,
    scaled, step_ref, values_ref, inject_ref, sems,
):
    copies = [
        pltpu.make_async_copy(step_any, step_ref, sems.at[0]),
        pltpu.make_async_copy(inject_any, inject_ref, sems.at[1]),
    ]
    for half in range(2):
        lanes = slice(half * 1024, (half + 1) * 1024)
        copies.append(pltpu.make_async_copy(values_any.at[:, lanes], values_ref.at[:, lanes], sems.at[2 + half]))
    for copy in copies:
        copy.start()
    copies[0].wait()
    core = lax.axis_index("core")
    step = softplus(step_ref[...])
    logs = step * -jnp.exp(column(decay_ref[...]))
    later = (iota((BLOCK, BLOCK), 0) > iota((BLOCK, BLOCK), 1)).astype(F32)
    after = jnp.zeros((HEADS, 1), F32)
    parts = []
    for b in reversed(range(TOK // BLOCK)):
        here = logs[:, b * BLOCK : (b + 1) * BLOCK]
        parts.append(jnp.dot(here, later, precision=EXACT, preferred_element_type=F32) + after)
        after = after + jnp.sum(here, axis=1, keepdims=True)
    weight = tokens_first(jnp.exp(jnp.concatenate(parts[::-1], axis=1)) * step)
    total = tokens_first(jnp.broadcast_to(jnp.exp(after), (HEADS, 128)))[0:8]
    copies[1].wait()
    inject_t = jnp.transpose(inject_ref[...].astype(F32)).astype(BF16)
    low = iota((TOK, 128), 1) < HEAD_DIM
    low_row = iota((8, 128), 1) < HEAD_DIM
    row = iota((16, 128), 0)
    tails = []
    for half in range(2):
        lanes = slice(half * 128, (half + 1) * 128)
        tail = jnp.zeros((16, 128), F32)
        for s in range(2):
            last = iota((SLEN, 128), 0) == length[s] - 1
            picked = jnp.sum(jnp.where(last, read_ref[s, :, lanes].astype(F32), 0.0), axis=0, keepdims=True)
            tail = jnp.where(row == 2 * core + s, picked, tail)
        tails.append(tail)
    for half in range(2):
        copies[2 + half].wait()
        for q in range(8):
            pair = half * 8 + q
            lanes = slice(pair * 128, (pair + 1) * 128)
            w = per_pair(weight, pair, (TOK, 128), low)
            scaled[:, q * 128 : (q + 1) * 128] = (values_ref[:, lanes].astype(F32) * w).astype(BF16)
        state = jnp.dot(inject_t, scaled[...], preferred_element_type=F32).astype(BF16)

        def put(out_ref, half=half, state=state):
            for q in range(8):
                decay = per_pair(total, half * 8 + q, (8, 128), low_row)[0:1]
                for n in range(2):
                    out_ref[2 * q + n, 0:128, :] = state[n * 128 : (n + 1) * 128, q * 128 : (q + 1) * 128]
                    out_ref[2 * q + n, 128:ROWS, :] = with_decay(tails[n], decay).astype(BF16)

        @pl.when(core == half)
        def _(put=put):
            put(keep_ref)

        @pl.when(core != half)
        def _(put=put):
            put(send_ref)


def join_cores_kernel(own_ref, sib_ref, out_ref):
    first = lax.axis_index("core") == 0
    row = iota((16, 128), 0)
    for k in range(16):
        own_tail = own_ref[k, 128:ROWS, :].astype(F32)
        sib_tail = sib_ref[k, 128:ROWS, :].astype(F32)
        own_decay, sib_decay = decay_of(own_tail), decay_of(sib_tail)
        own_weight = jnp.where(first, sib_decay, 1.0)
        sib_weight = jnp.where(first, 1.0, own_decay)
        out_ref[k, 0:128, :] = (
            own_ref[k, 0:128, :].astype(F32) * own_weight + sib_ref[k, 0:128, :].astype(F32) * sib_weight
        ).astype(BF16)
        tail = jnp.where(row < 8, own_tail + sib_tail, 0.0)
        out_ref[k, 128:ROWS, :] = with_decay(tail, own_decay * sib_decay).astype(BF16)


def prefix_kernel(in_ref, out_ref):
    state = jnp.zeros((128, 128), F32)
    for i in range(16):
        out_ref[i, 0:128, :] = state.astype(BF16)
        decay = decay_of(in_ref[i, 128:ROWS, :].astype(F32))
        state = state * decay + in_ref[i, 0:128, :].astype(F32)
    final = state.astype(BF16)
    for i in range(16):
        out_ref[i, 128:ROWS, :] = jnp.dot(
            in_ref[i, 128:ROWS, :], final, preferred_element_type=F32
        ).astype(BF16)


def split_cores_kernel(back_ref, own_ref, sib_ref, mine_ref, send_ref):
    first = lax.axis_index("core") == 0
    for k in range(16):
        q, n = k // 2, k % 2
        arrived = back_ref[k, 0:128, :].astype(F32)
        own_decay = decay_of(own_ref[k, 128:ROWS, :].astype(F32))
        sib_decay = decay_of(sib_ref[k, 128:ROWS, :].astype(F32))
        decay = jnp.where(first, own_decay, sib_decay)
        state = jnp.where(first, own_ref[k, 0:128, :].astype(F32), sib_ref[k, 0:128, :].astype(F32))
        second = arrived * decay + state
        mine_ref[n * 128 : (n + 1) * 128, q * 128 : (q + 1) * 128] = jnp.where(first, arrived, second).astype(BF16)
        send_ref[k, 0:128, :] = jnp.where(first, second, arrived).astype(BF16)
        send_ref[k, 128:ROWS, :] = back_ref[k, 128:ROWS, :]
    for q in range(8):
        mine_ref[256:272, q * 128 : (q + 1) * 128] = (
            back_ref[2 * q, 128:ROWS, :].astype(F32) + back_ref[2 * q + 1, 128:ROWS, :].astype(F32)
        ).astype(BF16)


def local_kernel(
    part, step_ref, decay_ref, skip_ref, values_ref, gate_ref, inject_ref, read_ref, *refs
):
    if part == 0:
        scaled_ref, gain_ref, carry, carry_before, ends, weighted, carried, state, before = refs
    else:
        start, start_before, scaled_ref, gain_ref, ends, weighted, carried, state, before = refs

    @pl.when(pl.program_id(0) == 0)
    def _():
        if part == 0:
            state[...] = jnp.zeros_like(state)
            before[...] = jnp.ones_like(before)
        else:
            state[...] = start[...].astype(F32)
            before[...] = start_before[...]

    step = softplus(step_ref[...])
    logs = step * -jnp.exp(column(decay_ref[...]))
    upto = (iota((BLOCK, BLOCK), 0) <= iota((BLOCK, BLOCK), 1)).astype(F32)
    running = jnp.dot(logs, upto, precision=EXACT, preferred_element_type=F32) * LOG2E
    running_t = tokens_first(running)
    step_t = tokens_first(step)
    read = read_ref[...]
    inject = inject_ref[...]
    inject_t = jnp.transpose(inject.astype(F32)).astype(BF16)
    scores = jnp.dot(read, inject_t, preferred_element_type=F32)
    carried[...] = jnp.dot(read, state[...].astype(BF16), preferred_element_type=F32)
    causal = iota((BLOCK, BLOCK), 0) >= iota((BLOCK, BLOCK), 1)
    low = iota((BLOCK, 128), 1) < HEAD_DIM
    for pair in range(16):
        lanes = slice(pair * 128, (pair + 1) * 128)
        mixing = []
        spread = []
        for h in (2 * pair, 2 * pair + 1):
            mine = jnp.broadcast_to(running_t[:, h : h + 1], (BLOCK, BLOCK))
            gap = jnp.where(causal, mine - running[h : h + 1, :], -1e30)
            mixing.append((scores * jnp.exp2(gap)).astype(BF16))
            spread.append(mine)
        now = jnp.where(low, spread[0], spread[1])
        grown = jnp.exp2(now)
        values = values_ref[:, lanes].astype(F32)
        stepped = values * per_pair(step_t, pair, (BLOCK, 128), low)
        diagonal = jnp.concatenate([jnp.where(low, stepped, 0.0), jnp.where(low, 0.0, stepped)], axis=0)
        local = jnp.dot(
            jnp.concatenate(mixing, axis=1), diagonal.astype(BF16), preferred_element_type=F32
        )
        skip = per_pair(skip_ref[...], pair, (1, 128), low[0:1])
        out = local + carried[:, lanes] * grown + skip * values
        gate = gate_ref[:, lanes].astype(F32)
        gate = gate / (1.0 + jnp.exp(-gate))
        scaled_ref[:, lanes] = (out * gate).astype(BF16)
        gain_ref[:, lanes] = (gate * grown * before[0:1, lanes]).astype(BF16)
        end = now[BLOCK - 1 : BLOCK, :]
        weighted[:, lanes] = (stepped * jnp.exp2(end - now)).astype(BF16)
        ends[0:1, lanes] = jnp.exp2(end)
    state[...] = state[...] * ends[0:1, :] + jnp.dot(inject_t, weighted[...], preferred_element_type=F32)
    before[0:1, :] = before[0:1, :] * ends[0:1, :]
    if part == 0:

        @pl.when(pl.program_id(0) == pl.num_programs(0) - 1)
        def _():
            carry[...] = state[...].astype(BF16)
            carry_before[...] = before[...]


def sample_kernel(
    length, step_ref, decay_ref, skip_ref, values_ref, gate_ref, inject_ref, read_ref, local_ref, grown_ref, gate_out_ref
):
    rate = -jnp.exp(column(decay_ref[...]))
    row = iota((16, CH), 0)
    place = iota((SLEN, 128), 0)
    place_wide = iota((SLEN, STATE), 0)
    narrow = []
    for s in range(2):
        last = length[s] - 1
        step = softplus(step_ref[s])
        logs = step * rate
        pad = jnp.zeros((HEADS, 128 - SLEN), F32)
        step_t = tokens_first(jnp.concatenate([step, pad], axis=1))[0:SLEN]
        logs_t = tokens_first(jnp.concatenate([logs, pad], axis=1))[0:SLEN]
        logs_t = jnp.where(place <= last, logs_t, 0.0)
        gap = jnp.zeros((SLEN, 128), F32)
        for k in range(SLEN):
            gap = gap + jnp.where(place < k, logs_t[k : k + 1], 0.0)
        whole = jnp.sum(logs_t, axis=0, keepdims=True)
        read = jnp.sum(jnp.where(place_wide == last, read_ref[s].astype(F32), 0.0), axis=0, keepdims=True)
        scores = jnp.sum(inject_ref[s].astype(F32) * read, axis=1, keepdims=True)
        narrow.append(jnp.where(place <= last, scores * jnp.exp(gap) * step_t, 0.0))
        narrow.append(jnp.broadcast_to(jnp.exp(whole), (SLEN, 128)))
    skip = jnp.concatenate([skip_ref[...], jnp.zeros((1, 128 - HEADS), F32)], axis=1)
    narrow.append(jnp.broadcast_to(skip, (SLEN, 128)))
    spread = (iota((128, CH), 1) // HEAD_DIM == iota((128, CH), 0)).astype(BF16)
    parts = jnp.concatenate(three_parts(jnp.concatenate(narrow, axis=0)), axis=0).astype(BF16)
    wide = jnp.dot(parts, spread, preferred_element_type=F32)
    wide = wide[0:80] + wide[80:160] + wide[160:240]
    local_all = jnp.zeros((16, CH), F32)
    grown_all = jnp.zeros((16, CH), F32)
    gate_all = jnp.zeros((16, CH), F32)
    for s in range(2):
        values = values_ref[s].astype(F32)
        at_last = iota((SLEN, CH), 0) == length[s] - 1
        picked = jnp.sum(jnp.where(at_last, values, 0.0), axis=0, keepdims=True)
        gate = jnp.sum(jnp.where(at_last, gate_ref[s].astype(F32), 0.0), axis=0, keepdims=True)
        local = jnp.sum(wide[32 * s : 32 * s + SLEN] * values, axis=0, keepdims=True) + wide[64:65] * picked
        local_all = jnp.where(row == s, local, local_all)
        grown_all = jnp.where(row == s, wide[32 * s + SLEN : 32 * s + SLEN + 1], grown_all)
        gate_all = jnp.where(row == s, gate / (1.0 + jnp.exp(-gate)), gate_all)
    local_ref[...] = local_all
    grown_ref[...] = grown_all
    gate_out_ref[...] = gate_all


def normalize(gated, weight):
    mean = jnp.sum(gated * gated, axis=1, keepdims=True) * (1.0 / CH)
    return (gated * lax.rsqrt(mean + 1e-05) * weight).astype(BF16)


FIRST = ((1, 0), (2, 0), (3, 1), (2, 1))
REST = ((3, 0), (1, 1), (0, 0), (0, 1))


def column_copies(pieces, weight_ref, held, sems):
    z = lax.axis_index("head")
    copies = []
    for i, (flip, half) in enumerate(pieces):
        at = pl.multiple_of(((z ^ flip) * 2 + half) * PIECE, PIECE)
        copies.append(pltpu.make_async_copy(weight_ref.at[:, pl.ds(at, PIECE)], held.at[i], sems.at[i]))
    for copy in copies:
        copy.start()
    return copies


def fetch_kernel(pieces, weight_ref, out_ref, sems):
    for copy in column_copies(pieces, weight_ref, out_ref, sems):
        copy.wait()


def resident(x):
    return pltpu.with_memory_space_constraint(x, pltpu.VMEM)


def fetch(pieces, weight):
    out = pl.pallas_call(
        functools.partial(fetch_kernel, pieces),
        out_shape=pltpu.VMEM((len(pieces), CH, PIECE), BF16),
        in_specs=[pl.BlockSpec(memory_space=pl.ANY)],
        out_specs=VMEM,
        scratch_shapes=[pltpu.SemaphoreType.DMA((len(pieces),))],
        compiler_params=pltpu.CompilerParams(vmem_limit_bytes=12 << 20),
        name="fetch_weight",
    )(*in_hbm(weight))
    return resident(out)


def project(normed, columns, outs):
    for column, (ref, k) in zip(columns, outs):
        ref[k] = jnp.dot(normed[...], column[...], preferred_element_type=F32).astype(BF16)


def gate_and_normalize(place, state_ref, read_ref, scaled_ref, gain_ref, norm_ref, normed):
    start, rows = CHUNKS[place]
    arrived = jnp.dot(read_ref[start : start + rows, :], state_ref[0:STATE, :], preferred_element_type=F32)
    here = slice(start % HALF, start % HALF + rows)
    gated = scaled_ref[here, :].astype(F32) + arrived * gain_ref[here, :].astype(F32)
    normed[0:rows, :] = normalize(gated, norm_ref[...])


def join_halves_kernel(mine_ref, theirs_ref, state_ref):
    core = lax.axis_index("core")
    state_ref[:, pl.ds(pl.multiple_of(core * 1024, 1024), 1024)] = mine_ref[...]
    for q in range(8):
        lanes = pl.ds(pl.multiple_of((1 - core) * 1024 + q * 128, 128), 128)
        for n in range(2):
            state_ref[n * 128 : (n + 1) * 128, lanes] = theirs_ref[2 * q + n, 0:128, :]
        state_ref[256:272, lanes] = (
            theirs_ref[2 * q, 128:ROWS, :].astype(F32) + theirs_ref[2 * q + 1, 128:ROWS, :].astype(F32)
        ).astype(BF16)


def chunk_kernel(place, sampled, state_ref, read_ref, scaled_ref, gain_ref, norm_ref, near_ref, far_ref, *refs):
    if place == LEADING:
        *sample, first_ref, second_ref, normed_ref, held, sems = refs
        copies = column_copies(FIRST[2:], far_ref, held, sems)
    else:
        *sample, first_ref, second_ref, normed_ref = refs
        held = far_ref
    gate_and_normalize(place, state_ref, read_ref, scaled_ref, gain_ref, norm_ref, normed_ref)
    if sampled:
        local_ref, grown_ref, gate_ref = sample
        readings = state_ref[256:272, :].astype(F32)
        moved = jnp.concatenate([readings[2:16], readings[0:2]], axis=0)
        readings = jnp.where(lax.axis_index("core") == 0, readings, moved)
        sampled = (local_ref[...] + readings * grown_ref[...]) * gate_ref[...]
        rows = CHUNKS[place][1]
        normed_ref[rows : rows + 16, :] = normalize(sampled, norm_ref[...])
    project(normed_ref, (near_ref.at[0], near_ref.at[1]), ((first_ref, 0), (first_ref, 1)))
    for i in range(2):
        if place == LEADING:
            copies[i].wait()
        project(normed_ref, (held.at[i],), ((second_ref, i),))


def rest_kernel(normed_ref, weight_ref, rest_ref):
    project(normed_ref, [weight_ref.at[i] for i in range(4)], ((rest_ref, 1), (rest_ref, 3), (rest_ref, 0), (rest_ref, 2)))


def onward_kernel(*refs):
    ins, (a_out, b_out) = refs[:-2], refs[-2:]
    start = 0
    for a_ref, b_ref, rest_ref in (ins[i : i + 3] for i in range(0, len(ins), 3)):
        rows = slice(start, start + a_ref.shape[1])
        a_out[rows, :] = (rest_ref[1].astype(F32) + a_ref[1].astype(F32)).astype(BF16)
        b_out[rows, :] = (rest_ref[3].astype(F32) + b_ref[1].astype(F32)).astype(BF16)
        start = rows.stop


def finish_kernel(*refs):
    ins, (out_ref, sample_ref, turned, sems) = refs[:-4], refs[-4:]
    copies = []
    skipped = 0
    for place, (start, rows) in enumerate(CHUNKS):
        ra, rb, rest = ins[3 * place : 3 * place + 3]
        sa, sb = ins[9:11] if place == 0 else ins[11:13]
        size = ra.shape[1]
        skipped = skipped if place > 1 else 0
        for half, (own, near, far) in enumerate(((0, ra, sa), (2, rb, sb))):
            total = rest[own].astype(F32) + near[0].astype(F32) + far[skipped : skipped + size, :].astype(F32)
            columns = slice(half * PIECE, (half + 1) * PIECE)
            here = (columns, slice(start, start + rows))
            turned[here] = jnp.transpose(total[0:rows]).astype(BF16)
            if place == LEADING:
                sample_ref[:, columns] = total[rows : rows + 2].astype(BF16)
            copies.append(pltpu.make_async_copy(turned.at[here], out_ref.at[here], sems.at[len(copies)]))
            copies[-1].start()
        skipped += size
    for copy in copies:
        copy.wait()


def in_hbm(*arrays):
    return tuple(pltpu.with_memory_space_constraint(x, pltpu.HBM) for x in arrays)


def call(kernel, name, out_shape, inputs, limit, scalars=0, **more):
    return pl.pallas_call(
        kernel,
        out_shape=out_shape,
        in_specs=[SMEM] * scalars + [VMEM] * (len(inputs) - scalars),
        out_specs=jax.tree.map(lambda _: VMEM, out_shape, is_leaf=lambda x: not isinstance(x, tuple)),
        compiler_params=pltpu.CompilerParams(vmem_limit_bytes=limit << 20),
        cost_estimate=pl.CostEstimate(flops=1, bytes_accessed=1, transcendentals=0),
        name=name,
        **more,
    )(*inputs)


SMEM = pl.BlockSpec(memory_space=pltpu.SMEM)
VMEM = pl.BlockSpec(memory_space=pltpu.VMEM)


def shape(dims, dtype=BF16):
    return jax.ShapeDtypeStruct(dims, dtype)


def swap(x, step):
    return lax.ppermute(x, "head", [(i, i ^ step) for i in range(4)])


def other_core(x):
    return lax.ppermute(x, "core", [(0, 1), (1, 0)])


def local_outputs(part, step, decay, skip, values, gate, inject, read, start=()):
    blocks = TOK // BLOCK // 2
    row = lambda width: pl.BlockSpec((1, width), lambda b: (0, 0))
    tokens = lambda width: pl.BlockSpec((BLOCK, width), lambda b: (b + part * blocks, 0))
    out = pl.BlockSpec((BLOCK, CH), lambda b: (b, 0))
    whole = lambda rows: pl.BlockSpec((rows, CH), lambda b: (0, 0))
    carry = (pltpu.HBM((STATE, CH), BF16), pltpu.HBM((8, CH), F32))
    results = (pltpu.HBM((TOK // 2, CH), BF16),) * 2
    scratch = [
        pltpu.VMEM((8, CH), F32), pltpu.VMEM((BLOCK, CH), BF16), pltpu.VMEM((BLOCK, CH), F32),
        pltpu.VMEM((STATE, CH), F32), pltpu.VMEM((8, CH), F32),
    ]
    if start:
        start_specs = [whole(STATE), whole(8)]
        out_specs = (out, out)
    else:
        start_specs = []
        results += carry
        out_specs = (out, out, whole(STATE), whole(8))
    step, values, gate, inject, read, *start = in_hbm(step, values, gate, inject, read, *start)
    return pl.pallas_call(
        functools.partial(local_kernel, part),
        grid=(blocks,),
        out_shape=results,
        in_specs=[
            pl.BlockSpec((HEADS, BLOCK), lambda b: (0, b + part * blocks)), row(HEADS), row(HEADS),
            tokens(CH), tokens(CH), tokens(STATE), tokens(STATE), *start_specs,
        ],
        out_specs=out_specs,
        scratch_shapes=scratch,
        compiler_params=pltpu.CompilerParams(vmem_limit_bytes=20 << 20),
        cost_estimate=pl.CostEstimate(flops=3 << 30, bytes_accessed=20 << 20, transcendentals=2 << 20),
        name="local_outputs",
    )(step, decay, skip, values, gate, inject, read, *start)


def per_device(
    prompt_values, prompt_gate, prompt_inject, prompt_read, prompt_step, decay_log, skip_gain, norm_weight, out_weight,
    sample_values, sample_gate, sample_inject, sample_read, sample_step, sample_length,
):
    inject = prompt_inject.reshape(TOK, STATE)
    read = prompt_read.reshape(TOK, STATE)
    decay = decay_log.reshape(1, HEADS)
    skip = skip_gain.reshape(1, HEADS)
    norm = norm_weight.reshape(1, CH)
    s_read = sample_read.reshape(2, SLEN, STATE)
    s_inject = sample_inject.reshape(2, SLEN, STATE)
    slices_shape = shape((16, ROWS, 128))

    anywhere = pl.BlockSpec(memory_space=pl.ANY)
    keep, send = pl.pallas_call(
        end_state_kernel,
        out_shape=(slices_shape,) * 2,
        in_specs=[SMEM, anywhere, VMEM, anywhere, anywhere, VMEM],
        out_specs=(VMEM, VMEM),
        scratch_shapes=[
            pltpu.VMEM((TOK, 1024), BF16), pltpu.VMEM((HEADS, TOK), F32), pltpu.VMEM((TOK, CH), BF16),
            pltpu.VMEM((TOK, STATE), BF16), pltpu.SemaphoreType.DMA((4,)),
        ],
        compiler_params=pltpu.CompilerParams(vmem_limit_bytes=24 << 20),
        name="end_state",
    )(*in_hbm(sample_length, prompt_step, decay, prompt_values, inject, s_read))
    sibling = other_core(send)
    joined = call(join_cores_kernel, "join_cores", slices_shape, (keep, sibling), 16)
    joined, step_1, s_step = lax.optimization_barrier((joined, prompt_step, sample_step.transpose(1, 0, 2)))
    slices = lax.all_to_all(joined, ("y", "x"), 0, 0, tiled=True)
    scaled_1, gain_1, *carry = local_outputs(
        0, step_1, decay, skip, prompt_values, prompt_gate, inject, read
    )
    sample = call(
        sample_kernel, "sample_outputs", (pltpu.HBM((16, CH), F32),) * 3,
        (sample_length, *in_hbm(s_step, decay, skip, sample_values, sample_gate, s_inject, s_read)), 16, 1,
    )
    slices, scaled_1, sample = lax.optimization_barrier((slices, scaled_1, sample))
    prefix = call(prefix_kernel, "prefix", slices_shape, (slices,), 16)
    prefix, step_2 = lax.optimization_barrier((prefix, prompt_step))
    back = lax.all_to_all(prefix, ("y", "x"), 0, 0, tiled=True)
    scaled_2, gain_2 = local_outputs(
        1, step_2, decay, skip, prompt_values, prompt_gate, inject, read, carry
    )
    back, scaled_2, weight = lax.optimization_barrier((back, scaled_2, out_weight))
    mine, send = call(
        split_cores_kernel, "split_cores", (shape((272, 1024)), slices_shape), (back, keep, sibling), 16
    )
    theirs = other_core(send)

    near_columns = fetch(FIRST[:2], weight)
    scaled = (scaled_1, scaled_2)
    gain = (gain_1, gain_2)
    state = call(join_halves_kernel, "join_halves", shape((272, CH)), (mine, theirs), 8)

    def chunk(place, norm, far_columns, *sample):
        start, rows = CHUNKS[place]
        size = rows + (16 if sample else 0)
        leading = place == LEADING
        piece = shape((2, size, PIECE))
        held = pltpu.VMEM((2, CH, PIECE), BF16)
        first, second, normed, *held = pl.pallas_call(
            functools.partial(chunk_kernel, place, bool(sample)),
            out_shape=(piece, piece, shape((size, CH)), *([held] if leading else [])),
            in_specs=[VMEM] * 6 + [anywhere if leading else VMEM] + [VMEM] * len(sample),
            out_specs=(VMEM,) * (4 if leading else 3),
            scratch_shapes=[pltpu.SemaphoreType.DMA((2,))] if leading else [],
            compiler_params=pltpu.CompilerParams(vmem_limit_bytes=24 << 20),
            name="chunk",
        )(state, read, scaled[start // HALF], gain[start // HALF], norm, near_columns, far_columns, *sample)
        near = lax.optimization_barrier((swap(first, 1), swap(second, 3)))
        return normed, near, *held

    normed_0, near_0, far_columns = chunk(0, norm, *in_hbm(weight), *sample)
    rest_columns = fetch(REST, weight)
    far_columns = resident(far_columns)

    def rest_of(normed):
        return call(rest_kernel, "rest", shape((4, normed.shape[0], PIECE)), (normed, rest_columns), 24)

    normed_1, near_1 = chunk(1, norm, far_columns)
    rest_0 = rest_of(normed_0)
    rest_0, norm = lax.optimization_barrier((rest_0, norm))
    normed_2, near_2 = chunk(2, norm, far_columns)
    near = [near_0, near_1, near_2]
    rests = [rest_0, rest_of(normed_1), rest_of(normed_2)]
    parts = [(*near[c], rests[c]) for c in range(3)]

    def onward(*parts):
        rows = sum(part[0].shape[1] for part in parts)
        return call(onward_kernel, "onward", (shape((rows, PIECE)),) * 2, sum(parts, ()), 8)

    def send_on(ons):
        return lax.optimization_barrier((swap(ons[0], 3), swap(ons[1], 1)))

    ons, parts[1] = lax.optimization_barrier((onward(parts[0]), parts[1]))
    far = (*send_on(ons), *send_on(onward(*parts[1:])))
    prompt_mixed, sample_mixed = pl.pallas_call(
        finish_kernel,
        out_shape=(shape((1024, TOK)), shape((2, 1024))),
        in_specs=[VMEM] * 13,
        out_specs=(anywhere, VMEM),
        scratch_shapes=[pltpu.VMEM((1024, TOK), BF16), pltpu.SemaphoreType.DMA((6,))],
        compiler_params=pltpu.CompilerParams(vmem_limit_bytes=16 << 20),
        name="finish",
    )(*sum(parts, ()), *far)
    return prompt_mixed, sample_mixed.T


def solution(mesh):
    split = Mesh(mesh.devices.reshape(4, 4, 2, mesh.shape["head"]), ("y", "x", "core", "head"))
    return jax.shard_map(
        per_device,
        mesh=split,
        in_specs=(
            P(CTX, "head"), P(CTX, "head"), P(CTX, "head", None), P(CTX, "head", None), P("head", CTX),
            P("head"), P("head"), P("head"), P("head", None),
            P(CTX, None, "head"), P(CTX, None, "head"), P(CTX, None, "head", None), P(CTX, None, "head", None),
            P("head", CTX, None), P(CTX),
        ),
        out_specs=(P("head", CTX), P("head", CTX)),
        check_vma=False,
    )
```

```python
import functools

import jax
import jax.numpy as jnp
from jax import lax
from jax.experimental import pallas as pl
from jax.experimental.pallas import tpu as pltpu
from jax.sharding import Mesh
from jax.sharding import PartitionSpec as P

HEADS = 32
HEAD_DIM = 64
STATE = 256
BLOCK = 128
SLEN = 16
TOK = 512
CH = HEADS * HEAD_DIM
PIECE = 512
HALF = TOK // 2
ROWS = 144
CTX = ("y", "x", "core")
F32 = jnp.float32
BF16 = jnp.bfloat16
EXACT = lax.Precision.HIGHEST
LOG2E = 1.4426950408889634
CHUNKS = ((256, 256), (0, 256))
LEADING = 0


def softplus(v):
    return jnp.maximum(v, 0.0) + jnp.log1p(jnp.exp(-jnp.abs(v)))


def iota(shape, dim):
    return lax.broadcasted_iota(jnp.int32, shape, dim)


def column(row):
    n = row.shape[1]
    square = jnp.broadcast_to(row, (n, n))
    return jnp.sum(jnp.where(iota((n, n), 0) == iota((n, n), 1), square, 0.0), axis=1, keepdims=True)


def tokens_first(x):
    pad = jnp.zeros((128 - x.shape[0], x.shape[1]), F32)
    return jnp.transpose(jnp.concatenate([x, pad], axis=0))


def per_pair(columns, pair, shape, low):
    first = jnp.broadcast_to(columns[:, 2 * pair : 2 * pair + 1], shape)
    second = jnp.broadcast_to(columns[:, 2 * pair + 1 : 2 * pair + 2], shape)
    return jnp.where(low, first, second)


def head_lanes(start, width):
    row, lane = iota((128, width), 0), iota((128, width), 1) + start
    return (((row & (HEADS - 1)) == (lane >> 6)) & (row < 3 * HEADS)).astype(BF16)


def three_parts(x):
    hi = x.astype(BF16).astype(F32)
    mid = (x - hi).astype(BF16).astype(F32)
    lo = (x - hi - mid).astype(BF16).astype(F32)
    return hi, mid, lo


def decay_of(tail):
    return tail[8:9] + tail[9:10] + tail[10:11]


def with_decay(tail, decay):
    row = iota((16, 128), 0)
    hi, mid, lo = three_parts(decay)
    tail = jnp.where(row == 8, hi, tail)
    tail = jnp.where(row == 9, mid, tail)
    return jnp.where(row == 10, lo, tail)


def end_state_kernel(
    length, step_any, decay_ref, values_any, inject_any, read_ref, keep_ref, send_ref,
    scaled, step_ref, values_ref, inject_ref, sems,
):
    copies = [
        pltpu.make_async_copy(step_any, step_ref, sems.at[0]),
        pltpu.make_async_copy(inject_any, inject_ref, sems.at[1]),
    ]
    for half in range(2):
        lanes = slice(half * 1024, (half + 1) * 1024)
        copies.append(pltpu.make_async_copy(values_any.at[:, lanes], values_ref.at[:, lanes], sems.at[2 + half]))
    for copy in copies:
        copy.start()
    copies[0].wait()
    core = lax.axis_index("core")
    step = softplus(step_ref[...])
    logs = step * -jnp.exp(column(decay_ref[...]))
    later = (iota((BLOCK, BLOCK), 0) > iota((BLOCK, BLOCK), 1)).astype(F32)
    after = jnp.zeros((HEADS, 1), F32)
    parts = []
    for b in reversed(range(TOK // BLOCK)):
        here = logs[:, b * BLOCK : (b + 1) * BLOCK]
        parts.append(jnp.dot(here, later, precision=EXACT, preferred_element_type=F32) + after)
        after = after + jnp.sum(here, axis=1, keepdims=True)
    weight = jnp.exp(jnp.concatenate(parts[::-1], axis=1)) * step
    weight = jnp.transpose(jnp.concatenate([*three_parts(weight), jnp.zeros((128 - 3 * HEADS, TOK), F32)], axis=0))
    weight = weight.astype(BF16)
    total = tokens_first(jnp.broadcast_to(jnp.exp(after), (HEADS, 128)))[0:8]
    copies[1].wait()
    inject_t = jnp.transpose(inject_ref[...].astype(F32)).astype(BF16)
    low_row = iota((8, 128), 1) < HEAD_DIM
    row = iota((16, 128), 0)
    tails = []
    for half in range(2):
        lanes = slice(half * 128, (half + 1) * 128)
        tail = jnp.zeros((16, 128), F32)
        for s in range(2):
            last = iota((SLEN, 128), 0) == length[s] - 1
            picked = jnp.sum(jnp.where(last, read_ref[s, :, lanes].astype(F32), 0.0), axis=0, keepdims=True)
            tail = jnp.where(row == 2 * core + s, picked, tail)
        tails.append(tail)
    for half in range(2):
        lanes = slice(half * 1024, (half + 1) * 1024)
        wide = jnp.dot(weight, head_lanes(half * 1024, 1024), preferred_element_type=F32)
        copies[2 + half].wait()
        scaled[...] = (values_ref[:, lanes].astype(F32) * wide).astype(BF16)
        state = jnp.dot(inject_t, scaled[...], preferred_element_type=F32).astype(BF16)

        def put(out_ref, half=half, state=state):
            for q in range(8):
                decay = per_pair(total, half * 8 + q, (8, 128), low_row)[0:1]
                for n in range(2):
                    out_ref[2 * q + n, 0:128, :] = state[n * 128 : (n + 1) * 128, q * 128 : (q + 1) * 128]
                    out_ref[2 * q + n, 128:ROWS, :] = with_decay(tails[n], decay).astype(BF16)

        @pl.when(core == half)
        def _(put=put):
            put(keep_ref)

        @pl.when(core != half)
        def _(put=put):
            put(send_ref)


def join_cores_kernel(own_ref, sib_ref, out_ref):
    first = lax.axis_index("core") == 0
    row = iota((16, 128), 0)
    for k in range(16):
        own_tail = own_ref[k, 128:ROWS, :].astype(F32)
        sib_tail = sib_ref[k, 128:ROWS, :].astype(F32)
        own_decay, sib_decay = decay_of(own_tail), decay_of(sib_tail)
        own_weight = jnp.where(first, sib_decay, 1.0)
        sib_weight = jnp.where(first, 1.0, own_decay)
        out_ref[k, 0:128, :] = (
            own_ref[k, 0:128, :].astype(F32) * own_weight + sib_ref[k, 0:128, :].astype(F32) * sib_weight
        ).astype(BF16)
        tail = jnp.where(row < 8, own_tail + sib_tail, 0.0)
        out_ref[k, 128:ROWS, :] = with_decay(tail, own_decay * sib_decay).astype(BF16)


def prefix_kernel(in_ref, out_ref):
    state = jnp.zeros((128, 128), F32)
    for i in range(16):
        out_ref[i, 0:128, :] = state.astype(BF16)
        decay = decay_of(in_ref[i, 128:ROWS, :].astype(F32))
        state = state * decay + in_ref[i, 0:128, :].astype(F32)
    final = state.astype(BF16)
    for i in range(16):
        out_ref[i, 128:ROWS, :] = jnp.dot(
            in_ref[i, 128:ROWS, :], final, preferred_element_type=F32
        ).astype(BF16)


def split_cores_kernel(back_ref, own_ref, sib_ref, mine_ref, send_ref):
    first = lax.axis_index("core") == 0
    for k in range(16):
        q, n = k // 2, k % 2
        arrived = back_ref[k, 0:128, :].astype(F32)
        own_decay = decay_of(own_ref[k, 128:ROWS, :].astype(F32))
        sib_decay = decay_of(sib_ref[k, 128:ROWS, :].astype(F32))
        decay = jnp.where(first, own_decay, sib_decay)
        state = jnp.where(first, own_ref[k, 0:128, :].astype(F32), sib_ref[k, 0:128, :].astype(F32))
        second = arrived * decay + state
        mine_ref[n * 128 : (n + 1) * 128, q * 128 : (q + 1) * 128] = jnp.where(first, arrived, second).astype(BF16)
        send_ref[k, 0:128, :] = jnp.where(first, second, arrived).astype(BF16)
        send_ref[k, 128:ROWS, :] = back_ref[k, 128:ROWS, :]
    for q in range(8):
        mine_ref[256:272, q * 128 : (q + 1) * 128] = (
            back_ref[2 * q, 128:ROWS, :].astype(F32) + back_ref[2 * q + 1, 128:ROWS, :].astype(F32)
        ).astype(BF16)


def local_kernel(
    part, step_ref, decay_ref, skip_ref, values_ref, gate_ref, inject_ref, read_ref, *refs
):
    if part == 0:
        scaled_ref, gain_ref, carry, carry_before, ends, weighted, carried, state, before, stepped_all = refs
    else:
        start, start_before, scaled_ref, gain_ref, ends, weighted, carried, state, before, stepped_all = refs

    @pl.when(pl.program_id(0) == 0)
    def _():
        if part == 0:
            state[...] = jnp.zeros_like(state)
            before[...] = jnp.ones_like(before)
        else:
            state[...] = start[...].astype(F32)
            before[...] = start_before[...]

    step = softplus(step_ref[...])
    logs = step * -jnp.exp(column(decay_ref[...]))
    upto = (iota((BLOCK, BLOCK), 0) <= iota((BLOCK, BLOCK), 1)).astype(F32)
    running = jnp.dot(logs, upto, precision=EXACT, preferred_element_type=F32) * LOG2E
    running_t = tokens_first(running)
    parts = jnp.concatenate([*three_parts(step), jnp.zeros((128 - 3 * HEADS, BLOCK), F32)], axis=0)
    stepped_all[...] = values_ref[...].astype(F32) * jnp.dot(
        jnp.transpose(parts).astype(BF16), head_lanes(0, CH), preferred_element_type=F32
    )
    read = read_ref[...]
    inject = inject_ref[...]
    inject_t = jnp.transpose(inject.astype(F32)).astype(BF16)
    scores = jnp.dot(read, inject_t, preferred_element_type=F32)
    carried[...] = jnp.dot(read, state[...].astype(BF16), preferred_element_type=F32)
    causal = iota((BLOCK, BLOCK), 0) >= iota((BLOCK, BLOCK), 1)
    low = iota((BLOCK, 128), 1) < HEAD_DIM
    for pair in range(16):
        lanes = slice(pair * 128, (pair + 1) * 128)
        mixing = []
        spread = []
        for h in (2 * pair, 2 * pair + 1):
            mine = jnp.broadcast_to(running_t[:, h : h + 1], (BLOCK, BLOCK))
            gap = jnp.where(causal, mine - running[h : h + 1, :], -1e30)
            mixing.append((scores * jnp.exp2(gap)).astype(BF16))
            spread.append(mine)
        now = jnp.where(low, spread[0], spread[1])
        grown = jnp.exp2(now)
        values = values_ref[:, lanes].astype(F32)
        stepped = stepped_all[:, lanes]
        diagonal = jnp.concatenate([jnp.where(low, stepped, 0.0), jnp.where(low, 0.0, stepped)], axis=0)
        local = jnp.dot(
            jnp.concatenate(mixing, axis=1), diagonal.astype(BF16), preferred_element_type=F32
        )
        skip = per_pair(skip_ref[...], pair, (1, 128), low[0:1])
        out = local + carried[:, lanes] * grown + skip * values
        gate = gate_ref[:, lanes].astype(F32)
        gate = gate / (1.0 + jnp.exp(-gate))
        scaled_ref[:, lanes] = (out * gate).astype(BF16)
        gain_ref[:, lanes] = (gate * grown * before[0:1, lanes]).astype(BF16)
        end = now[BLOCK - 1 : BLOCK, :]
        weighted[:, lanes] = (stepped * jnp.exp2(end - now)).astype(BF16)
        ends[0:1, lanes] = jnp.exp2(end)
    state[...] = state[...] * ends[0:1, :] + jnp.dot(inject_t, weighted[...], preferred_element_type=F32)
    before[0:1, :] = before[0:1, :] * ends[0:1, :]
    if part == 0:

        @pl.when(pl.program_id(0) == pl.num_programs(0) - 1)
        def _():
            carry[...] = state[...].astype(BF16)
            carry_before[...] = before[...]


def sample_kernel(
    length, step_ref, decay_ref, skip_ref, values_ref, gate_ref, inject_ref, read_ref, local_ref, grown_ref, gate_out_ref
):
    rate = -jnp.exp(column(decay_ref[...]))
    row = iota((16, CH), 0)
    place = iota((SLEN, 128), 0)
    place_wide = iota((SLEN, STATE), 0)
    narrow = []
    for s in range(2):
        last = length[s] - 1
        step = softplus(step_ref[s])
        logs = step * rate
        pad = jnp.zeros((HEADS, 128 - SLEN), F32)
        step_t = tokens_first(jnp.concatenate([step, pad], axis=1))[0:SLEN]
        logs_t = tokens_first(jnp.concatenate([logs, pad], axis=1))[0:SLEN]
        logs_t = jnp.where(place <= last, logs_t, 0.0)
        gap = jnp.zeros((SLEN, 128), F32)
        for k in range(SLEN):
            gap = gap + jnp.where(place < k, logs_t[k : k + 1], 0.0)
        whole = jnp.sum(logs_t, axis=0, keepdims=True)
        read = jnp.sum(jnp.where(place_wide == last, read_ref[s].astype(F32), 0.0), axis=0, keepdims=True)
        scores = jnp.sum(inject_ref[s].astype(F32) * read, axis=1, keepdims=True)
        narrow.append(jnp.where(place <= last, scores * jnp.exp(gap) * step_t, 0.0))
        narrow.append(jnp.broadcast_to(jnp.exp(whole), (SLEN, 128)))
    skip = jnp.concatenate([skip_ref[...], jnp.zeros((1, 128 - HEADS), F32)], axis=1)
    narrow.append(jnp.broadcast_to(skip, (SLEN, 128)))
    spread = (iota((128, CH), 1) // HEAD_DIM == iota((128, CH), 0)).astype(BF16)
    parts = jnp.concatenate(three_parts(jnp.concatenate(narrow, axis=0)), axis=0).astype(BF16)
    wide = jnp.dot(parts, spread, preferred_element_type=F32)
    wide = wide[0:80] + wide[80:160] + wide[160:240]
    local_all = jnp.zeros((16, CH), F32)
    grown_all = jnp.zeros((16, CH), F32)
    gate_all = jnp.zeros((16, CH), F32)
    for s in range(2):
        values = values_ref[s].astype(F32)
        at_last = iota((SLEN, CH), 0) == length[s] - 1
        picked = jnp.sum(jnp.where(at_last, values, 0.0), axis=0, keepdims=True)
        gate = jnp.sum(jnp.where(at_last, gate_ref[s].astype(F32), 0.0), axis=0, keepdims=True)
        local = jnp.sum(wide[32 * s : 32 * s + SLEN] * values, axis=0, keepdims=True) + wide[64:65] * picked
        local_all = jnp.where(row == s, local, local_all)
        grown_all = jnp.where(row == s, wide[32 * s + SLEN : 32 * s + SLEN + 1], grown_all)
        gate_all = jnp.where(row == s, gate / (1.0 + jnp.exp(-gate)), gate_all)
    local_ref[...] = local_all
    grown_ref[...] = grown_all
    gate_out_ref[...] = gate_all


def normalize(gated, weight):
    mean = jnp.sum(gated * gated, axis=1, keepdims=True) * (1.0 / CH)
    return (gated * lax.rsqrt(mean + 1e-05) * weight).astype(BF16)


FIRST = ((1, 0), (2, 0), (3, 1), (2, 1))
REST = ((3, 0), (1, 1), (0, 0), (0, 1))


def column_copies(pieces, weight_ref, held, sems):
    z = lax.axis_index("head")
    copies = []
    for i, (flip, half) in enumerate(pieces):
        at = pl.multiple_of(((z ^ flip) * 2 + half) * PIECE, PIECE)
        copies.append(pltpu.make_async_copy(weight_ref.at[:, pl.ds(at, PIECE)], held.at[i], sems.at[i]))
    for copy in copies:
        copy.start()
    return copies


def fetch_kernel(pieces, weight_ref, out_ref, sems):
    for copy in column_copies(pieces, weight_ref, out_ref, sems):
        copy.wait()


def resident(x):
    return pltpu.with_memory_space_constraint(x, pltpu.VMEM)


def fetch(pieces, weight):
    out = pl.pallas_call(
        functools.partial(fetch_kernel, pieces),
        out_shape=pltpu.VMEM((len(pieces), CH, PIECE), BF16),
        in_specs=[pl.BlockSpec(memory_space=pl.ANY)],
        out_specs=VMEM,
        scratch_shapes=[pltpu.SemaphoreType.DMA((len(pieces),))],
        compiler_params=pltpu.CompilerParams(vmem_limit_bytes=12 << 20),
        name="fetch_weight",
    )(*in_hbm(weight))
    return resident(out)


def project(normed, columns, outs):
    for column, (ref, k) in zip(columns, outs):
        ref[k] = jnp.dot(normed[...], column[...], preferred_element_type=F32).astype(BF16)


def gate_and_normalize(place, state_ref, read_ref, scaled_ref, gain_ref, norm_ref, normed):
    start, rows = CHUNKS[place]
    arrived = jnp.dot(read_ref[start : start + rows, :], state_ref[0:STATE, :], preferred_element_type=F32)
    here = slice(start % HALF, start % HALF + rows)
    gated = scaled_ref[here, :].astype(F32) + arrived * gain_ref[here, :].astype(F32)
    normed[0:rows, :] = normalize(gated, norm_ref[...])


def join_halves_kernel(mine_ref, theirs_ref, state_ref):
    core = lax.axis_index("core")
    state_ref[:, pl.ds(pl.multiple_of(core * 1024, 1024), 1024)] = mine_ref[...]
    for q in range(8):
        lanes = pl.ds(pl.multiple_of((1 - core) * 1024 + q * 128, 128), 128)
        for n in range(2):
            state_ref[n * 128 : (n + 1) * 128, lanes] = theirs_ref[2 * q + n, 0:128, :]
        state_ref[256:272, lanes] = (
            theirs_ref[2 * q, 128:ROWS, :].astype(F32) + theirs_ref[2 * q + 1, 128:ROWS, :].astype(F32)
        ).astype(BF16)


def chunk_kernel(place, sampled, state_ref, read_ref, scaled_ref, gain_ref, norm_ref, near_ref, far_ref, *refs):
    if place == LEADING:
        *sample, first_ref, second_ref, normed_ref, held, sems = refs
        copies = column_copies(FIRST[1:], far_ref, held, sems)
    else:
        *sample, first_ref, second_ref, normed_ref = refs
        held = far_ref
    gate_and_normalize(place, state_ref, read_ref, scaled_ref, gain_ref, norm_ref, normed_ref)
    if sampled:
        local_ref, grown_ref, gate_ref = sample
        readings = state_ref[256:272, :].astype(F32)
        moved = jnp.concatenate([readings[2:16], readings[0:2]], axis=0)
        readings = jnp.where(lax.axis_index("core") == 0, readings, moved)
        sampled = (local_ref[...] + readings * grown_ref[...]) * gate_ref[...]
        rows = CHUNKS[place][1]
        normed_ref[rows : rows + 16, :] = normalize(sampled, norm_ref[...])
    project(normed_ref, (near_ref.at[0],), ((first_ref, 0),))
    for i, out in enumerate(((first_ref, 1), (second_ref, 0), (second_ref, 1))):
        if place == LEADING:
            copies[i].wait()
        project(normed_ref, (held.at[i],), (out,))


def rest_kernel(normed_ref, weight_ref, rest_ref):
    project(normed_ref, [weight_ref.at[i] for i in range(4)], ((rest_ref, 1), (rest_ref, 3), (rest_ref, 0), (rest_ref, 2)))


def onward_kernel(a_ref, b_ref, rest_ref, a_out, b_out):
    a_out[...] = (rest_ref[1].astype(F32) + a_ref[1].astype(F32)).astype(BF16)
    b_out[...] = (rest_ref[3].astype(F32) + b_ref[1].astype(F32)).astype(BF16)


def finish_kernel(*refs):
    ins, (out_ref, sample_ref, turned, sems) = refs[:-4], refs[-4:]
    copies = []
    for place, (start, rows) in enumerate(CHUNKS):
        ra, rb, rest, sa, sb = ins[5 * place : 5 * place + 5]
        for half, (own, near, far) in enumerate(((0, ra, sa), (2, rb, sb))):
            total = rest[own].astype(F32) + near[0].astype(F32) + far[...].astype(F32)
            columns = slice(half * PIECE, (half + 1) * PIECE)
            here = (columns, slice(start, start + rows))
            turned[here] = jnp.transpose(total[0:rows]).astype(BF16)
            if place == LEADING:
                sample_ref[:, columns] = total[rows : rows + 2].astype(BF16)
            copies.append(pltpu.make_async_copy(turned.at[here], out_ref.at[here], sems.at[len(copies)]))
            copies[-1].start()
    for copy in copies:
        copy.wait()


def in_hbm(*arrays):
    return tuple(pltpu.with_memory_space_constraint(x, pltpu.HBM) for x in arrays)


def call(kernel, name, out_shape, inputs, limit, scalars=0, **more):
    return pl.pallas_call(
        kernel,
        out_shape=out_shape,
        in_specs=[SMEM] * scalars + [VMEM] * (len(inputs) - scalars),
        out_specs=jax.tree.map(lambda _: VMEM, out_shape, is_leaf=lambda x: not isinstance(x, tuple)),
        compiler_params=pltpu.CompilerParams(vmem_limit_bytes=limit << 20),
        cost_estimate=pl.CostEstimate(flops=1, bytes_accessed=1, transcendentals=0),
        name=name,
        **more,
    )(*inputs)


SMEM = pl.BlockSpec(memory_space=pltpu.SMEM)
VMEM = pl.BlockSpec(memory_space=pltpu.VMEM)


def shape(dims, dtype=BF16):
    return jax.ShapeDtypeStruct(dims, dtype)


def swap(x, step):
    return lax.ppermute(x, "head", [(i, i ^ step) for i in range(4)])


def other_core(x):
    return lax.ppermute(x, "core", [(0, 1), (1, 0)])


def local_outputs(part, step, decay, skip, values, gate, inject, read, start=()):
    blocks = TOK // BLOCK // 2
    row = lambda width: pl.BlockSpec((1, width), lambda b: (0, 0))
    tokens = lambda width: pl.BlockSpec((BLOCK, width), lambda b: (b + part * blocks, 0))
    out = pl.BlockSpec((BLOCK, CH), lambda b: (b, 0))
    whole = lambda rows: pl.BlockSpec((rows, CH), lambda b: (0, 0))
    carry = (pltpu.HBM((STATE, CH), BF16), pltpu.HBM((8, CH), F32))
    results = (pltpu.HBM((TOK // 2, CH), BF16),) * 2
    scratch = [
        pltpu.VMEM((8, CH), F32), pltpu.VMEM((BLOCK, CH), BF16), pltpu.VMEM((BLOCK, CH), F32),
        pltpu.VMEM((STATE, CH), F32), pltpu.VMEM((8, CH), F32), pltpu.VMEM((BLOCK, CH), F32),
    ]
    if start:
        start_specs = [whole(STATE), whole(8)]
        out_specs = (out, out)
    else:
        start_specs = []
        results += carry
        out_specs = (out, out, whole(STATE), whole(8))
    step, values, gate, inject, read, *start = in_hbm(step, values, gate, inject, read, *start)
    return pl.pallas_call(
        functools.partial(local_kernel, part),
        grid=(blocks,),
        out_shape=results,
        in_specs=[
            pl.BlockSpec((HEADS, BLOCK), lambda b: (0, b + part * blocks)), row(HEADS), row(HEADS),
            tokens(CH), tokens(CH), tokens(STATE), tokens(STATE), *start_specs,
        ],
        out_specs=out_specs,
        scratch_shapes=scratch,
        compiler_params=pltpu.CompilerParams(vmem_limit_bytes=20 << 20),
        cost_estimate=pl.CostEstimate(flops=3 << 30, bytes_accessed=20 << 20, transcendentals=2 << 20),
        name="local_outputs",
    )(step, decay, skip, values, gate, inject, read, *start)


def per_device(
    prompt_values, prompt_gate, prompt_inject, prompt_read, prompt_step, decay_log, skip_gain, norm_weight, out_weight,
    sample_values, sample_gate, sample_inject, sample_read, sample_step, sample_length,
):
    inject = prompt_inject.reshape(TOK, STATE)
    read = prompt_read.reshape(TOK, STATE)
    decay = decay_log.reshape(1, HEADS)
    skip = skip_gain.reshape(1, HEADS)
    norm = norm_weight.reshape(1, CH)
    s_read = sample_read.reshape(2, SLEN, STATE)
    s_inject = sample_inject.reshape(2, SLEN, STATE)
    slices_shape = shape((16, ROWS, 128))

    anywhere = pl.BlockSpec(memory_space=pl.ANY)
    keep, send = pl.pallas_call(
        end_state_kernel,
        out_shape=(slices_shape,) * 2,
        in_specs=[SMEM, anywhere, VMEM, anywhere, anywhere, VMEM],
        out_specs=(VMEM, VMEM),
        scratch_shapes=[
            pltpu.VMEM((TOK, 1024), BF16), pltpu.VMEM((HEADS, TOK), F32), pltpu.VMEM((TOK, CH), BF16),
            pltpu.VMEM((TOK, STATE), BF16), pltpu.SemaphoreType.DMA((4,)),
        ],
        compiler_params=pltpu.CompilerParams(vmem_limit_bytes=24 << 20),
        name="end_state",
    )(*in_hbm(sample_length, prompt_step, decay, prompt_values, inject, s_read))
    sibling = other_core(send)
    joined = call(join_cores_kernel, "join_cores", slices_shape, (keep, sibling), 16)
    joined, step_1, s_step = lax.optimization_barrier((joined, prompt_step, sample_step.transpose(1, 0, 2)))
    slices = lax.all_to_all(joined, ("y", "x"), 0, 0, tiled=True)
    scaled_1, gain_1, *carry = local_outputs(
        0, step_1, decay, skip, prompt_values, prompt_gate, inject, read
    )
    sample = call(
        sample_kernel, "sample_outputs", (pltpu.HBM((16, CH), F32),) * 3,
        (sample_length, *in_hbm(s_step, decay, skip, sample_values, sample_gate, s_inject, s_read)), 16, 1,
    )
    slices, scaled_1, sample = lax.optimization_barrier((slices, scaled_1, sample))
    prefix = call(prefix_kernel, "prefix", slices_shape, (slices,), 16)
    prefix, step_2 = lax.optimization_barrier((prefix, prompt_step))
    back = lax.all_to_all(prefix, ("y", "x"), 0, 0, tiled=True)
    scaled_2, gain_2 = local_outputs(
        1, step_2, decay, skip, prompt_values, prompt_gate, inject, read, carry
    )
    back, scaled_2, weight = lax.optimization_barrier((back, scaled_2, out_weight))
    mine, send = call(
        split_cores_kernel, "split_cores", (shape((272, 1024)), slices_shape), (back, keep, sibling), 16
    )
    theirs = other_core(send)

    near_columns = fetch(FIRST[:1], weight)
    scaled = (scaled_1, scaled_2)
    gain = (gain_1, gain_2)
    state = call(join_halves_kernel, "join_halves", shape((272, CH)), (mine, theirs), 8)

    def chunk(place, far_columns, *sample):
        start, rows = CHUNKS[place]
        size = rows + (16 if sample else 0)
        leading = place == LEADING
        local = (scaled[start // HALF], gain[start // HALF])
        local = local if leading else in_hbm(*local)
        piece = shape((2, size, PIECE))
        held = pltpu.VMEM((3, CH, PIECE), BF16)
        first, second, normed, *held = pl.pallas_call(
            functools.partial(chunk_kernel, place, bool(sample)),
            out_shape=(piece, piece, shape((size, CH)), *([held] if leading else [])),
            in_specs=[VMEM] * 6 + [anywhere if leading else VMEM] + [VMEM] * len(sample),
            out_specs=(VMEM,) * (4 if leading else 3),
            scratch_shapes=[pltpu.SemaphoreType.DMA((3,))] if leading else [],
            compiler_params=pltpu.CompilerParams(vmem_limit_bytes=24 << 20),
            name="chunk",
        )(state, read, *local, norm, near_columns, far_columns, *sample)
        near = lax.optimization_barrier((swap(first, 1), swap(second, 3)))
        return normed, near, *held

    def exchange(normed, near, rest_columns):
        rest = call(rest_kernel, "rest", shape((4, normed.shape[0], PIECE)), (normed, rest_columns), 24)
        a, b = near
        a_on, b_on = call(onward_kernel, "onward", (shape(a.shape[1:]),) * 2, (a, b, rest), 8)
        return (a, b, rest, *lax.optimization_barrier((swap(a_on, 3), swap(b_on, 1))))

    normed_0, near_0, far_columns = chunk(0, *in_hbm(weight), *sample)
    rest_columns = fetch(REST, weight)
    normed_1, near_1 = chunk(1, resident(far_columns))
    parts = exchange(normed_0, near_0, rest_columns) + exchange(normed_1, near_1, rest_columns)
    prompt_mixed, sample_mixed = pl.pallas_call(
        finish_kernel,
        out_shape=(shape((1024, TOK)), shape((2, 1024))),
        in_specs=[VMEM] * 10,
        out_specs=(anywhere, VMEM),
        scratch_shapes=[pltpu.VMEM((1024, TOK), BF16), pltpu.SemaphoreType.DMA((4,))],
        compiler_params=pltpu.CompilerParams(vmem_limit_bytes=16 << 20),
        name="finish",
    )(*parts)
    return prompt_mixed, sample_mixed.T


def solution(mesh):
    split = Mesh(mesh.devices.reshape(4, 4, 2, mesh.shape["head"]), ("y", "x", "core", "head"))
    return jax.shard_map(
        per_device,
        mesh=split,
        in_specs=(
            P(CTX, "head"), P(CTX, "head"), P(CTX, "head", None), P(CTX, "head", None), P("head", CTX),
            P("head"), P("head"), P("head"), P("head", None),
            P(CTX, None, "head"), P(CTX, None, "head"), P(CTX, None, "head", None), P(CTX, None, "head", None),
            P("head", CTX, None), P(CTX),
        ),
        out_specs=(P("head", CTX), P("head", CTX)),
        check_vma=False,
    )
```

```python
import functools

import jax
import jax.numpy as jnp
from jax import lax
from jax.experimental import pallas as pl
from jax.experimental.pallas import tpu as pltpu
from jax.sharding import Mesh
from jax.sharding import PartitionSpec as P

HEADS = 32
HEAD_DIM = 64
STATE = 256
BLOCK = 128
SLEN = 16
TOK = 512
CH = HEADS * HEAD_DIM
PIECE = 512
HALF = TOK // 2
TAIL = 8
ROWS = 128 + TAIL
CTX = ("y", "x", "core")
F32 = jnp.float32
BF16 = jnp.bfloat16
EXACT = lax.Precision.HIGHEST
LOG2E = 1.4426950408889634
CHUNKS = ((256, 256), (0, 256))
LEADING = 0


def softplus(v):
    return jnp.maximum(v, 0.0) + jnp.log1p(jnp.exp(-jnp.abs(v)))


def iota(shape, dim):
    return lax.broadcasted_iota(jnp.int32, shape, dim)


def column(row):
    n = row.shape[1]
    square = jnp.broadcast_to(row, (n, n))
    return jnp.sum(jnp.where(iota((n, n), 0) == iota((n, n), 1), square, 0.0), axis=1, keepdims=True)


def tokens_first(x):
    pad = jnp.zeros((128 - x.shape[0], x.shape[1]), F32)
    return jnp.transpose(jnp.concatenate([x, pad], axis=0))


def per_pair(columns, pair, shape, low):
    first = jnp.broadcast_to(columns[:, 2 * pair : 2 * pair + 1], shape)
    second = jnp.broadcast_to(columns[:, 2 * pair + 1 : 2 * pair + 2], shape)
    return jnp.where(low, first, second)


def head_lanes(start, width):
    row, lane = iota((128, width), 0), iota((128, width), 1) + start
    return (((row & (HEADS - 1)) == (lane >> 6)) & (row < 3 * HEADS)).astype(BF16)


def three_parts(x):
    hi = x.astype(BF16).astype(F32)
    mid = (x - hi).astype(BF16).astype(F32)
    lo = (x - hi - mid).astype(BF16).astype(F32)
    return hi, mid, lo


def decay_of(tail):
    return tail[4:5] + tail[5:6] + tail[6:7]


def with_decay(tail, decay):
    row = iota((TAIL, 128), 0)
    for i, part in enumerate(three_parts(decay)):
        tail = jnp.where(row == 4 + i, part, tail)
    return tail


def end_state_kernel(
    length, step_any, decay_ref, values_any, inject_any, read_ref, keep_ref, send_ref,
    scaled, step_ref, values_ref, inject_ref, sems,
):
    copies = [
        pltpu.make_async_copy(step_any, step_ref, sems.at[0]),
        pltpu.make_async_copy(inject_any, inject_ref, sems.at[1]),
    ]
    for half in range(2):
        lanes = slice(half * 1024, (half + 1) * 1024)
        copies.append(pltpu.make_async_copy(values_any.at[:, lanes], values_ref.at[:, lanes], sems.at[2 + half]))
    for copy in copies:
        copy.start()
    copies[0].wait()
    core = lax.axis_index("core")
    step = softplus(step_ref[...])
    logs = step * -jnp.exp(column(decay_ref[...]))
    later = (iota((BLOCK, BLOCK), 0) > iota((BLOCK, BLOCK), 1)).astype(F32)
    after = jnp.zeros((HEADS, 1), F32)
    parts = []
    for b in reversed(range(TOK // BLOCK)):
        here = logs[:, b * BLOCK : (b + 1) * BLOCK]
        parts.append(jnp.dot(here, later, precision=EXACT, preferred_element_type=F32) + after)
        after = after + jnp.sum(here, axis=1, keepdims=True)
    weight = jnp.exp(jnp.concatenate(parts[::-1], axis=1)) * step
    weight = jnp.transpose(jnp.concatenate([*three_parts(weight), jnp.zeros((128 - 3 * HEADS, TOK), F32)], axis=0))
    weight = weight.astype(BF16)
    total = tokens_first(jnp.broadcast_to(jnp.exp(after), (HEADS, 128)))[0:8]
    copies[1].wait()
    inject_t = jnp.transpose(inject_ref[...].astype(F32)).astype(BF16)
    low_row = iota((8, 128), 1) < HEAD_DIM
    row = iota((TAIL, 128), 0)
    tails = []
    for half in range(2):
        lanes = slice(half * 128, (half + 1) * 128)
        tail = jnp.zeros((TAIL, 128), F32)
        for s in range(2):
            last = iota((SLEN, 128), 0) == length[s] - 1
            picked = jnp.sum(jnp.where(last, read_ref[s, :, lanes].astype(F32), 0.0), axis=0, keepdims=True)
            tail = jnp.where(row == 2 * core + s, picked, tail)
        tails.append(tail)
    for half in range(2):
        lanes = slice(half * 1024, (half + 1) * 1024)
        wide = jnp.dot(weight, head_lanes(half * 1024, 1024), preferred_element_type=F32)
        copies[2 + half].wait()
        scaled[...] = (values_ref[:, lanes].astype(F32) * wide).astype(BF16)
        state = jnp.dot(inject_t, scaled[...], preferred_element_type=F32).astype(BF16)

        def put(out_ref, half=half, state=state):
            for q in range(8):
                decay = per_pair(total, half * 8 + q, (8, 128), low_row)[0:1]
                for n in range(2):
                    out_ref[2 * q + n, 0:128, :] = state[n * 128 : (n + 1) * 128, q * 128 : (q + 1) * 128]
                    out_ref[2 * q + n, 128:ROWS, :] = with_decay(tails[n], decay).astype(BF16)

        @pl.when(core == half)
        def _(put=put):
            put(keep_ref)

        @pl.when(core != half)
        def _(put=put):
            put(send_ref)


def join_cores_kernel(own_ref, sib_ref, out_ref):
    first = lax.axis_index("core") == 0
    row = iota((TAIL, 128), 0)
    for k in range(16):
        own_tail = own_ref[k, 128:ROWS, :].astype(F32)
        sib_tail = sib_ref[k, 128:ROWS, :].astype(F32)
        own_decay, sib_decay = decay_of(own_tail), decay_of(sib_tail)
        own_weight = jnp.where(first, sib_decay, 1.0)
        sib_weight = jnp.where(first, 1.0, own_decay)
        out_ref[k, 0:128, :] = (
            own_ref[k, 0:128, :].astype(F32) * own_weight + sib_ref[k, 0:128, :].astype(F32) * sib_weight
        ).astype(BF16)
        tail = jnp.where(row < 4, own_tail + sib_tail, 0.0)
        out_ref[k, 128:ROWS, :] = with_decay(tail, own_decay * sib_decay).astype(BF16)


def prefix_kernel(in_ref, out_ref):
    state = jnp.zeros((128, 128), F32)
    for i in range(16):
        out_ref[i, 0:128, :] = state.astype(BF16)
        decay = decay_of(in_ref[i, 128:ROWS, :].astype(F32))
        state = state * decay + in_ref[i, 0:128, :].astype(F32)
    tails = jnp.concatenate([in_ref[i, 128:ROWS, :].astype(F32) for i in range(16)], axis=0).astype(BF16)
    readings = jnp.dot(tails, state.astype(BF16), preferred_element_type=F32)
    for i in range(16):
        out_ref[i, 128:ROWS, :] = readings[TAIL * i : TAIL * (i + 1)].astype(BF16)


def split_cores_kernel(back_ref, own_ref, sib_ref, mine_ref, send_ref):
    first = lax.axis_index("core") == 0
    for k in range(16):
        q, n = k // 2, k % 2
        arrived = back_ref[k, 0:128, :].astype(F32)
        own_decay = decay_of(own_ref[k, 128:ROWS, :].astype(F32))
        sib_decay = decay_of(sib_ref[k, 128:ROWS, :].astype(F32))
        decay = jnp.where(first, own_decay, sib_decay)
        state = jnp.where(first, own_ref[k, 0:128, :].astype(F32), sib_ref[k, 0:128, :].astype(F32))
        second = arrived * decay + state
        mine_ref[n * 128 : (n + 1) * 128, q * 128 : (q + 1) * 128] = jnp.where(first, arrived, second).astype(BF16)
        send_ref[k, 0:128, :] = jnp.where(first, second, arrived).astype(BF16)
        send_ref[k, 128:ROWS, :] = back_ref[k, 128:ROWS, :]
    for q in range(8):
        mine_ref[STATE : STATE + TAIL, q * 128 : (q + 1) * 128] = (
            back_ref[2 * q, 128:ROWS, :].astype(F32) + back_ref[2 * q + 1, 128:ROWS, :].astype(F32)
        ).astype(BF16)


def local_kernel(
    part, step_ref, decay_ref, skip_ref, values_ref, gate_ref, inject_ref, read_ref, *refs
):
    if part == 0:
        scaled_ref, gain_ref, carry, carry_before, ends, weighted, carried, state, before, stepped_all = refs
    else:
        start, start_before, scaled_ref, gain_ref, ends, weighted, carried, state, before, stepped_all = refs

    @pl.when(pl.program_id(0) == 0)
    def _():
        if part == 0:
            state[...] = jnp.zeros_like(state)
            before[...] = jnp.ones_like(before)
        else:
            state[...] = start[...].astype(F32)
            before[...] = start_before[...]

    step = softplus(step_ref[...])
    logs = step * -jnp.exp(column(decay_ref[...]))
    upto = (iota((BLOCK, BLOCK), 0) <= iota((BLOCK, BLOCK), 1)).astype(F32)
    running = jnp.dot(logs, upto, precision=EXACT, preferred_element_type=F32) * LOG2E
    running_t = tokens_first(running)
    parts = jnp.concatenate([*three_parts(step), jnp.zeros((128 - 3 * HEADS, BLOCK), F32)], axis=0)
    stepped_all[...] = values_ref[...].astype(F32) * jnp.dot(
        jnp.transpose(parts).astype(BF16), head_lanes(0, CH), preferred_element_type=F32
    )
    read = read_ref[...]
    inject = inject_ref[...]
    inject_t = jnp.transpose(inject.astype(F32)).astype(BF16)
    scores = jnp.dot(read, inject_t, preferred_element_type=F32)
    carried[...] = jnp.dot(read, state[...].astype(BF16), preferred_element_type=F32)
    causal = iota((BLOCK, BLOCK), 0) >= iota((BLOCK, BLOCK), 1)
    low = iota((BLOCK, 128), 1) < HEAD_DIM
    for pair in range(16):
        lanes = slice(pair * 128, (pair + 1) * 128)
        mixing = []
        spread = []
        for h in (2 * pair, 2 * pair + 1):
            mine = jnp.broadcast_to(running_t[:, h : h + 1], (BLOCK, BLOCK))
            gap = jnp.where(causal, mine - running[h : h + 1, :], -1e30)
            mixing.append((scores * jnp.exp2(gap)).astype(BF16))
            spread.append(mine)
        now = jnp.where(low, spread[0], spread[1])
        grown = jnp.exp2(now)
        values = values_ref[:, lanes].astype(F32)
        stepped = stepped_all[:, lanes]
        diagonal = jnp.concatenate([jnp.where(low, stepped, 0.0), jnp.where(low, 0.0, stepped)], axis=0)
        local = jnp.dot(
            jnp.concatenate(mixing, axis=1), diagonal.astype(BF16), preferred_element_type=F32
        )
        skip = per_pair(skip_ref[...], pair, (1, 128), low[0:1])
        out = local + carried[:, lanes] * grown + skip * values
        gate = gate_ref[:, lanes].astype(F32)
        gate = gate * jax.nn.sigmoid(gate)
        scaled_ref[:, lanes] = (out * gate).astype(BF16)
        gain_ref[:, lanes] = (gate * grown * before[0:1, lanes]).astype(BF16)
        end = now[BLOCK - 1 : BLOCK, :]
        weighted[:, lanes] = (stepped * jnp.exp2(end - now)).astype(BF16)
        ends[0:1, lanes] = jnp.exp2(end)
    state[...] = state[...] * ends[0:1, :] + jnp.dot(inject_t, weighted[...], preferred_element_type=F32)
    before[0:1, :] = before[0:1, :] * ends[0:1, :]
    if part == 0:

        @pl.when(pl.program_id(0) == pl.num_programs(0) - 1)
        def _():
            carry[...] = state[...].astype(BF16)
            carry_before[...] = before[...]


def sample_kernel(
    length, step_ref, decay_ref, skip_ref, values_ref, gate_ref, inject_ref, read_ref, local_ref, grown_ref, gate_out_ref
):
    rate = -jnp.exp(column(decay_ref[...]))
    row = iota((16, CH), 0)
    place = iota((SLEN, 128), 0)
    place_wide = iota((SLEN, STATE), 0)
    narrow = []
    for s in range(2):
        last = length[s] - 1
        step = softplus(step_ref[s])
        logs = step * rate
        pad = jnp.zeros((HEADS, 128 - SLEN), F32)
        step_t = tokens_first(jnp.concatenate([step, pad], axis=1))[0:SLEN]
        logs_t = tokens_first(jnp.concatenate([logs, pad], axis=1))[0:SLEN]
        logs_t = jnp.where(place <= last, logs_t, 0.0)
        gap = jnp.zeros((SLEN, 128), F32)
        for k in range(SLEN):
            gap = gap + jnp.where(place < k, logs_t[k : k + 1], 0.0)
        whole = jnp.sum(logs_t, axis=0, keepdims=True)
        read = jnp.sum(jnp.where(place_wide == last, read_ref[s].astype(F32), 0.0), axis=0, keepdims=True)
        scores = jnp.sum(inject_ref[s].astype(F32) * read, axis=1, keepdims=True)
        narrow.append(jnp.where(place <= last, scores * jnp.exp(gap) * step_t, 0.0))
        narrow.append(jnp.broadcast_to(jnp.exp(whole), (SLEN, 128)))
    skip = jnp.concatenate([skip_ref[...], jnp.zeros((1, 128 - HEADS), F32)], axis=1)
    narrow.append(jnp.broadcast_to(skip, (SLEN, 128)))
    spread = (iota((128, CH), 1) // HEAD_DIM == iota((128, CH), 0)).astype(BF16)
    parts = jnp.concatenate(three_parts(jnp.concatenate(narrow, axis=0)), axis=0).astype(BF16)
    wide = jnp.dot(parts, spread, preferred_element_type=F32)
    wide = wide[0:80] + wide[80:160] + wide[160:240]
    local_all = jnp.zeros((16, CH), F32)
    grown_all = jnp.zeros((16, CH), F32)
    gate_all = jnp.zeros((16, CH), F32)
    for s in range(2):
        values = values_ref[s].astype(F32)
        at_last = iota((SLEN, CH), 0) == length[s] - 1
        picked = jnp.sum(jnp.where(at_last, values, 0.0), axis=0, keepdims=True)
        gate = jnp.sum(jnp.where(at_last, gate_ref[s].astype(F32), 0.0), axis=0, keepdims=True)
        local = jnp.sum(wide[32 * s : 32 * s + SLEN] * values, axis=0, keepdims=True) + wide[64:65] * picked
        local_all = jnp.where(row == s, local, local_all)
        grown_all = jnp.where(row == s, wide[32 * s + SLEN : 32 * s + SLEN + 1], grown_all)
        gate_all = jnp.where(row == s, gate / (1.0 + jnp.exp(-gate)), gate_all)
    local_ref[...] = local_all
    grown_ref[...] = grown_all
    gate_out_ref[...] = gate_all


def normalize(gated, weight):
    mean = jnp.sum(gated * gated, axis=1, keepdims=True) * (1.0 / CH)
    return (gated * lax.rsqrt(mean + 1e-05) * weight).astype(BF16)


FIRST = ((1, 0), (2, 0), (3, 1), (2, 1))
REST = ((3, 0), (1, 1), (0, 0), (0, 1))


def column_copies(pieces, weight_ref, held, sems):
    z = lax.axis_index("head")
    copies = []
    for i, (flip, half) in enumerate(pieces):
        at = pl.multiple_of(((z ^ flip) * 2 + half) * PIECE, PIECE)
        copies.append(pltpu.make_async_copy(weight_ref.at[:, pl.ds(at, PIECE)], held.at[i], sems.at[i]))
    return copies


def fetch_kernel(pieces, weight_ref, out_ref, sems):
    copies = column_copies(pieces, weight_ref, out_ref, sems)
    for copy in copies:
        copy.start()
    for copy in copies:
        copy.wait()


def resident(x):
    return pltpu.with_memory_space_constraint(x, pltpu.VMEM)


def fetch(pieces, weight):
    out = pl.pallas_call(
        functools.partial(fetch_kernel, pieces),
        out_shape=pltpu.VMEM((len(pieces), CH, PIECE), BF16),
        in_specs=[pl.BlockSpec(memory_space=pl.ANY)],
        out_specs=VMEM,
        scratch_shapes=[pltpu.SemaphoreType.DMA((len(pieces),))],
        compiler_params=pltpu.CompilerParams(vmem_limit_bytes=12 << 20),
        name="fetch_weight",
    )(*in_hbm(weight))
    return resident(out)


def project(normed, columns, outs):
    for column, (ref, k) in zip(columns, outs):
        ref[k] = jnp.dot(normed[...], column[...], preferred_element_type=F32).astype(BF16)


HERE = tuple(slice(start % HALF, start % HALF + rows) for start, rows in CHUNKS)


def arriving(place, state_ref, read_ref):
    start, rows = CHUNKS[place]
    return jnp.dot(read_ref[start : start + rows, :], state_ref[0:STATE, :], preferred_element_type=F32)


def join_halves_kernel(mine_ref, theirs_ref, state_ref):
    core = lax.axis_index("core")
    state_ref[:, pl.ds(pl.multiple_of(core * 1024, 1024), 1024)] = mine_ref[...]
    for q in range(8):
        lanes = pl.ds(pl.multiple_of((1 - core) * 1024 + q * 128, 128), 128)
        for n in range(2):
            state_ref[n * 128 : (n + 1) * 128, lanes] = theirs_ref[2 * q + n, 0:128, :]
        state_ref[STATE : STATE + TAIL, lanes] = (
            theirs_ref[2 * q, 128:ROWS, :].astype(F32) + theirs_ref[2 * q + 1, 128:ROWS, :].astype(F32)
        ).astype(BF16)


def chunk_kernel(place, sampled, state_ref, read_ref, scaled_ref, gain_ref, norm_ref, near_ref, far_ref, *refs):
    if place == LEADING:
        *sample, first_ref, second_ref, normed_ref, held, sems = refs
        copies = column_copies(FIRST[1:], far_ref, held, sems)
        copies[0].start()
    else:
        *sample, first_ref, second_ref, normed_ref = refs
        held = far_ref
    arrived = arriving(place, state_ref, read_ref)
    if place == LEADING:
        copies[1].start()
    gated = scaled_ref[HERE[place], :].astype(F32) + arrived * gain_ref[HERE[place], :].astype(F32)
    normed_ref[0 : CHUNKS[place][1], :] = normalize(gated, norm_ref[...])
    if place == LEADING:
        copies[2].start()
    if sampled:
        local_ref, grown_ref, gate_ref = sample
        readings = state_ref[STATE : STATE + TAIL, :].astype(F32)
        moved = jnp.concatenate([readings[2:TAIL], readings[0:2]], axis=0)
        readings = jnp.where(lax.axis_index("core") == 0, readings, moved)
        readings = jnp.concatenate([readings, jnp.zeros((16 - TAIL, CH), F32)], axis=0)
        sampled = (local_ref[...] + readings * grown_ref[...]) * gate_ref[...]
        rows = CHUNKS[place][1]
        normed_ref[rows : rows + 16, :] = normalize(sampled, norm_ref[...])
    project(normed_ref, (near_ref.at[0],), ((first_ref, 0),))
    for i, out in enumerate(((first_ref, 1), (second_ref, 0), (second_ref, 1))):
        if place == LEADING:
            copies[i].wait()
        project(normed_ref, (held.at[i],), (out,))


def rest_kernel(normed_ref, weight_ref, rest_ref):
    project(normed_ref, [weight_ref.at[i] for i in range(4)], ((rest_ref, 1), (rest_ref, 3), (rest_ref, 0), (rest_ref, 2)))


def onward_kernel(a_ref, b_ref, rest_ref, a_out, b_out):
    a_out[...] = (rest_ref[1].astype(F32) + a_ref[1].astype(F32)).astype(BF16)
    b_out[...] = (rest_ref[3].astype(F32) + b_ref[1].astype(F32)).astype(BF16)


def finish_kernel(*refs):
    ins, out_ref, sample_ref = refs[:-2], refs[-2], refs[-1]
    for place, (start, rows) in enumerate(CHUNKS):
        ra, rb, rest, sa, sb = ins[5 * place : 5 * place + 5]
        for half, (own, near, far) in enumerate(((0, ra, sa), (2, rb, sb))):
            total = rest[own].astype(F32) + near[0].astype(F32) + far[...].astype(F32)
            columns = slice(half * PIECE, (half + 1) * PIECE)
            out_ref[columns, start : start + rows] = jnp.transpose(total[0:rows]).astype(BF16)
            if place == LEADING:
                sample_ref[:, columns] = total[rows : rows + 2].astype(BF16)


def in_hbm(*arrays):
    return tuple(pltpu.with_memory_space_constraint(x, pltpu.HBM) for x in arrays)


def call(kernel, name, out_shape, inputs, limit, scalars=0, **more):
    return pl.pallas_call(
        kernel,
        out_shape=out_shape,
        in_specs=[SMEM] * scalars + [VMEM] * (len(inputs) - scalars),
        out_specs=jax.tree.map(lambda _: VMEM, out_shape, is_leaf=lambda x: not isinstance(x, tuple)),
        compiler_params=pltpu.CompilerParams(vmem_limit_bytes=limit << 20),
        cost_estimate=pl.CostEstimate(flops=1, bytes_accessed=1, transcendentals=0),
        name=name,
        **more,
    )(*inputs)


SMEM = pl.BlockSpec(memory_space=pltpu.SMEM)
VMEM = pl.BlockSpec(memory_space=pltpu.VMEM)


def shape(dims, dtype=BF16):
    return jax.ShapeDtypeStruct(dims, dtype)


def swap(x, step):
    return lax.ppermute(x, "head", [(i, i ^ step) for i in range(4)])


def other_core(x):
    return lax.ppermute(x, "core", [(0, 1), (1, 0)])


def local_outputs(part, step, decay, skip, values, gate, inject, read, start=()):
    blocks = TOK // BLOCK // 2
    row = lambda width: pl.BlockSpec((1, width), lambda b: (0, 0))
    tokens = lambda width: pl.BlockSpec((BLOCK, width), lambda b: (b + part * blocks, 0))
    out = pl.BlockSpec((BLOCK, CH), lambda b: (b, 0))
    whole = lambda rows: pl.BlockSpec((rows, CH), lambda b: (0, 0))
    carry = (pltpu.HBM((STATE, CH), BF16), pltpu.HBM((8, CH), F32))
    results = (pltpu.HBM((TOK // 2, CH), BF16),) * 2
    scratch = [
        pltpu.VMEM((8, CH), F32), pltpu.VMEM((BLOCK, CH), BF16), pltpu.VMEM((BLOCK, CH), F32),
        pltpu.VMEM((STATE, CH), F32), pltpu.VMEM((8, CH), F32), pltpu.VMEM((BLOCK, CH), F32),
    ]
    if start:
        start_specs = [whole(STATE), whole(8)]
        out_specs = (out, out)
    else:
        start_specs = []
        results += carry
        out_specs = (out, out, whole(STATE), whole(8))
    step, values, gate, inject, read, *start = in_hbm(step, values, gate, inject, read, *start)
    return pl.pallas_call(
        functools.partial(local_kernel, part),
        grid=(blocks,),
        out_shape=results,
        in_specs=[
            pl.BlockSpec((HEADS, BLOCK), lambda b: (0, b + part * blocks)), row(HEADS), row(HEADS),
            tokens(CH), tokens(CH), tokens(STATE), tokens(STATE), *start_specs,
        ],
        out_specs=out_specs,
        scratch_shapes=scratch,
        compiler_params=pltpu.CompilerParams(vmem_limit_bytes=20 << 20),
        cost_estimate=pl.CostEstimate(flops=3 << 30, bytes_accessed=20 << 20, transcendentals=2 << 20),
        name="local_outputs",
    )(step, decay, skip, values, gate, inject, read, *start)


def per_device(
    prompt_values, prompt_gate, prompt_inject, prompt_read, prompt_step, decay_log, skip_gain, norm_weight, out_weight,
    sample_values, sample_gate, sample_inject, sample_read, sample_step, sample_length,
):
    inject = prompt_inject.reshape(TOK, STATE)
    read = prompt_read.reshape(TOK, STATE)
    decay = decay_log.reshape(1, HEADS)
    skip = skip_gain.reshape(1, HEADS)
    norm = norm_weight.reshape(1, CH)
    s_read = sample_read.reshape(2, SLEN, STATE)
    s_inject = sample_inject.reshape(2, SLEN, STATE)
    slices_shape = shape((16, ROWS, 128))

    anywhere = pl.BlockSpec(memory_space=pl.ANY)
    keep, send = pl.pallas_call(
        end_state_kernel,
        out_shape=(slices_shape,) * 2,
        in_specs=[SMEM, anywhere, VMEM, anywhere, anywhere, VMEM],
        out_specs=(VMEM, VMEM),
        scratch_shapes=[
            pltpu.VMEM((TOK, 1024), BF16), pltpu.VMEM((HEADS, TOK), F32), pltpu.VMEM((TOK, CH), BF16),
            pltpu.VMEM((TOK, STATE), BF16), pltpu.SemaphoreType.DMA((4,)),
        ],
        compiler_params=pltpu.CompilerParams(vmem_limit_bytes=24 << 20),
        name="end_state",
    )(*in_hbm(sample_length, prompt_step, decay, prompt_values, inject, s_read))
    sibling = other_core(send)
    joined = call(join_cores_kernel, "join_cores", slices_shape, (keep, sibling), 16)
    joined, step_1, s_step = lax.optimization_barrier((joined, prompt_step, sample_step.transpose(1, 0, 2)))
    slices = lax.all_to_all(joined, ("y", "x"), 0, 0, tiled=True)
    scaled_1, gain_1, *carry = local_outputs(
        0, step_1, decay, skip, prompt_values, prompt_gate, inject, read
    )
    sample = call(
        sample_kernel, "sample_outputs", (pltpu.HBM((16, CH), F32),) * 3,
        (sample_length, *in_hbm(s_step, decay, skip, sample_values, sample_gate, s_inject, s_read)), 16, 1,
    )
    slices, scaled_1, sample = lax.optimization_barrier((slices, scaled_1, sample))
    prefix = call(prefix_kernel, "prefix", slices_shape, (slices,), 16)
    prefix, step_2 = lax.optimization_barrier((prefix, prompt_step))
    back = lax.all_to_all(prefix, ("y", "x"), 0, 0, tiled=True)
    scaled_2, gain_2 = local_outputs(
        1, step_2, decay, skip, prompt_values, prompt_gate, inject, read, carry
    )
    back, scaled_2, weight = lax.optimization_barrier((back, scaled_2, out_weight))
    mine, send = call(
        split_cores_kernel, "split_cores", (shape((STATE + TAIL, 1024)), slices_shape), (back, keep, sibling), 16
    )
    theirs = other_core(send)

    near_columns = fetch(FIRST[:1], weight)
    scaled = (scaled_1, scaled_2)
    gain = (gain_1, gain_2)
    state = call(join_halves_kernel, "join_halves", shape((STATE + TAIL, CH)), (mine, theirs), 8)

    def chunk(place, far_columns, *sample):
        start, rows = CHUNKS[place]
        size = rows + (16 if sample else 0)
        leading = place == LEADING
        local = (scaled[start // HALF], gain[start // HALF])
        local = local if leading else in_hbm(*local)
        piece = shape((2, size, PIECE))
        held = pltpu.VMEM((3, CH, PIECE), BF16)
        first, second, normed, *held = pl.pallas_call(
            functools.partial(chunk_kernel, place, bool(sample)),
            out_shape=(piece, piece, shape((size, CH)), *([held] if leading else [])),
            in_specs=[VMEM] * 6 + [anywhere if leading else VMEM] + [VMEM] * len(sample),
            out_specs=(VMEM,) * (4 if leading else 3),
            scratch_shapes=[pltpu.SemaphoreType.DMA((3,))] if leading else [],
            compiler_params=pltpu.CompilerParams(vmem_limit_bytes=24 << 20),
            name="chunk",
        )(state, read, *local, norm, near_columns, far_columns, *sample)
        near = lax.optimization_barrier((swap(first, 1), swap(second, 3)))
        return normed, near, *held

    def exchange(normed, near, rest_columns):
        rest = call(rest_kernel, "rest", shape((4, normed.shape[0], PIECE)), (normed, rest_columns), 24)
        a, b = near
        a_on, b_on = call(onward_kernel, "onward", (shape(a.shape[1:]),) * 2, (a, b, rest), 8)
        return (a, b, rest, *lax.optimization_barrier((swap(a_on, 3), swap(b_on, 1))))

    normed_0, near_0, far_columns = chunk(0, *in_hbm(weight), *sample)
    rest_columns = fetch(REST, weight)
    normed_1, near_1 = chunk(1, resident(far_columns))
    parts = exchange(normed_0, near_0, rest_columns) + exchange(normed_1, near_1, rest_columns)
    prompt_mixed, sample_mixed = call(finish_kernel, "finish", (shape((1024, TOK)), shape((2, 1024))), parts, 16)
    return prompt_mixed, sample_mixed.T


def solution(mesh):
    split = Mesh(mesh.devices.reshape(4, 4, 2, mesh.shape["head"]), ("y", "x", "core", "head"))
    return jax.shard_map(
        per_device,
        mesh=split,
        in_specs=(
            P(CTX, "head"), P(CTX, "head"), P(CTX, "head", None), P(CTX, "head", None), P("head", CTX),
            P("head"), P("head"), P("head"), P("head", None),
            P(CTX, None, "head"), P(CTX, None, "head"), P(CTX, None, "head", None), P(CTX, None, "head", None),
            P("head", CTX, None), P(CTX),
        ),
        out_specs=(P("head", CTX), P("head", CTX)),
        check_vma=False,
    )
```

```python
import functools

import jax
import jax.numpy as jnp
from jax import lax
from jax.experimental import pallas as pl
from jax.experimental.pallas import tpu as pltpu
from jax.sharding import Mesh
from jax.sharding import PartitionSpec as P

HEADS = 32
HEAD_DIM = 64
STATE = 256
BLOCK = 128
SLEN = 16
TOK = 512
CH = HEADS * HEAD_DIM
PIECE = 512
HALF = TOK // 2
TAIL = 8
ROWS = 128 + TAIL
CTX = ("y", "x", "core")
F32 = jnp.float32
BF16 = jnp.bfloat16
EXACT = lax.Precision.HIGHEST
LOG2E = 1.4426950408889634
CHUNKS = ((256, 256), (0, 256))
LEADING = 0


def softplus(v):
    return jnp.maximum(v, 0.0) + jnp.log1p(jnp.exp(-jnp.abs(v)))


def iota(shape, dim):
    return lax.broadcasted_iota(jnp.int32, shape, dim)


def column(row):
    n = row.shape[1]
    square = jnp.broadcast_to(row, (n, n))
    return jnp.sum(jnp.where(iota((n, n), 0) == iota((n, n), 1), square, 0.0), axis=1, keepdims=True)


def tokens_first(x):
    pad = jnp.zeros((128 - x.shape[0], x.shape[1]), F32)
    return jnp.transpose(jnp.concatenate([x, pad], axis=0))


def per_pair(columns, pair, shape, low):
    first = jnp.broadcast_to(columns[:, 2 * pair : 2 * pair + 1], shape)
    second = jnp.broadcast_to(columns[:, 2 * pair + 1 : 2 * pair + 2], shape)
    return jnp.where(low, first, second)


def head_lanes(start, width):
    row, lane = iota((128, width), 0), iota((128, width), 1) + start
    return (((row & (HEADS - 1)) == (lane >> 6)) & (row < 3 * HEADS)).astype(BF16)


def three_parts(x):
    hi = x.astype(BF16).astype(F32)
    mid = (x - hi).astype(BF16).astype(F32)
    lo = (x - hi - mid).astype(BF16).astype(F32)
    return hi, mid, lo


def decay_of(tail):
    return tail[4:5] + tail[5:6] + tail[6:7]


def with_decay(tail, decay):
    row = iota((TAIL, 128), 0)
    for i, part in enumerate(three_parts(decay)):
        tail = jnp.where(row == 4 + i, part, tail)
    return tail


def end_state_kernel(
    length, step_any, decay_ref, values_any, inject_any, read_ref, keep_ref, send_ref,
    scaled, step_ref, values_ref, inject_ref, sems,
):
    copies = [
        pltpu.make_async_copy(step_any, step_ref, sems.at[0]),
        pltpu.make_async_copy(inject_any, inject_ref, sems.at[1]),
    ]
    for half in range(2):
        lanes = slice(half * 1024, (half + 1) * 1024)
        copies.append(pltpu.make_async_copy(values_any.at[:, lanes], values_ref.at[:, lanes], sems.at[2 + half]))
    for copy in copies:
        copy.start()
    copies[0].wait()
    core = lax.axis_index("core")
    step = softplus(step_ref[...])
    logs = step * -jnp.exp(column(decay_ref[...]))
    later = (iota((BLOCK, BLOCK), 0) > iota((BLOCK, BLOCK), 1)).astype(F32)
    after = jnp.zeros((HEADS, 1), F32)
    parts = []
    for b in reversed(range(TOK // BLOCK)):
        here = logs[:, b * BLOCK : (b + 1) * BLOCK]
        parts.append(jnp.dot(here, later, precision=EXACT, preferred_element_type=F32) + after)
        after = after + jnp.sum(here, axis=1, keepdims=True)
    weight = jnp.exp(jnp.concatenate(parts[::-1], axis=1)) * step
    weight = jnp.transpose(jnp.concatenate([*three_parts(weight), jnp.zeros((128 - 3 * HEADS, TOK), F32)], axis=0))
    weight = weight.astype(BF16)
    total = tokens_first(jnp.broadcast_to(jnp.exp(after), (HEADS, 128)))[0:8]
    copies[1].wait()
    inject_t = jnp.transpose(inject_ref[...].astype(F32)).astype(BF16)
    low_row = iota((8, 128), 1) < HEAD_DIM
    row = iota((TAIL, 128), 0)
    tails = []
    for half in range(2):
        lanes = slice(half * 128, (half + 1) * 128)
        tail = jnp.zeros((TAIL, 128), F32)
        for s in range(2):
            last = iota((SLEN, 128), 0) == length[s] - 1
            picked = jnp.sum(jnp.where(last, read_ref[s, :, lanes].astype(F32), 0.0), axis=0, keepdims=True)
            tail = jnp.where(row == 2 * core + s, picked, tail)
        tails.append(tail)
    for half in range(2):
        lanes = slice(half * 1024, (half + 1) * 1024)
        wide = jnp.dot(weight, head_lanes(half * 1024, 1024), preferred_element_type=F32)
        copies[2 + half].wait()
        scaled[...] = (values_ref[:, lanes].astype(F32) * wide).astype(BF16)
        state = jnp.dot(inject_t, scaled[...], preferred_element_type=F32).astype(BF16)

        def put(out_ref, half=half, state=state):
            for q in range(8):
                decay = per_pair(total, half * 8 + q, (8, 128), low_row)[0:1]
                for n in range(2):
                    out_ref[2 * q + n, 0:128, :] = state[n * 128 : (n + 1) * 128, q * 128 : (q + 1) * 128]
                    out_ref[2 * q + n, 128:ROWS, :] = with_decay(tails[n], decay).astype(BF16)

        @pl.when(core == half)
        def _(put=put):
            put(keep_ref)

        @pl.when(core != half)
        def _(put=put):
            put(send_ref)


def join_cores_kernel(own_ref, sib_ref, out_ref):
    first = lax.axis_index("core") == 0
    row = iota((TAIL, 128), 0)
    for k in range(16):
        own_tail = own_ref[k, 128:ROWS, :].astype(F32)
        sib_tail = sib_ref[k, 128:ROWS, :].astype(F32)
        own_decay, sib_decay = decay_of(own_tail), decay_of(sib_tail)
        own_weight = jnp.where(first, sib_decay, 1.0)
        sib_weight = jnp.where(first, 1.0, own_decay)
        out_ref[k, 0:128, :] = (
            own_ref[k, 0:128, :].astype(F32) * own_weight + sib_ref[k, 0:128, :].astype(F32) * sib_weight
        ).astype(BF16)
        tail = jnp.where(row < 4, own_tail + sib_tail, 0.0)
        out_ref[k, 128:ROWS, :] = with_decay(tail, own_decay * sib_decay).astype(BF16)


def prefix_kernel(in_ref, out_ref):
    state = jnp.zeros((128, 128), F32)
    for i in range(16):
        out_ref[i, 0:128, :] = state.astype(BF16)
        decay = decay_of(in_ref[i, 128:ROWS, :].astype(F32))
        state = state * decay + in_ref[i, 0:128, :].astype(F32)
    tails = jnp.concatenate([in_ref[i, 128:ROWS, :].astype(F32) for i in range(16)], axis=0).astype(BF16)
    readings = jnp.dot(tails, state.astype(BF16), preferred_element_type=F32)
    for i in range(16):
        out_ref[i, 128:ROWS, :] = readings[TAIL * i : TAIL * (i + 1)].astype(BF16)


def split_cores_kernel(back_ref, own_ref, sib_ref, mine_ref, send_ref):
    first = lax.axis_index("core") == 0
    for k in range(16):
        q, n = k // 2, k % 2
        arrived = back_ref[k, 0:128, :].astype(F32)
        own_decay = decay_of(own_ref[k, 128:ROWS, :].astype(F32))
        sib_decay = decay_of(sib_ref[k, 128:ROWS, :].astype(F32))
        decay = jnp.where(first, own_decay, sib_decay)
        state = jnp.where(first, own_ref[k, 0:128, :].astype(F32), sib_ref[k, 0:128, :].astype(F32))
        second = arrived * decay + state
        mine_ref[n * 128 : (n + 1) * 128, q * 128 : (q + 1) * 128] = jnp.where(first, arrived, second).astype(BF16)
        send_ref[k, 0:128, :] = jnp.where(first, second, arrived).astype(BF16)
        send_ref[k, 128:ROWS, :] = back_ref[k, 128:ROWS, :]
    for q in range(8):
        mine_ref[STATE : STATE + TAIL, q * 128 : (q + 1) * 128] = (
            back_ref[2 * q, 128:ROWS, :].astype(F32) + back_ref[2 * q + 1, 128:ROWS, :].astype(F32)
        ).astype(BF16)


def local_kernel(
    part, step_ref, decay_ref, skip_ref, values_ref, gate_ref, inject_ref, read_ref, *refs
):
    if part == 0:
        scaled_ref, gain_ref, carry, carry_before, ends, weighted, carried, state, before, stepped_all = refs
    else:
        start, start_before, scaled_ref, gain_ref, ends, weighted, carried, state, before, stepped_all = refs

    @pl.when(pl.program_id(0) == 0)
    def _():
        if part == 0:
            state[...] = jnp.zeros_like(state)
            before[...] = jnp.ones_like(before)
        else:
            state[...] = start[...].astype(F32)
            before[...] = start_before[...]

    step = softplus(step_ref[...])
    logs = step * -jnp.exp(column(decay_ref[...]))
    upto = (iota((BLOCK, BLOCK), 0) <= iota((BLOCK, BLOCK), 1)).astype(F32)
    running = jnp.dot(logs, upto, precision=EXACT, preferred_element_type=F32) * LOG2E
    running_t = tokens_first(running)
    parts = jnp.concatenate([*three_parts(step), jnp.zeros((128 - 3 * HEADS, BLOCK), F32)], axis=0)
    stepped_all[...] = values_ref[...].astype(F32) * jnp.dot(
        jnp.transpose(parts).astype(BF16), head_lanes(0, CH), preferred_element_type=F32
    )
    read = read_ref[...]
    inject = inject_ref[...]
    inject_t = jnp.transpose(inject.astype(F32)).astype(BF16)
    scores = jnp.dot(read, inject_t, preferred_element_type=F32)
    carried[...] = jnp.dot(read, state[...].astype(BF16), preferred_element_type=F32)
    causal = iota((BLOCK, BLOCK), 0) >= iota((BLOCK, BLOCK), 1)
    low = iota((BLOCK, 128), 1) < HEAD_DIM
    for pair in range(16):
        lanes = slice(pair * 128, (pair + 1) * 128)
        mixing = []
        spread = []
        for h in (2 * pair, 2 * pair + 1):
            mine = jnp.broadcast_to(running_t[:, h : h + 1], (BLOCK, BLOCK))
            gap = jnp.where(causal, mine - running[h : h + 1, :], -1e30)
            mixing.append((scores * jnp.exp2(gap)).astype(BF16))
            spread.append(mine)
        now = jnp.where(low, spread[0], spread[1])
        grown = jnp.exp2(now)
        values = values_ref[:, lanes].astype(F32)
        stepped = stepped_all[:, lanes]
        diagonal = jnp.concatenate([jnp.where(low, stepped, 0.0), jnp.where(low, 0.0, stepped)], axis=0)
        local = jnp.dot(
            jnp.concatenate(mixing, axis=1), diagonal.astype(BF16), preferred_element_type=F32
        )
        skip = per_pair(skip_ref[...], pair, (1, 128), low[0:1])
        out = local + carried[:, lanes] * grown + skip * values
        gate = gate_ref[:, lanes].astype(F32)
        gate = gate * jax.nn.sigmoid(gate)
        scaled_ref[:, lanes] = (out * gate).astype(BF16)
        gain_ref[:, lanes] = (gate * grown * before[0:1, lanes]).astype(BF16)
        end = now[BLOCK - 1 : BLOCK, :]
        weighted[:, lanes] = (stepped * jnp.exp2(end - now)).astype(BF16)
        ends[0:1, lanes] = jnp.exp2(end)
    state[...] = state[...] * ends[0:1, :] + jnp.dot(inject_t, weighted[...], preferred_element_type=F32)
    before[0:1, :] = before[0:1, :] * ends[0:1, :]
    if part == 0:

        @pl.when(pl.program_id(0) == pl.num_programs(0) - 1)
        def _():
            carry[...] = state[...].astype(BF16)
            carry_before[...] = before[...]


def sample_kernel(
    length, step_ref, decay_ref, skip_ref, values_ref, gate_ref, inject_ref, read_ref, local_ref, grown_ref, gate_out_ref
):
    rate = -jnp.exp(column(decay_ref[...]))
    row = iota((16, CH), 0)
    place = iota((SLEN, 128), 0)
    place_wide = iota((SLEN, STATE), 0)
    narrow = []
    for s in range(2):
        last = length[s] - 1
        step = softplus(step_ref[s])
        logs = step * rate
        pad = jnp.zeros((HEADS, 128 - SLEN), F32)
        step_t = tokens_first(jnp.concatenate([step, pad], axis=1))[0:SLEN]
        logs_t = tokens_first(jnp.concatenate([logs, pad], axis=1))[0:SLEN]
        logs_t = jnp.where(place <= last, logs_t, 0.0)
        gap = jnp.zeros((SLEN, 128), F32)
        for k in range(SLEN):
            gap = gap + jnp.where(place < k, logs_t[k : k + 1], 0.0)
        whole = jnp.sum(logs_t, axis=0, keepdims=True)
        read = jnp.sum(jnp.where(place_wide == last, read_ref[s].astype(F32), 0.0), axis=0, keepdims=True)
        scores = jnp.sum(inject_ref[s].astype(F32) * read, axis=1, keepdims=True)
        narrow.append(jnp.where(place <= last, scores * jnp.exp(gap) * step_t, 0.0))
        narrow.append(jnp.broadcast_to(jnp.exp(whole), (SLEN, 128)))
    skip = jnp.concatenate([skip_ref[...], jnp.zeros((1, 128 - HEADS), F32)], axis=1)
    narrow.append(jnp.broadcast_to(skip, (SLEN, 128)))
    spread = (iota((128, CH), 1) // HEAD_DIM == iota((128, CH), 0)).astype(BF16)
    parts = jnp.concatenate(three_parts(jnp.concatenate(narrow, axis=0)), axis=0).astype(BF16)
    wide = jnp.dot(parts, spread, preferred_element_type=F32)
    wide = wide[0:80] + wide[80:160] + wide[160:240]
    local_all = jnp.zeros((16, CH), F32)
    grown_all = jnp.zeros((16, CH), F32)
    gate_all = jnp.zeros((16, CH), F32)
    for s in range(2):
        values = values_ref[s].astype(F32)
        at_last = iota((SLEN, CH), 0) == length[s] - 1
        picked = jnp.sum(jnp.where(at_last, values, 0.0), axis=0, keepdims=True)
        gate = jnp.sum(jnp.where(at_last, gate_ref[s].astype(F32), 0.0), axis=0, keepdims=True)
        local = jnp.sum(wide[32 * s : 32 * s + SLEN] * values, axis=0, keepdims=True) + wide[64:65] * picked
        local_all = jnp.where(row == s, local, local_all)
        grown_all = jnp.where(row == s, wide[32 * s + SLEN : 32 * s + SLEN + 1], grown_all)
        gate_all = jnp.where(row == s, gate / (1.0 + jnp.exp(-gate)), gate_all)
    local_ref[...] = local_all
    grown_ref[...] = grown_all
    gate_out_ref[...] = gate_all


def normalize(gated, weight):
    mean = jnp.sum(gated * gated, axis=1, keepdims=True) * (1.0 / CH)
    return (gated * lax.rsqrt(mean + 1e-05) * weight).astype(BF16)


FIRST = ((1, 0), (2, 0), (3, 1), (2, 1))
REST = ((3, 0), (1, 1), (0, 0), (0, 1))


def column_copies(pieces, weight_ref, held, sems):
    z = lax.axis_index("head")
    copies = []
    for i, (flip, half) in enumerate(pieces):
        at = pl.multiple_of(((z ^ flip) * 2 + half) * PIECE, PIECE)
        copies.append(pltpu.make_async_copy(weight_ref.at[:, pl.ds(at, PIECE)], held.at[i], sems.at[i]))
    return copies


def fetch_kernel(pieces, weight_ref, *refs):
    extra = (len(refs) - 2) // 2
    extra_refs, (out_ref, *extra_outs, sems) = refs[:extra], refs[extra:]
    copies = column_copies(pieces, weight_ref, out_ref, sems)
    for i, (src, dst) in enumerate(zip(extra_refs, extra_outs)):
        copies.append(pltpu.make_async_copy(src, dst, sems.at[len(pieces) + i]))
    for copy in copies:
        copy.start()
    for copy in copies:
        copy.wait()


def resident(x):
    return pltpu.with_memory_space_constraint(x, pltpu.VMEM)


def fetch(pieces, weight, *extra):
    held = pltpu.VMEM((len(pieces), CH, PIECE), BF16)
    out = pl.pallas_call(
        functools.partial(fetch_kernel, pieces),
        out_shape=(held, *(pltpu.VMEM(x.shape, x.dtype) for x in extra)),
        in_specs=[pl.BlockSpec(memory_space=pl.ANY)] * (1 + len(extra)),
        out_specs=(VMEM,) * (1 + len(extra)),
        scratch_shapes=[pltpu.SemaphoreType.DMA((len(pieces) + len(extra),))],
        compiler_params=pltpu.CompilerParams(vmem_limit_bytes=12 << 20),
        name="fetch_weight",
    )(*in_hbm(weight, *extra))
    return tuple(resident(x) for x in out)


def project(normed, columns, outs):
    for column, (ref, k) in zip(columns, outs):
        ref[k] = jnp.dot(normed[...], column[...], preferred_element_type=F32).astype(BF16)


HERE = tuple(slice(start % HALF, start % HALF + rows) for start, rows in CHUNKS)


def arriving(place, state_ref, read_ref):
    start, rows = CHUNKS[place]
    return jnp.dot(read_ref[start : start + rows, :], state_ref[0:STATE, :], preferred_element_type=F32)


def join_halves_kernel(mine_ref, theirs_ref, state_ref):
    core = lax.axis_index("core")
    state_ref[:, pl.ds(pl.multiple_of(core * 1024, 1024), 1024)] = mine_ref[...]
    for q in range(8):
        lanes = pl.ds(pl.multiple_of((1 - core) * 1024 + q * 128, 128), 128)
        for n in range(2):
            state_ref[n * 128 : (n + 1) * 128, lanes] = theirs_ref[2 * q + n, 0:128, :]
        state_ref[STATE : STATE + TAIL, lanes] = (
            theirs_ref[2 * q, 128:ROWS, :].astype(F32) + theirs_ref[2 * q + 1, 128:ROWS, :].astype(F32)
        ).astype(BF16)


def chunk_kernel(place, sampled, state_ref, read_ref, scaled_ref, gain_ref, norm_ref, near_ref, far_ref, *refs):
    if place == LEADING:
        *sample, first_ref, second_ref, normed_ref, held, sems = refs
        copies = column_copies(FIRST[1:], far_ref, held, sems)
        copies[0].start()
    else:
        *sample, first_ref, second_ref, normed_ref = refs
        held = far_ref
    arrived = arriving(place, state_ref, read_ref)
    if place == LEADING:
        copies[1].start()
    gated = scaled_ref[HERE[place], :].astype(F32) + arrived * gain_ref[HERE[place], :].astype(F32)
    normed_ref[0 : CHUNKS[place][1], :] = normalize(gated, norm_ref[...])
    if place == LEADING:
        copies[2].start()
    if sampled:
        local_ref, grown_ref, gate_ref = sample
        readings = state_ref[STATE : STATE + TAIL, :].astype(F32)
        moved = jnp.concatenate([readings[2:TAIL], readings[0:2]], axis=0)
        readings = jnp.where(lax.axis_index("core") == 0, readings, moved)
        readings = jnp.concatenate([readings, jnp.zeros((16 - TAIL, CH), F32)], axis=0)
        sampled = (local_ref[...] + readings * grown_ref[...]) * gate_ref[...]
        rows = CHUNKS[place][1]
        normed_ref[rows : rows + 16, :] = normalize(sampled, norm_ref[...])
    project(normed_ref, (near_ref.at[0],), ((first_ref, 0),))
    for i, out in enumerate(((first_ref, 1), (second_ref, 0), (second_ref, 1))):
        if place == LEADING:
            copies[i].wait()
        project(normed_ref, (held.at[i],), (out,))


def rest_kernel(normed_ref, weight_ref, rest_ref):
    project(normed_ref, [weight_ref.at[i] for i in range(4)], ((rest_ref, 1), (rest_ref, 3), (rest_ref, 0), (rest_ref, 2)))


def onward_kernel(a_ref, b_ref, rest_ref, a_out, b_out):
    a_out[...] = (rest_ref[1].astype(F32) + a_ref[1].astype(F32)).astype(BF16)
    b_out[...] = (rest_ref[3].astype(F32) + b_ref[1].astype(F32)).astype(BF16)


def own_sum_kernel(a_ref, b_ref, rest_ref, out_ref):
    out_ref[0] = rest_ref[0].astype(F32) + a_ref[0].astype(F32)
    out_ref[1] = rest_ref[2].astype(F32) + b_ref[0].astype(F32)


def finish_kernel(*refs):
    ins, out_ref, sample_ref = refs[:-2], refs[-2], refs[-1]
    for place, (start, rows) in enumerate(CHUNKS):
        own, *far = ins[3 * place : 3 * place + 3]
        for half in range(2):
            total = own[half] + far[half][...].astype(F32)
            columns = slice(half * PIECE, (half + 1) * PIECE)
            out_ref[columns, start : start + rows] = jnp.transpose(total[0:rows]).astype(BF16)
            if place == LEADING:
                sample_ref[:, columns] = total[rows : rows + 2].astype(BF16)


def in_hbm(*arrays):
    return tuple(pltpu.with_memory_space_constraint(x, pltpu.HBM) for x in arrays)


def call(kernel, name, out_shape, inputs, limit, scalars=0, **more):
    return pl.pallas_call(
        kernel,
        out_shape=out_shape,
        in_specs=[SMEM] * scalars + [VMEM] * (len(inputs) - scalars),
        out_specs=jax.tree.map(lambda _: VMEM, out_shape, is_leaf=lambda x: not isinstance(x, tuple)),
        compiler_params=pltpu.CompilerParams(vmem_limit_bytes=limit << 20),
        cost_estimate=pl.CostEstimate(flops=1, bytes_accessed=1, transcendentals=0),
        name=name,
        **more,
    )(*inputs)


SMEM = pl.BlockSpec(memory_space=pltpu.SMEM)
VMEM = pl.BlockSpec(memory_space=pltpu.VMEM)


def shape(dims, dtype=BF16):
    return jax.ShapeDtypeStruct(dims, dtype)


def swap(x, step):
    return lax.ppermute(x, "head", [(i, i ^ step) for i in range(4)])


def other_core(x):
    return lax.ppermute(x, "core", [(0, 1), (1, 0)])


def local_outputs(part, step, decay, skip, values, gate, inject, read, start=()):
    blocks = TOK // BLOCK // 2
    row = lambda width: pl.BlockSpec((1, width), lambda b: (0, 0))
    tokens = lambda width: pl.BlockSpec((BLOCK, width), lambda b: (b + part * blocks, 0))
    out = pl.BlockSpec((BLOCK, CH), lambda b: (b, 0))
    whole = lambda rows: pl.BlockSpec((rows, CH), lambda b: (0, 0))
    carry = (pltpu.HBM((STATE, CH), BF16), pltpu.HBM((8, CH), F32))
    results = (pltpu.HBM((TOK // 2, CH), BF16),) * 2
    scratch = [
        pltpu.VMEM((8, CH), F32), pltpu.VMEM((BLOCK, CH), BF16), pltpu.VMEM((BLOCK, CH), F32),
        pltpu.VMEM((STATE, CH), F32), pltpu.VMEM((8, CH), F32), pltpu.VMEM((BLOCK, CH), F32),
    ]
    if start:
        start_specs = [whole(STATE), whole(8)]
        out_specs = (out, out)
    else:
        start_specs = []
        results += carry
        out_specs = (out, out, whole(STATE), whole(8))
    step, values, gate, inject, read, *start = in_hbm(step, values, gate, inject, read, *start)
    return pl.pallas_call(
        functools.partial(local_kernel, part),
        grid=(blocks,),
        out_shape=results,
        in_specs=[
            pl.BlockSpec((HEADS, BLOCK), lambda b: (0, b + part * blocks)), row(HEADS), row(HEADS),
            tokens(CH), tokens(CH), tokens(STATE), tokens(STATE), *start_specs,
        ],
        out_specs=out_specs,
        scratch_shapes=scratch,
        compiler_params=pltpu.CompilerParams(vmem_limit_bytes=20 << 20),
        cost_estimate=pl.CostEstimate(flops=3 << 30, bytes_accessed=20 << 20, transcendentals=2 << 20),
        name="local_outputs",
    )(step, decay, skip, values, gate, inject, read, *start)


def per_device(
    prompt_values, prompt_gate, prompt_inject, prompt_read, prompt_step, decay_log, skip_gain, norm_weight, out_weight,
    sample_values, sample_gate, sample_inject, sample_read, sample_step, sample_length,
):
    inject = prompt_inject.reshape(TOK, STATE)
    read = prompt_read.reshape(TOK, STATE)
    decay = decay_log.reshape(1, HEADS)
    skip = skip_gain.reshape(1, HEADS)
    norm = norm_weight.reshape(1, CH)
    s_read = sample_read.reshape(2, SLEN, STATE)
    s_inject = sample_inject.reshape(2, SLEN, STATE)
    slices_shape = shape((16, ROWS, 128))

    anywhere = pl.BlockSpec(memory_space=pl.ANY)
    keep, send = pl.pallas_call(
        end_state_kernel,
        out_shape=(slices_shape,) * 2,
        in_specs=[SMEM, anywhere, VMEM, anywhere, anywhere, VMEM],
        out_specs=(VMEM, VMEM),
        scratch_shapes=[
            pltpu.VMEM((TOK, 1024), BF16), pltpu.VMEM((HEADS, TOK), F32), pltpu.VMEM((TOK, CH), BF16),
            pltpu.VMEM((TOK, STATE), BF16), pltpu.SemaphoreType.DMA((4,)),
        ],
        compiler_params=pltpu.CompilerParams(vmem_limit_bytes=24 << 20),
        name="end_state",
    )(*in_hbm(sample_length, prompt_step, decay, prompt_values, inject, s_read))
    sibling = other_core(send)
    joined = call(join_cores_kernel, "join_cores", slices_shape, (keep, sibling), 16)
    joined, step_1, s_step = lax.optimization_barrier((joined, prompt_step, sample_step.transpose(1, 0, 2)))
    slices = lax.all_to_all(joined, ("y", "x"), 0, 0, tiled=True)
    scaled_1, gain_1, *carry = local_outputs(
        0, step_1, decay, skip, prompt_values, prompt_gate, inject, read
    )
    sample = call(
        sample_kernel, "sample_outputs", (pltpu.HBM((16, CH), F32),) * 3,
        (sample_length, *in_hbm(s_step, decay, skip, sample_values, sample_gate, s_inject, s_read)), 16, 1,
    )
    slices, scaled_1, sample = lax.optimization_barrier((slices, scaled_1, sample))
    prefix = call(prefix_kernel, "prefix", slices_shape, (slices,), 16)
    prefix, step_2 = lax.optimization_barrier((prefix, prompt_step))
    back = lax.all_to_all(prefix, ("y", "x"), 0, 0, tiled=True)
    scaled_2, gain_2 = local_outputs(
        1, step_2, decay, skip, prompt_values, prompt_gate, inject, read, carry
    )
    back, scaled_2, weight = lax.optimization_barrier((back, scaled_2, out_weight))
    mine, send = call(
        split_cores_kernel, "split_cores", (shape((STATE + TAIL, 1024)), slices_shape), (back, keep, sibling), 16
    )
    theirs = other_core(send)

    near_columns, scaled_2, gain_2 = fetch(FIRST[:1], weight, scaled_2, gain_2)
    scaled = (scaled_1, scaled_2)
    gain = (gain_1, gain_2)
    state = call(join_halves_kernel, "join_halves", shape((STATE + TAIL, CH)), (mine, theirs), 8)

    def chunk(place, far_columns, *sample):
        start, rows = CHUNKS[place]
        size = rows + (16 if sample else 0)
        leading = place == LEADING
        local = (scaled[start // HALF], gain[start // HALF])
        local = local if leading else in_hbm(*local)
        piece = shape((2, size, PIECE))
        held = pltpu.VMEM((3, CH, PIECE), BF16)
        first, second, normed, *held = pl.pallas_call(
            functools.partial(chunk_kernel, place, bool(sample)),
            out_shape=(piece, piece, shape((size, CH)), *([held] if leading else [])),
            in_specs=[VMEM] * 6 + [anywhere if leading else VMEM] + [VMEM] * len(sample),
            out_specs=(VMEM,) * (4 if leading else 3),
            scratch_shapes=[pltpu.SemaphoreType.DMA((3,))] if leading else [],
            compiler_params=pltpu.CompilerParams(vmem_limit_bytes=24 << 20),
            name="chunk",
        )(state, read, *local, norm, near_columns, far_columns, *sample)
        near = lax.optimization_barrier((swap(first, 1), swap(second, 3)))
        return normed, near, *held

    normed_0, near_0, far_columns = chunk(0, *in_hbm(weight), *sample)
    (rest_columns,) = fetch(REST, weight)
    normed_1, near_1 = chunk(1, resident(far_columns))
    rest_0, rest_1 = (
        call(rest_kernel, "rest", shape((4, normed.shape[0], PIECE)), (normed, rest_columns), 24)
        for normed in (normed_0, normed_1)
    )

    def onward(near, rest):
        return call(onward_kernel, "onward", (shape(near[0].shape[1:]),) * 2, (*near, rest), 8)

    def send_on(ons):
        return lax.optimization_barrier((swap(ons[0], 3), swap(ons[1], 1)))

    def own_sum(near, rest):
        return call(own_sum_kernel, "own_sum", shape((2, *near[0].shape[1:]), F32), (*near, rest), 8)

    ons_0, own_0, rest_1 = lax.optimization_barrier((onward(near_0, rest_0), own_sum(near_0, rest_0), rest_1))
    far_0 = send_on(ons_0)
    far_1 = send_on(onward(near_1, rest_1))
    parts = (own_0, *far_0, own_sum(near_1, rest_1), *far_1)
    prompt_mixed, sample_mixed = call(finish_kernel, "finish", (shape((1024, TOK)), shape((2, 1024))), parts, 16)
    return prompt_mixed, sample_mixed.T


def solution(mesh):
    split = Mesh(mesh.devices.reshape(4, 4, 2, mesh.shape["head"]), ("y", "x", "core", "head"))
    return jax.shard_map(
        per_device,
        mesh=split,
        in_specs=(
            P(CTX, "head"), P(CTX, "head"), P(CTX, "head", None), P(CTX, "head", None), P("head", CTX),
            P("head"), P("head"), P("head"), P("head", None),
            P(CTX, None, "head"), P(CTX, None, "head"), P(CTX, None, "head", None), P(CTX, None, "head", None),
            P("head", CTX, None), P(CTX),
        ),
        out_specs=(P("head", CTX), P("head", CTX)),
        check_vma=False,
    )
```

```python
import functools

import jax
import jax.numpy as jnp
from jax import lax
from jax.experimental import pallas as pl
from jax.experimental.pallas import tpu as pltpu
from jax.sharding import Mesh
from jax.sharding import PartitionSpec as P

HEADS = 32
HEAD_DIM = 64
STATE = 256
BLOCK = 128
SLEN = 16
TOK = 512
CH = HEADS * HEAD_DIM
PIECE = 512
HALF = TOK // 2
TAIL = 8
ROWS = 128 + TAIL
CTX = ("y", "x", "core")
F32 = jnp.float32
BF16 = jnp.bfloat16
EXACT = lax.Precision.HIGHEST
LOG2E = 1.4426950408889634
CHUNKS = ((256, 256), (0, 256))
LEADING = 0


def softplus(v):
    return jnp.maximum(v, 0.0) + jnp.log1p(jnp.exp(-jnp.abs(v)))


def iota(shape, dim):
    return lax.broadcasted_iota(jnp.int32, shape, dim)


def column(row):
    n = row.shape[1]
    square = jnp.broadcast_to(row, (n, n))
    return jnp.sum(jnp.where(iota((n, n), 0) == iota((n, n), 1), square, 0.0), axis=1, keepdims=True)


def tokens_first(x):
    pad = jnp.zeros((128 - x.shape[0], x.shape[1]), F32)
    return jnp.transpose(jnp.concatenate([x, pad], axis=0))


def per_pair(columns, pair, shape, low):
    first = jnp.broadcast_to(columns[:, 2 * pair : 2 * pair + 1], shape)
    second = jnp.broadcast_to(columns[:, 2 * pair + 1 : 2 * pair + 2], shape)
    return jnp.where(low, first, second)


def head_lanes(start, width):
    row, lane = iota((128, width), 0), iota((128, width), 1) + start
    return (((row & (HEADS - 1)) == (lane >> 6)) & (row < 3 * HEADS)).astype(BF16)


def three_parts(x):
    hi = x.astype(BF16).astype(F32)
    mid = (x - hi).astype(BF16).astype(F32)
    lo = (x - hi - mid).astype(BF16).astype(F32)
    return hi, mid, lo


def decay_of(tail):
    return tail[4:5] + tail[5:6] + tail[6:7]


def with_decay(tail, decay):
    row = iota((TAIL, 128), 0)
    for i, part in enumerate(three_parts(decay)):
        tail = jnp.where(row == 4 + i, part, tail)
    return tail


def end_state_kernel(
    length, step_any, decay_ref, values_any, inject_any, read_ref, keep_ref, send_ref,
    scaled, step_ref, values_ref, inject_ref, sems,
):
    copies = [
        pltpu.make_async_copy(step_any, step_ref, sems.at[0]),
        pltpu.make_async_copy(inject_any, inject_ref, sems.at[1]),
    ]
    for half in range(2):
        lanes = slice(half * 1024, (half + 1) * 1024)
        copies.append(pltpu.make_async_copy(values_any.at[:, lanes], values_ref.at[:, lanes], sems.at[2 + half]))
    for copy in copies:
        copy.start()
    copies[0].wait()
    core = lax.axis_index("core")
    step = softplus(step_ref[...])
    logs = step * -jnp.exp(column(decay_ref[...]))
    later = (iota((BLOCK, BLOCK), 0) > iota((BLOCK, BLOCK), 1)).astype(F32)
    after = jnp.zeros((HEADS, 1), F32)
    parts = []
    for b in reversed(range(TOK // BLOCK)):
        here = logs[:, b * BLOCK : (b + 1) * BLOCK]
        parts.append(jnp.dot(here, later, precision=EXACT, preferred_element_type=F32) + after)
        after = after + jnp.sum(here, axis=1, keepdims=True)
    weight = jnp.exp(jnp.concatenate(parts[::-1], axis=1)) * step
    weight = jnp.transpose(jnp.concatenate([*three_parts(weight), jnp.zeros((128 - 3 * HEADS, TOK), F32)], axis=0))
    weight = weight.astype(BF16)
    total = tokens_first(jnp.broadcast_to(jnp.exp(after), (HEADS, 128)))[0:8]
    copies[1].wait()
    inject_t = jnp.transpose(inject_ref[...].astype(F32)).astype(BF16)
    low_row = iota((8, 128), 1) < HEAD_DIM
    row = iota((TAIL, 128), 0)
    tails = []
    for half in range(2):
        lanes = slice(half * 128, (half + 1) * 128)
        tail = jnp.zeros((TAIL, 128), F32)
        for s in range(2):
            last = iota((SLEN, 128), 0) == length[s] - 1
            picked = jnp.sum(jnp.where(last, read_ref[s, :, lanes].astype(F32), 0.0), axis=0, keepdims=True)
            tail = jnp.where(row == 2 * core + s, picked, tail)
        tails.append(tail)
    for half in range(2):
        lanes = slice(half * 1024, (half + 1) * 1024)
        wide = jnp.dot(weight, head_lanes(half * 1024, 1024), preferred_element_type=F32)
        copies[2 + half].wait()
        scaled[...] = (values_ref[:, lanes].astype(F32) * wide).astype(BF16)
        state = jnp.dot(inject_t, scaled[...], preferred_element_type=F32).astype(BF16)

        def put(out_ref, half=half, state=state):
            for q in range(8):
                decay = per_pair(total, half * 8 + q, (8, 128), low_row)[0:1]
                for n in range(2):
                    out_ref[2 * q + n, 0:128, :] = state[n * 128 : (n + 1) * 128, q * 128 : (q + 1) * 128]
                    out_ref[2 * q + n, 128:ROWS, :] = with_decay(tails[n], decay).astype(BF16)

        @pl.when(core == half)
        def _(put=put):
            put(keep_ref)

        @pl.when(core != half)
        def _(put=put):
            put(send_ref)


def join_cores_kernel(own_ref, sib_ref, out_ref):
    first = lax.axis_index("core") == 0
    row = iota((TAIL, 128), 0)
    for k in range(16):
        own_tail = own_ref[k, 128:ROWS, :].astype(F32)
        sib_tail = sib_ref[k, 128:ROWS, :].astype(F32)
        own_decay, sib_decay = decay_of(own_tail), decay_of(sib_tail)
        own_weight = jnp.where(first, sib_decay, 1.0)
        sib_weight = jnp.where(first, 1.0, own_decay)
        out_ref[k, 0:128, :] = (
            own_ref[k, 0:128, :].astype(F32) * own_weight + sib_ref[k, 0:128, :].astype(F32) * sib_weight
        ).astype(BF16)
        tail = jnp.where(row < 4, own_tail + sib_tail, 0.0)
        out_ref[k, 128:ROWS, :] = with_decay(tail, own_decay * sib_decay).astype(BF16)


def prefix_kernel(in_ref, out_ref):
    state = jnp.zeros((128, 128), F32)
    for i in range(16):
        out_ref[i, 0:128, :] = state.astype(BF16)
        decay = decay_of(in_ref[i, 128:ROWS, :].astype(F32))
        state = state * decay + in_ref[i, 0:128, :].astype(F32)
    tails = jnp.concatenate([in_ref[i, 128:ROWS, :].astype(F32) for i in range(16)], axis=0).astype(BF16)
    readings = jnp.dot(tails, state.astype(BF16), preferred_element_type=F32)
    for i in range(16):
        out_ref[i, 128:ROWS, :] = readings[TAIL * i : TAIL * (i + 1)].astype(BF16)


def split_cores_kernel(back_ref, own_ref, sib_ref, mine_ref, send_ref):
    first = lax.axis_index("core") == 0
    for k in range(16):
        q, n = k // 2, k % 2
        arrived = back_ref[k, 0:128, :].astype(F32)
        own_decay = decay_of(own_ref[k, 128:ROWS, :].astype(F32))
        sib_decay = decay_of(sib_ref[k, 128:ROWS, :].astype(F32))
        decay = jnp.where(first, own_decay, sib_decay)
        state = jnp.where(first, own_ref[k, 0:128, :].astype(F32), sib_ref[k, 0:128, :].astype(F32))
        second = arrived * decay + state
        mine_ref[n * 128 : (n + 1) * 128, q * 128 : (q + 1) * 128] = jnp.where(first, arrived, second).astype(BF16)
        send_ref[k, 0:128, :] = jnp.where(first, second, arrived).astype(BF16)
        send_ref[k, 128:ROWS, :] = back_ref[k, 128:ROWS, :]
    for q in range(8):
        mine_ref[STATE : STATE + TAIL, q * 128 : (q + 1) * 128] = (
            back_ref[2 * q, 128:ROWS, :].astype(F32) + back_ref[2 * q + 1, 128:ROWS, :].astype(F32)
        ).astype(BF16)


def local_kernel(
    part, step_ref, decay_ref, skip_ref, values_ref, gate_ref, inject_ref, read_ref, *refs
):
    if part == 0:
        scaled_ref, gain_ref, carry, carry_before, ends, weighted, carried, state, before, stepped_all = refs
    else:
        start, start_before, scaled_ref, gain_ref, ends, weighted, carried, state, before, stepped_all = refs

    @pl.when(pl.program_id(0) == 0)
    def _():
        if part == 0:
            state[...] = jnp.zeros_like(state)
            before[...] = jnp.ones_like(before)
        else:
            state[...] = start[...].astype(F32)
            before[...] = start_before[...]

    step = softplus(step_ref[...])
    logs = step * -jnp.exp(column(decay_ref[...]))
    upto = (iota((BLOCK, BLOCK), 0) <= iota((BLOCK, BLOCK), 1)).astype(F32)
    running = jnp.dot(logs, upto, precision=EXACT, preferred_element_type=F32) * LOG2E
    running_t = tokens_first(running)
    parts = jnp.concatenate([*three_parts(step), jnp.zeros((128 - 3 * HEADS, BLOCK), F32)], axis=0)
    stepped_all[...] = values_ref[...].astype(F32) * jnp.dot(
        jnp.transpose(parts).astype(BF16), head_lanes(0, CH), preferred_element_type=F32
    )
    read = read_ref[...]
    inject = inject_ref[...]
    inject_t = jnp.transpose(inject.astype(F32)).astype(BF16)
    scores = jnp.dot(read, inject_t, preferred_element_type=F32)
    carried[...] = jnp.dot(read, state[...].astype(BF16), preferred_element_type=F32)
    causal = iota((BLOCK, BLOCK), 0) >= iota((BLOCK, BLOCK), 1)
    low = iota((BLOCK, 128), 1) < HEAD_DIM
    for pair in range(16):
        lanes = slice(pair * 128, (pair + 1) * 128)
        mixing = []
        spread = []
        for h in (2 * pair, 2 * pair + 1):
            mine = jnp.broadcast_to(running_t[:, h : h + 1], (BLOCK, BLOCK))
            gap = jnp.where(causal, mine - running[h : h + 1, :], -1e30)
            mixing.append((scores * jnp.exp2(gap)).astype(BF16))
            spread.append(mine)
        now = jnp.where(low, spread[0], spread[1])
        grown = jnp.exp2(now)
        values = values_ref[:, lanes].astype(F32)
        stepped = stepped_all[:, lanes]
        diagonal = jnp.concatenate([jnp.where(low, stepped, 0.0), jnp.where(low, 0.0, stepped)], axis=0)
        local = jnp.dot(
            jnp.concatenate(mixing, axis=1), diagonal.astype(BF16), preferred_element_type=F32
        )
        skip = per_pair(skip_ref[...], pair, (1, 128), low[0:1])
        out = local + carried[:, lanes] * grown + skip * values
        gate = gate_ref[:, lanes].astype(F32)
        gate = gate * jax.nn.sigmoid(gate)
        scaled_ref[:, lanes] = (out * gate).astype(BF16)
        gain_ref[:, lanes] = (gate * grown * before[0:1, lanes]).astype(BF16)
        end = now[BLOCK - 1 : BLOCK, :]
        weighted[:, lanes] = (stepped * jnp.exp2(end - now)).astype(BF16)
        ends[0:1, lanes] = jnp.exp2(end)
    state[...] = state[...] * ends[0:1, :] + jnp.dot(inject_t, weighted[...], preferred_element_type=F32)
    before[0:1, :] = before[0:1, :] * ends[0:1, :]
    if part == 0:

        @pl.when(pl.program_id(0) == pl.num_programs(0) - 1)
        def _():
            carry[...] = state[...].astype(BF16)
            carry_before[...] = before[...]


def sample_kernel(
    length, step_ref, decay_ref, skip_ref, values_ref, gate_ref, inject_ref, read_ref, local_ref, grown_ref, gate_out_ref
):
    rate = -jnp.exp(column(decay_ref[...]))
    row = iota((16, CH), 0)
    place = iota((SLEN, 128), 0)
    place_wide = iota((SLEN, STATE), 0)
    narrow = []
    for s in range(2):
        last = length[s] - 1
        step = softplus(step_ref[s])
        logs = step * rate
        pad = jnp.zeros((HEADS, 128 - SLEN), F32)
        step_t = tokens_first(jnp.concatenate([step, pad], axis=1))[0:SLEN]
        logs_t = tokens_first(jnp.concatenate([logs, pad], axis=1))[0:SLEN]
        logs_t = jnp.where(place <= last, logs_t, 0.0)
        gap = jnp.zeros((SLEN, 128), F32)
        for k in range(SLEN):
            gap = gap + jnp.where(place < k, logs_t[k : k + 1], 0.0)
        whole = jnp.sum(logs_t, axis=0, keepdims=True)
        read = jnp.sum(jnp.where(place_wide == last, read_ref[s].astype(F32), 0.0), axis=0, keepdims=True)
        scores = jnp.sum(inject_ref[s].astype(F32) * read, axis=1, keepdims=True)
        narrow.append(jnp.where(place <= last, scores * jnp.exp(gap) * step_t, 0.0))
        narrow.append(jnp.broadcast_to(jnp.exp(whole), (SLEN, 128)))
    skip = jnp.concatenate([skip_ref[...], jnp.zeros((1, 128 - HEADS), F32)], axis=1)
    narrow.append(jnp.broadcast_to(skip, (SLEN, 128)))
    spread = (iota((128, CH), 1) // HEAD_DIM == iota((128, CH), 0)).astype(BF16)
    parts = jnp.concatenate(three_parts(jnp.concatenate(narrow, axis=0)), axis=0).astype(BF16)
    wide = jnp.dot(parts, spread, preferred_element_type=F32)
    wide = wide[0:80] + wide[80:160] + wide[160:240]
    local_all = jnp.zeros((16, CH), F32)
    grown_all = jnp.zeros((16, CH), F32)
    gate_all = jnp.zeros((16, CH), F32)
    for s in range(2):
        values = values_ref[s].astype(F32)
        at_last = iota((SLEN, CH), 0) == length[s] - 1
        picked = jnp.sum(jnp.where(at_last, values, 0.0), axis=0, keepdims=True)
        gate = jnp.sum(jnp.where(at_last, gate_ref[s].astype(F32), 0.0), axis=0, keepdims=True)
        local = jnp.sum(wide[32 * s : 32 * s + SLEN] * values, axis=0, keepdims=True) + wide[64:65] * picked
        local_all = jnp.where(row == s, local, local_all)
        grown_all = jnp.where(row == s, wide[32 * s + SLEN : 32 * s + SLEN + 1], grown_all)
        gate_all = jnp.where(row == s, gate / (1.0 + jnp.exp(-gate)), gate_all)
    local_ref[...] = local_all
    grown_ref[...] = grown_all
    gate_out_ref[...] = gate_all


def normalize(gated, weight):
    mean = jnp.sum(gated * gated, axis=1, keepdims=True) * (1.0 / CH)
    return (gated * lax.rsqrt(mean + 1e-05) * weight).astype(BF16)


FIRST = ((1, 0), (2, 0), (3, 1), (2, 1))
REST = ((3, 0), (1, 1), (0, 0), (0, 1))


def column_copies(pieces, weight_ref, held, sems):
    z = lax.axis_index("head")
    copies = []
    for i, (flip, half) in enumerate(pieces):
        at = pl.multiple_of(((z ^ flip) * 2 + half) * PIECE, PIECE)
        copies.append(pltpu.make_async_copy(weight_ref.at[:, pl.ds(at, PIECE)], held.at[i], sems.at[i]))
    return copies


def fetch_kernel(pieces, weight_ref, *refs):
    extra = (len(refs) - 2) // 2
    extra_refs, (out_ref, *extra_outs, sems) = refs[:extra], refs[extra:]
    copies = column_copies(pieces, weight_ref, out_ref, sems)
    for i, (src, dst) in enumerate(zip(extra_refs, extra_outs)):
        copies.append(pltpu.make_async_copy(src, dst, sems.at[len(pieces) + i]))
    for copy in copies:
        copy.start()
    for copy in copies:
        copy.wait()


def resident(x):
    return pltpu.with_memory_space_constraint(x, pltpu.VMEM)


def fetch(pieces, weight, *extra):
    held = pltpu.VMEM((len(pieces), CH, PIECE), BF16)
    out = pl.pallas_call(
        functools.partial(fetch_kernel, pieces),
        out_shape=(held, *(pltpu.VMEM(x.shape, x.dtype) for x in extra)),
        in_specs=[pl.BlockSpec(memory_space=pl.ANY)] * (1 + len(extra)),
        out_specs=(VMEM,) * (1 + len(extra)),
        scratch_shapes=[pltpu.SemaphoreType.DMA((len(pieces) + len(extra),))],
        compiler_params=pltpu.CompilerParams(vmem_limit_bytes=12 << 20),
        name="fetch_weight",
    )(*in_hbm(weight, *extra))
    return tuple(resident(x) for x in out)


def project(normed, columns, outs):
    for column, (ref, k) in zip(columns, outs):
        ref[k] = jnp.dot(normed[...], column[...], preferred_element_type=F32).astype(BF16)


HERE = tuple(slice(start % HALF, start % HALF + rows) for start, rows in CHUNKS)


def arriving(place, state_ref, read_ref):
    start, rows = CHUNKS[place]
    return jnp.dot(read_ref[start : start + rows, :], state_ref[0:STATE, :], preferred_element_type=F32)


def join_halves_kernel(mine_ref, theirs_ref, state_ref):
    core = lax.axis_index("core")
    state_ref[:, pl.ds(pl.multiple_of(core * 1024, 1024), 1024)] = mine_ref[...]
    for q in range(8):
        lanes = pl.ds(pl.multiple_of((1 - core) * 1024 + q * 128, 128), 128)
        for n in range(2):
            state_ref[n * 128 : (n + 1) * 128, lanes] = theirs_ref[2 * q + n, 0:128, :]
        state_ref[STATE : STATE + TAIL, lanes] = (
            theirs_ref[2 * q, 128:ROWS, :].astype(F32) + theirs_ref[2 * q + 1, 128:ROWS, :].astype(F32)
        ).astype(BF16)


def chunk_kernel(place, sampled, state_ref, read_ref, scaled_ref, gain_ref, norm_ref, near_ref, far_ref, *refs):
    if place == LEADING:
        *sample, first_ref, second_ref, normed_ref, held, sems = refs
        copies = column_copies(FIRST[1:], far_ref, held, sems)
        copies[0].start()
    else:
        *sample, first_ref, second_ref, normed_ref = refs
        held = far_ref
    arrived = arriving(place, state_ref, read_ref)
    if place == LEADING:
        copies[1].start()
    gated = scaled_ref[HERE[place], :].astype(F32) + arrived * gain_ref[HERE[place], :].astype(F32)
    normed_ref[0 : CHUNKS[place][1], :] = normalize(gated, norm_ref[...])
    if place == LEADING:
        copies[2].start()
    if sampled:
        local_ref, grown_ref, gate_ref = sample
        readings = state_ref[STATE : STATE + TAIL, :].astype(F32)
        moved = jnp.concatenate([readings[2:TAIL], readings[0:2]], axis=0)
        readings = jnp.where(lax.axis_index("core") == 0, readings, moved)
        readings = jnp.concatenate([readings, jnp.zeros((16 - TAIL, CH), F32)], axis=0)
        sampled = (local_ref[...] + readings * grown_ref[...]) * gate_ref[...]
        rows = CHUNKS[place][1]
        normed_ref[rows : rows + 16, :] = normalize(sampled, norm_ref[...])
    project(normed_ref, (near_ref.at[0],), ((first_ref, 0),))
    for i, out in enumerate(((first_ref, 1), (second_ref, 0), (second_ref, 1))):
        if place == LEADING:
            copies[i].wait()
        project(normed_ref, (held.at[i],), (out,))


def rest_kernel(normed_ref, weight_ref, rest_ref):
    project(normed_ref, [weight_ref.at[i] for i in range(4)], ((rest_ref, 1), (rest_ref, 3), (rest_ref, 0), (rest_ref, 2)))


def onward_kernel(a_ref, b_ref, rest_ref, a_out, b_out):
    a_out[...] = (rest_ref[1].astype(F32) + a_ref[1].astype(F32)).astype(BF16)
    b_out[...] = (rest_ref[3].astype(F32) + b_ref[1].astype(F32)).astype(BF16)


def own_sum_kernel(a_ref, b_ref, rest_ref, out_ref):
    out_ref[0] = rest_ref[0].astype(F32) + a_ref[0].astype(F32)
    out_ref[1] = rest_ref[2].astype(F32) + b_ref[0].astype(F32)


def finish_kernel(*refs):
    ins, out_ref, sample_ref = refs[:-2], refs[-2], refs[-1]
    for place, (start, rows) in enumerate(CHUNKS):
        own, *far = ins[3 * place : 3 * place + 3]
        for half in range(2):
            total = own[half] + far[half][...].astype(F32)
            columns = slice(half * PIECE, (half + 1) * PIECE)
            out_ref[columns, start : start + rows] = jnp.transpose(total[0:rows]).astype(BF16)
            if place == LEADING:
                sample_ref[:, columns] = total[rows : rows + 2].astype(BF16)


def in_hbm(*arrays):
    return tuple(pltpu.with_memory_space_constraint(x, pltpu.HBM) for x in arrays)


def call(kernel, name, out_shape, inputs, limit, scalars=0, **more):
    return pl.pallas_call(
        kernel,
        out_shape=out_shape,
        in_specs=[SMEM] * scalars + [VMEM] * (len(inputs) - scalars),
        out_specs=jax.tree.map(lambda _: VMEM, out_shape, is_leaf=lambda x: not isinstance(x, tuple)),
        compiler_params=pltpu.CompilerParams(vmem_limit_bytes=limit << 20),
        cost_estimate=pl.CostEstimate(flops=1, bytes_accessed=1, transcendentals=0),
        name=name,
        **more,
    )(*inputs)


SMEM = pl.BlockSpec(memory_space=pltpu.SMEM)
VMEM = pl.BlockSpec(memory_space=pltpu.VMEM)


def shape(dims, dtype=BF16):
    return jax.ShapeDtypeStruct(dims, dtype)


def swap(x, step):
    return lax.ppermute(x, "head", [(i, i ^ step) for i in range(4)])


def other_core(x):
    return lax.ppermute(x, "core", [(0, 1), (1, 0)])


def local_outputs(part, step, decay, skip, values, gate, inject, read, start=()):
    blocks = TOK // BLOCK // 2
    row = lambda width: pl.BlockSpec((1, width), lambda b: (0, 0))
    tokens = lambda width: pl.BlockSpec((BLOCK, width), lambda b: (b + part * blocks, 0))
    out = pl.BlockSpec((BLOCK, CH), lambda b: (b, 0))
    whole = lambda rows: pl.BlockSpec((rows, CH), lambda b: (0, 0))
    carry = (pltpu.HBM((STATE, CH), BF16), pltpu.HBM((8, CH), F32))
    results = (pltpu.HBM((TOK // 2, CH), BF16),) * 2
    scratch = [
        pltpu.VMEM((8, CH), F32), pltpu.VMEM((BLOCK, CH), BF16), pltpu.VMEM((BLOCK, CH), F32),
        pltpu.VMEM((STATE, CH), F32), pltpu.VMEM((8, CH), F32), pltpu.VMEM((BLOCK, CH), F32),
    ]
    if start:
        start_specs = [whole(STATE), whole(8)]
        out_specs = (out, out)
    else:
        start_specs = []
        results += carry
        out_specs = (out, out, whole(STATE), whole(8))
    step, values, gate, inject, read, *start = in_hbm(step, values, gate, inject, read, *start)
    return pl.pallas_call(
        functools.partial(local_kernel, part),
        grid=(blocks,),
        out_shape=results,
        in_specs=[
            pl.BlockSpec((HEADS, BLOCK), lambda b: (0, b + part * blocks)), row(HEADS), row(HEADS),
            tokens(CH), tokens(CH), tokens(STATE), tokens(STATE), *start_specs,
        ],
        out_specs=out_specs,
        scratch_shapes=scratch,
        compiler_params=pltpu.CompilerParams(vmem_limit_bytes=20 << 20),
        cost_estimate=pl.CostEstimate(flops=3 << 30, bytes_accessed=20 << 20, transcendentals=2 << 20),
        name="local_outputs",
    )(step, decay, skip, values, gate, inject, read, *start)


def per_device(
    prompt_values, prompt_gate, prompt_inject, prompt_read, prompt_step, decay_log, skip_gain, norm_weight, out_weight,
    sample_values, sample_gate, sample_inject, sample_read, sample_step, sample_length,
):
    inject = prompt_inject.reshape(TOK, STATE)
    read = prompt_read.reshape(TOK, STATE)
    decay = decay_log.reshape(1, HEADS)
    skip = skip_gain.reshape(1, HEADS)
    norm = norm_weight.reshape(1, CH)
    s_read = sample_read.reshape(2, SLEN, STATE)
    s_inject = sample_inject.reshape(2, SLEN, STATE)
    slices_shape = shape((16, ROWS, 128))

    anywhere = pl.BlockSpec(memory_space=pl.ANY)
    keep, send = pl.pallas_call(
        end_state_kernel,
        out_shape=(slices_shape,) * 2,
        in_specs=[SMEM, anywhere, VMEM, anywhere, anywhere, VMEM],
        out_specs=(VMEM, VMEM),
        scratch_shapes=[
            pltpu.VMEM((TOK, 1024), BF16), pltpu.VMEM((HEADS, TOK), F32), pltpu.VMEM((TOK, CH), BF16),
            pltpu.VMEM((TOK, STATE), BF16), pltpu.SemaphoreType.DMA((4,)),
        ],
        compiler_params=pltpu.CompilerParams(vmem_limit_bytes=24 << 20),
        name="end_state",
    )(*in_hbm(sample_length, prompt_step, decay, prompt_values, inject, s_read))
    sibling = other_core(send)
    joined = call(join_cores_kernel, "join_cores", slices_shape, (keep, sibling), 16)
    joined, step_1, s_step = lax.optimization_barrier((joined, prompt_step, sample_step.transpose(1, 0, 2)))
    slices = lax.all_to_all(joined, ("y", "x"), 0, 0, tiled=True)
    scaled_1, gain_1, *carry = local_outputs(
        0, step_1, decay, skip, prompt_values, prompt_gate, inject, read
    )
    scaled_1, s_values = lax.optimization_barrier((scaled_1, sample_values))
    sample = call(
        sample_kernel, "sample_outputs", (pltpu.HBM((16, CH), F32),) * 3,
        (sample_length, s_step, decay, skip, s_values, sample_gate, s_inject, s_read), 16, 1,
    )
    slices, scaled_1, sample = lax.optimization_barrier((slices, scaled_1, sample))
    prefix = call(prefix_kernel, "prefix", slices_shape, (slices,), 16)
    prefix, step_2 = lax.optimization_barrier((prefix, prompt_step))
    back = lax.all_to_all(prefix, ("y", "x"), 0, 0, tiled=True)
    scaled_2, gain_2 = local_outputs(
        1, step_2, decay, skip, prompt_values, prompt_gate, inject, read, carry
    )
    back, scaled_2, weight, read_2 = lax.optimization_barrier((back, scaled_2, out_weight, read))
    mine, send = call(
        split_cores_kernel, "split_cores", (shape((STATE + TAIL, 1024)), slices_shape), (back, keep, sibling), 16
    )
    theirs = other_core(send)

    near_columns, scaled_2, gain_2, read_2, norm, *sample = fetch(
        FIRST[:1], weight, scaled_2, gain_2, read_2, norm, *sample
    )
    scaled = (scaled_1, scaled_2)
    gain = (gain_1, gain_2)
    state = call(join_halves_kernel, "join_halves", shape((STATE + TAIL, CH)), (mine, theirs), 8)

    def chunk(place, far_columns, *sample):
        start, rows = CHUNKS[place]
        size = rows + (16 if sample else 0)
        leading = place == LEADING
        local = (scaled[start // HALF], gain[start // HALF])
        local = local if leading else in_hbm(*local)
        piece = shape((2, size, PIECE))
        held = pltpu.VMEM((3, CH, PIECE), BF16)
        first, second, normed, *held = pl.pallas_call(
            functools.partial(chunk_kernel, place, bool(sample)),
            out_shape=(piece, piece, shape((size, CH)), *([held] if leading else [])),
            in_specs=[VMEM] * 6 + [anywhere if leading else VMEM] + [VMEM] * len(sample),
            out_specs=(VMEM,) * (4 if leading else 3),
            scratch_shapes=[pltpu.SemaphoreType.DMA((3,))] if leading else [],
            compiler_params=pltpu.CompilerParams(vmem_limit_bytes=24 << 20),
            name="chunk",
        )(state, read_2, *local, norm, near_columns, far_columns, *sample)
        near = lax.optimization_barrier((swap(first, 1), swap(second, 3)))
        return normed, near, *held

    normed_0, near_0, far_columns = chunk(0, *in_hbm(weight), *sample)
    (rest_columns,) = fetch(REST, weight)
    normed_1, near_1 = chunk(1, resident(far_columns))
    rest_0, rest_1 = (
        call(rest_kernel, "rest", shape((4, normed.shape[0], PIECE)), (normed, rest_columns), 24)
        for normed in (normed_0, normed_1)
    )

    def onward(near, rest):
        return call(onward_kernel, "onward", (shape(near[0].shape[1:]),) * 2, (*near, rest), 8)

    def send_on(ons):
        return lax.optimization_barrier((swap(ons[0], 3), swap(ons[1], 1)))

    def own_sum(near, rest):
        return call(own_sum_kernel, "own_sum", shape((2, *near[0].shape[1:]), F32), (*near, rest), 8)

    ons_0, own_0, rest_1 = lax.optimization_barrier((onward(near_0, rest_0), own_sum(near_0, rest_0), rest_1))
    far_0 = send_on(ons_0)
    far_1 = send_on(onward(near_1, rest_1))
    parts = (own_0, *far_0, own_sum(near_1, rest_1), *far_1)
    prompt_mixed, sample_mixed = call(finish_kernel, "finish", (shape((1024, TOK)), shape((2, 1024))), parts, 16)
    return prompt_mixed, sample_mixed.T


def solution(mesh):
    split = Mesh(mesh.devices.reshape(4, 4, 2, mesh.shape["head"]), ("y", "x", "core", "head"))
    return jax.shard_map(
        per_device,
        mesh=split,
        in_specs=(
            P(CTX, "head"), P(CTX, "head"), P(CTX, "head", None), P(CTX, "head", None), P("head", CTX),
            P("head"), P("head"), P("head"), P("head", None),
            P(CTX, None, "head"), P(CTX, None, "head"), P(CTX, None, "head", None), P(CTX, None, "head", None),
            P("head", CTX, None), P(CTX),
        ),
        out_specs=(P("head", CTX), P("head", CTX)),
        check_vma=False,
    )
```

```python
import functools

import jax
import jax.numpy as jnp
from jax import lax
from jax.experimental import pallas as pl
from jax.experimental.pallas import tpu as pltpu
from jax.sharding import Mesh
from jax.sharding import PartitionSpec as P

HEADS = 32
HEAD_DIM = 64
STATE = 256
BLOCK = 128
SLEN = 16
TOK = 512
CH = HEADS * HEAD_DIM
PIECE = 512
HALF = TOK // 2
TAIL = 8
ROWS = 128 + TAIL
CTX = ("y", "x", "core")
F32 = jnp.float32
BF16 = jnp.bfloat16
EXACT = lax.Precision.HIGHEST
LOG2E = 1.4426950408889634
CHUNKS = ((256, 256), (0, 256))
LEADING = 0


def softplus(v):
    return jnp.maximum(v, 0.0) + jnp.log1p(jnp.exp(-jnp.abs(v)))


def iota(shape, dim):
    return lax.broadcasted_iota(jnp.int32, shape, dim)


def column(row):
    n = row.shape[1]
    square = jnp.broadcast_to(row, (n, n))
    return jnp.sum(jnp.where(iota((n, n), 0) == iota((n, n), 1), square, 0.0), axis=1, keepdims=True)


def tokens_first(x):
    pad = jnp.zeros((128 - x.shape[0], x.shape[1]), F32)
    return jnp.transpose(jnp.concatenate([x, pad], axis=0))


def per_pair(columns, pair, shape, low):
    first = jnp.broadcast_to(columns[:, 2 * pair : 2 * pair + 1], shape)
    second = jnp.broadcast_to(columns[:, 2 * pair + 1 : 2 * pair + 2], shape)
    return jnp.where(low, first, second)


def head_lanes(start, width):
    row, lane = iota((128, width), 0), iota((128, width), 1) + start
    return (((row & (HEADS - 1)) == (lane >> 6)) & (row < 3 * HEADS)).astype(BF16)


def three_parts(x):
    hi = x.astype(BF16).astype(F32)
    mid = (x - hi).astype(BF16).astype(F32)
    lo = (x - hi - mid).astype(BF16).astype(F32)
    return hi, mid, lo


def decay_of(tail):
    return tail[4:5] + tail[5:6] + tail[6:7]


def with_decay(tail, decay):
    row = iota((TAIL, 128), 0)
    for i, part in enumerate(three_parts(decay)):
        tail = jnp.where(row == 4 + i, part, tail)
    return tail


def end_state_kernel(
    length, step_any, decay_ref, values_any, inject_any, read_ref, keep_ref, send_ref,
    scaled, step_ref, values_ref, inject_ref, sems,
):
    copies = [
        pltpu.make_async_copy(step_any, step_ref, sems.at[0]),
        pltpu.make_async_copy(inject_any, inject_ref, sems.at[1]),
    ]
    for half in range(2):
        lanes = slice(half * 1024, (half + 1) * 1024)
        copies.append(pltpu.make_async_copy(values_any.at[:, lanes], values_ref.at[:, lanes], sems.at[2 + half]))
    for copy in copies:
        copy.start()
    copies[0].wait()
    core = lax.axis_index("core")
    step = softplus(step_ref[...])
    logs = step * -jnp.exp(column(decay_ref[...]))
    later = (iota((BLOCK, BLOCK), 0) > iota((BLOCK, BLOCK), 1)).astype(F32)
    after = jnp.zeros((HEADS, 1), F32)
    parts = []
    for b in reversed(range(TOK // BLOCK)):
        here = logs[:, b * BLOCK : (b + 1) * BLOCK]
        parts.append(jnp.dot(here, later, precision=EXACT, preferred_element_type=F32) + after)
        after = after + jnp.sum(here, axis=1, keepdims=True)
    weight = jnp.exp(jnp.concatenate(parts[::-1], axis=1)) * step
    weight = jnp.transpose(jnp.concatenate([*three_parts(weight), jnp.zeros((128 - 3 * HEADS, TOK), F32)], axis=0))
    weight = weight.astype(BF16)
    total = tokens_first(jnp.broadcast_to(jnp.exp(after), (HEADS, 128)))[0:8]
    copies[1].wait()
    inject_t = jnp.transpose(inject_ref[...].astype(F32)).astype(BF16)
    low_row = iota((8, 128), 1) < HEAD_DIM
    row = iota((TAIL, 128), 0)
    tails = []
    for half in range(2):
        lanes = slice(half * 128, (half + 1) * 128)
        tail = jnp.zeros((TAIL, 128), F32)
        for s in range(2):
            last = iota((SLEN, 128), 0) == length[s] - 1
            picked = jnp.sum(jnp.where(last, read_ref[s, :, lanes].astype(F32), 0.0), axis=0, keepdims=True)
            tail = jnp.where(row == 2 * core + s, picked, tail)
        tails.append(tail)
    for half in range(2):
        lanes = slice(half * 1024, (half + 1) * 1024)
        wide = jnp.dot(weight, head_lanes(half * 1024, 1024), preferred_element_type=F32)
        copies[2 + half].wait()
        scaled[...] = (values_ref[:, lanes].astype(F32) * wide).astype(BF16)
        state = jnp.dot(inject_t, scaled[...], preferred_element_type=F32).astype(BF16)

        def put(out_ref, half=half, state=state):
            for q in range(8):
                decay = per_pair(total, half * 8 + q, (8, 128), low_row)[0:1]
                for n in range(2):
                    out_ref[2 * q + n, 0:128, :] = state[n * 128 : (n + 1) * 128, q * 128 : (q + 1) * 128]
                    out_ref[2 * q + n, 128:ROWS, :] = with_decay(tails[n], decay).astype(BF16)

        @pl.when(core == half)
        def _(put=put):
            put(keep_ref)

        @pl.when(core != half)
        def _(put=put):
            put(send_ref)


def join_cores_kernel(own_ref, sib_ref, out_ref):
    first = lax.axis_index("core") == 0
    row = iota((TAIL, 128), 0)
    for k in range(16):
        own_tail = own_ref[k, 128:ROWS, :].astype(F32)
        sib_tail = sib_ref[k, 128:ROWS, :].astype(F32)
        own_decay, sib_decay = decay_of(own_tail), decay_of(sib_tail)
        own_weight = jnp.where(first, sib_decay, 1.0)
        sib_weight = jnp.where(first, 1.0, own_decay)
        out_ref[k, 0:128, :] = (
            own_ref[k, 0:128, :].astype(F32) * own_weight + sib_ref[k, 0:128, :].astype(F32) * sib_weight
        ).astype(BF16)
        tail = jnp.where(row < 4, own_tail + sib_tail, 0.0)
        out_ref[k, 128:ROWS, :] = with_decay(tail, own_decay * sib_decay).astype(BF16)


def prefix_kernel(in_ref, out_ref):
    state = jnp.zeros((128, 128), F32)
    for i in range(16):
        out_ref[i, 0:128, :] = state.astype(BF16)
        decay = decay_of(in_ref[i, 128:ROWS, :].astype(F32))
        state = state * decay + in_ref[i, 0:128, :].astype(F32)
    tails = jnp.concatenate([in_ref[i, 128:ROWS, :].astype(F32) for i in range(16)], axis=0).astype(BF16)
    readings = jnp.dot(tails, state.astype(BF16), preferred_element_type=F32)
    for i in range(16):
        out_ref[i, 128:ROWS, :] = readings[TAIL * i : TAIL * (i + 1)].astype(BF16)


def split_cores_kernel(back_ref, own_ref, sib_ref, mine_ref, send_ref):
    first = lax.axis_index("core") == 0
    for k in range(16):
        q, n = k // 2, k % 2
        arrived = back_ref[k, 0:128, :].astype(F32)
        own_decay = decay_of(own_ref[k, 128:ROWS, :].astype(F32))
        sib_decay = decay_of(sib_ref[k, 128:ROWS, :].astype(F32))
        decay = jnp.where(first, own_decay, sib_decay)
        state = jnp.where(first, own_ref[k, 0:128, :].astype(F32), sib_ref[k, 0:128, :].astype(F32))
        second = arrived * decay + state
        mine_ref[n * 128 : (n + 1) * 128, q * 128 : (q + 1) * 128] = jnp.where(first, arrived, second).astype(BF16)
        send_ref[k, 0:128, :] = jnp.where(first, second, arrived).astype(BF16)
        send_ref[k, 128:ROWS, :] = back_ref[k, 128:ROWS, :]
    for q in range(8):
        mine_ref[STATE : STATE + TAIL, q * 128 : (q + 1) * 128] = (
            back_ref[2 * q, 128:ROWS, :].astype(F32) + back_ref[2 * q + 1, 128:ROWS, :].astype(F32)
        ).astype(BF16)


def local_kernel(
    part, step_ref, decay_ref, skip_ref, values_ref, gate_ref, inject_ref, read_ref, *refs
):
    if part == 0:
        scaled_ref, gain_ref, carry, carry_before, ends, weighted, carried, state, before, stepped_all = refs
    else:
        start, start_before, scaled_ref, gain_ref, ends, weighted, carried, state, before, stepped_all = refs

    @pl.when(pl.program_id(0) == 0)
    def _():
        if part == 0:
            state[...] = jnp.zeros_like(state)
            before[...] = jnp.ones_like(before)
        else:
            state[...] = start[...].astype(F32)
            before[...] = start_before[...]

    step = softplus(step_ref[...])
    logs = step * -jnp.exp(column(decay_ref[...]))
    upto = (iota((BLOCK, BLOCK), 0) <= iota((BLOCK, BLOCK), 1)).astype(F32)
    running = jnp.dot(logs, upto, precision=EXACT, preferred_element_type=F32) * LOG2E
    running_t = tokens_first(running)
    parts = jnp.concatenate([*three_parts(step), jnp.zeros((128 - 3 * HEADS, BLOCK), F32)], axis=0)
    stepped_all[...] = values_ref[...].astype(F32) * jnp.dot(
        jnp.transpose(parts).astype(BF16), head_lanes(0, CH), preferred_element_type=F32
    )
    read = read_ref[...]
    inject = inject_ref[...]
    inject_t = jnp.transpose(inject.astype(F32)).astype(BF16)
    scores = jnp.dot(read, inject_t, preferred_element_type=F32)
    carried[...] = jnp.dot(read, state[...].astype(BF16), preferred_element_type=F32)
    causal = iota((BLOCK, BLOCK), 0) >= iota((BLOCK, BLOCK), 1)
    low = iota((BLOCK, 128), 1) < HEAD_DIM
    for pair in range(16):
        lanes = slice(pair * 128, (pair + 1) * 128)
        mixing = []
        spread = []
        for h in (2 * pair, 2 * pair + 1):
            mine = jnp.broadcast_to(running_t[:, h : h + 1], (BLOCK, BLOCK))
            gap = jnp.where(causal, mine - running[h : h + 1, :], -1e30)
            mixing.append((scores * jnp.exp2(gap)).astype(BF16))
            spread.append(mine)
        now = jnp.where(low, spread[0], spread[1])
        grown = jnp.exp2(now)
        values = values_ref[:, lanes].astype(F32)
        stepped = stepped_all[:, lanes]
        diagonal = jnp.concatenate([jnp.where(low, stepped, 0.0), jnp.where(low, 0.0, stepped)], axis=0)
        local = jnp.dot(
            jnp.concatenate(mixing, axis=1), diagonal.astype(BF16), preferred_element_type=F32
        )
        skip = per_pair(skip_ref[...], pair, (1, 128), low[0:1])
        out = local + carried[:, lanes] * grown + skip * values
        gate = gate_ref[:, lanes].astype(F32)
        gate = gate * jax.nn.sigmoid(gate)
        scaled_ref[:, lanes] = (out * gate).astype(BF16)
        gain_ref[:, lanes] = (gate * grown * before[0:1, lanes]).astype(BF16)
        end = now[BLOCK - 1 : BLOCK, :]
        weighted[:, lanes] = (stepped * jnp.exp2(end - now)).astype(BF16)
        ends[0:1, lanes] = jnp.exp2(end)
    state[...] = state[...] * ends[0:1, :] + jnp.dot(inject_t, weighted[...], preferred_element_type=F32)
    before[0:1, :] = before[0:1, :] * ends[0:1, :]
    if part == 0:

        @pl.when(pl.program_id(0) == pl.num_programs(0) - 1)
        def _():
            carry[...] = state[...].astype(BF16)
            carry_before[...] = before[...]


def sample_kernel(
    length, step_ref, decay_ref, skip_ref, values_ref, gate_ref, inject_ref, read_ref, local_ref, grown_ref, gate_out_ref
):
    rate = -jnp.exp(column(decay_ref[...]))
    row = iota((16, CH), 0)
    place = iota((SLEN, 128), 0)
    place_wide = iota((SLEN, STATE), 0)
    narrow = []
    for s in range(2):
        last = length[s] - 1
        step = softplus(step_ref[s])
        logs = step * rate
        pad = jnp.zeros((HEADS, 128 - SLEN), F32)
        step_t = tokens_first(jnp.concatenate([step, pad], axis=1))[0:SLEN]
        logs_t = tokens_first(jnp.concatenate([logs, pad], axis=1))[0:SLEN]
        logs_t = jnp.where(place <= last, logs_t, 0.0)
        gap = jnp.zeros((SLEN, 128), F32)
        for k in range(SLEN):
            gap = gap + jnp.where(place < k, logs_t[k : k + 1], 0.0)
        whole = jnp.sum(logs_t, axis=0, keepdims=True)
        read = jnp.sum(jnp.where(place_wide == last, read_ref[s].astype(F32), 0.0), axis=0, keepdims=True)
        scores = jnp.sum(inject_ref[s].astype(F32) * read, axis=1, keepdims=True)
        narrow.append(jnp.where(place <= last, scores * jnp.exp(gap) * step_t, 0.0))
        narrow.append(jnp.broadcast_to(jnp.exp(whole), (SLEN, 128)))
    skip = jnp.concatenate([skip_ref[...], jnp.zeros((1, 128 - HEADS), F32)], axis=1)
    narrow.append(jnp.broadcast_to(skip, (SLEN, 128)))
    spread = (iota((128, CH), 1) // HEAD_DIM == iota((128, CH), 0)).astype(BF16)
    parts = jnp.concatenate(three_parts(jnp.concatenate(narrow, axis=0)), axis=0).astype(BF16)
    wide = jnp.dot(parts, spread, preferred_element_type=F32)
    wide = wide[0:80] + wide[80:160] + wide[160:240]
    local_all = jnp.zeros((16, CH), F32)
    grown_all = jnp.zeros((16, CH), F32)
    gate_all = jnp.zeros((16, CH), F32)
    for s in range(2):
        values = values_ref[s].astype(F32)
        at_last = iota((SLEN, CH), 0) == length[s] - 1
        picked = jnp.sum(jnp.where(at_last, values, 0.0), axis=0, keepdims=True)
        gate = jnp.sum(jnp.where(at_last, gate_ref[s].astype(F32), 0.0), axis=0, keepdims=True)
        local = jnp.sum(wide[32 * s : 32 * s + SLEN] * values, axis=0, keepdims=True) + wide[64:65] * picked
        local_all = jnp.where(row == s, local, local_all)
        grown_all = jnp.where(row == s, wide[32 * s + SLEN : 32 * s + SLEN + 1], grown_all)
        gate_all = jnp.where(row == s, gate / (1.0 + jnp.exp(-gate)), gate_all)
    local_ref[...] = local_all
    grown_ref[...] = grown_all
    gate_out_ref[...] = gate_all


def normalize(gated, weight):
    mean = jnp.sum(gated * gated, axis=1, keepdims=True) * (1.0 / CH)
    return (gated * lax.rsqrt(mean + 1e-05) * weight).astype(BF16)


FIRST = ((1, 0), (2, 0), (3, 1), (2, 1))
REST = ((3, 0), (1, 1), (0, 0), (0, 1))


def column_copies(pieces, weight_ref, held, sems):
    z = lax.axis_index("head")
    copies = []
    for i, (flip, half) in enumerate(pieces):
        at = pl.multiple_of(((z ^ flip) * 2 + half) * PIECE, PIECE)
        copies.append(pltpu.make_async_copy(weight_ref.at[:, pl.ds(at, PIECE)], held.at[i], sems.at[i]))
    return copies


def fetch_kernel(pieces, weight_ref, *refs):
    extra = (len(refs) - 2) // 2
    extra_refs, (out_ref, *extra_outs, sems) = refs[:extra], refs[extra:]
    copies = column_copies(pieces, weight_ref, out_ref, sems)
    for i, (src, dst) in enumerate(zip(extra_refs, extra_outs)):
        copies.append(pltpu.make_async_copy(src, dst, sems.at[len(pieces) + i]))
    for copy in copies:
        copy.start()
    for copy in copies:
        copy.wait()


def resident(x):
    return pltpu.with_memory_space_constraint(x, pltpu.VMEM)


def fetch(pieces, weight, *extra):
    held = pltpu.VMEM((len(pieces), CH, PIECE), BF16)
    out = pl.pallas_call(
        functools.partial(fetch_kernel, pieces),
        out_shape=(held, *(pltpu.VMEM(x.shape, x.dtype) for x in extra)),
        in_specs=[pl.BlockSpec(memory_space=pl.ANY)] * (1 + len(extra)),
        out_specs=(VMEM,) * (1 + len(extra)),
        scratch_shapes=[pltpu.SemaphoreType.DMA((len(pieces) + len(extra),))],
        compiler_params=pltpu.CompilerParams(vmem_limit_bytes=12 << 20),
        name="fetch_weight",
    )(*in_hbm(weight, *extra))
    return tuple(resident(x) for x in out)


def project(normed, columns, outs):
    for column, (ref, k) in zip(columns, outs):
        ref[k] = jnp.dot(normed[...], column[...], preferred_element_type=F32).astype(BF16)


HERE = tuple(slice(start % HALF, start % HALF + rows) for start, rows in CHUNKS)


def arriving(place, state_ref, read_ref):
    start, rows = CHUNKS[place]
    return jnp.dot(read_ref[start : start + rows, :], state_ref[0:STATE, :], preferred_element_type=F32)


def join_halves_kernel(mine_ref, theirs_ref, state_ref):
    core = lax.axis_index("core")
    state_ref[:, pl.ds(pl.multiple_of(core * 1024, 1024), 1024)] = mine_ref[...]
    for q in range(8):
        lanes = pl.ds(pl.multiple_of((1 - core) * 1024 + q * 128, 128), 128)
        for n in range(2):
            state_ref[n * 128 : (n + 1) * 128, lanes] = theirs_ref[2 * q + n, 0:128, :]
        state_ref[STATE : STATE + TAIL, lanes] = (
            theirs_ref[2 * q, 128:ROWS, :].astype(F32) + theirs_ref[2 * q + 1, 128:ROWS, :].astype(F32)
        ).astype(BF16)


def chunk_kernel(place, sampled, state_ref, read_ref, scaled_ref, gain_ref, norm_ref, near_ref, far_ref, *refs):
    if place == LEADING:
        *sample, first_ref, second_ref, normed_ref, held, sems = refs
        copies = column_copies(FIRST[1:], far_ref, held, sems)
        copies[0].start()
    else:
        *sample, first_ref, second_ref, normed_ref = refs
        held = far_ref
    arrived = arriving(place, state_ref, read_ref)
    if place == LEADING:
        copies[1].start()
    gated = scaled_ref[HERE[place], :].astype(F32) + arrived * gain_ref[HERE[place], :].astype(F32)
    normed_ref[0 : CHUNKS[place][1], :] = normalize(gated, norm_ref[...])
    if place == LEADING:
        copies[2].start()
    if sampled:
        local_ref, grown_ref, gate_ref = sample
        readings = state_ref[STATE : STATE + TAIL, :].astype(F32)
        moved = jnp.concatenate([readings[2:TAIL], readings[0:2]], axis=0)
        readings = jnp.where(lax.axis_index("core") == 0, readings, moved)
        readings = jnp.concatenate([readings, jnp.zeros((16 - TAIL, CH), F32)], axis=0)
        sampled = (local_ref[...] + readings * grown_ref[...]) * gate_ref[...]
        rows = CHUNKS[place][1]
        normed_ref[rows : rows + 16, :] = normalize(sampled, norm_ref[...])
    project(normed_ref, (near_ref.at[0],), ((first_ref, 0),))
    for i, out in enumerate(((first_ref, 1), (second_ref, 0), (second_ref, 1))):
        if place == LEADING:
            copies[i].wait()
        project(normed_ref, (held.at[i],), (out,))


def rest_kernel(normed_ref, weight_ref, rest_ref):
    project(normed_ref, [weight_ref.at[i] for i in range(4)], ((rest_ref, 1), (rest_ref, 3), (rest_ref, 0), (rest_ref, 2)))


def onward_kernel(piece, near_ref, rest_ref, out_ref):
    out_ref[...] = (rest_ref[piece].astype(F32) + near_ref[1].astype(F32)).astype(BF16)


def own_sum_kernel(a_ref, b_ref, rest_ref, out_ref):
    out_ref[0] = rest_ref[0].astype(F32) + a_ref[0].astype(F32)
    out_ref[1] = rest_ref[2].astype(F32) + b_ref[0].astype(F32)


def finish_kernel(*refs):
    ins, out_ref, sample_ref = refs[:-2], refs[-2], refs[-1]
    for place, (start, rows) in enumerate(CHUNKS):
        own, *far = ins[3 * place : 3 * place + 3]
        for half in range(2):
            total = own[half] + far[half][...].astype(F32)
            columns = slice(half * PIECE, (half + 1) * PIECE)
            out_ref[columns, start : start + rows] = jnp.transpose(total[0:rows]).astype(BF16)
            if place == LEADING:
                sample_ref[:, columns] = total[rows : rows + 2].astype(BF16)


def in_hbm(*arrays):
    return tuple(pltpu.with_memory_space_constraint(x, pltpu.HBM) for x in arrays)


def call(kernel, name, out_shape, inputs, limit, scalars=0, **more):
    return pl.pallas_call(
        kernel,
        out_shape=out_shape,
        in_specs=[SMEM] * scalars + [VMEM] * (len(inputs) - scalars),
        out_specs=jax.tree.map(lambda _: VMEM, out_shape, is_leaf=lambda x: not isinstance(x, tuple)),
        compiler_params=pltpu.CompilerParams(vmem_limit_bytes=limit << 20),
        cost_estimate=pl.CostEstimate(flops=1, bytes_accessed=1, transcendentals=0),
        name=name,
        **more,
    )(*inputs)


SMEM = pl.BlockSpec(memory_space=pltpu.SMEM)
VMEM = pl.BlockSpec(memory_space=pltpu.VMEM)


def shape(dims, dtype=BF16):
    return jax.ShapeDtypeStruct(dims, dtype)


def swap(x, step):
    return lax.ppermute(x, "head", [(i, i ^ step) for i in range(4)])


def other_core(x):
    return lax.ppermute(x, "core", [(0, 1), (1, 0)])


def local_outputs(part, step, decay, skip, values, gate, inject, read, start=()):
    blocks = TOK // BLOCK // 2
    row = lambda width: pl.BlockSpec((1, width), lambda b: (0, 0))
    tokens = lambda width: pl.BlockSpec((BLOCK, width), lambda b: (b + part * blocks, 0))
    out = pl.BlockSpec((BLOCK, CH), lambda b: (b, 0))
    whole = lambda rows: pl.BlockSpec((rows, CH), lambda b: (0, 0))
    carry = (pltpu.HBM((STATE, CH), BF16), pltpu.HBM((8, CH), F32))
    results = (pltpu.HBM((TOK // 2, CH), BF16),) * 2
    scratch = [
        pltpu.VMEM((8, CH), F32), pltpu.VMEM((BLOCK, CH), BF16), pltpu.VMEM((BLOCK, CH), F32),
        pltpu.VMEM((STATE, CH), F32), pltpu.VMEM((8, CH), F32), pltpu.VMEM((BLOCK, CH), F32),
    ]
    if start:
        start_specs = [whole(STATE), whole(8)]
        out_specs = (out, out)
    else:
        start_specs = []
        results += carry
        out_specs = (out, out, whole(STATE), whole(8))
    step, values, gate, inject, read, *start = in_hbm(step, values, gate, inject, read, *start)
    return pl.pallas_call(
        functools.partial(local_kernel, part),
        grid=(blocks,),
        out_shape=results,
        in_specs=[
            pl.BlockSpec((HEADS, BLOCK), lambda b: (0, b + part * blocks)), row(HEADS), row(HEADS),
            tokens(CH), tokens(CH), tokens(STATE), tokens(STATE), *start_specs,
        ],
        out_specs=out_specs,
        scratch_shapes=scratch,
        compiler_params=pltpu.CompilerParams(vmem_limit_bytes=20 << 20),
        cost_estimate=pl.CostEstimate(flops=3 << 30, bytes_accessed=20 << 20, transcendentals=2 << 20),
        name="local_outputs",
    )(step, decay, skip, values, gate, inject, read, *start)


def per_device(
    prompt_values, prompt_gate, prompt_inject, prompt_read, prompt_step, decay_log, skip_gain, norm_weight, out_weight,
    sample_values, sample_gate, sample_inject, sample_read, sample_step, sample_length,
):
    inject = prompt_inject.reshape(TOK, STATE)
    read = prompt_read.reshape(TOK, STATE)
    decay = decay_log.reshape(1, HEADS)
    skip = skip_gain.reshape(1, HEADS)
    norm = norm_weight.reshape(1, CH)
    s_read = sample_read.reshape(2, SLEN, STATE)
    s_inject = sample_inject.reshape(2, SLEN, STATE)
    slices_shape = shape((16, ROWS, 128))

    anywhere = pl.BlockSpec(memory_space=pl.ANY)
    keep, send = pl.pallas_call(
        end_state_kernel,
        out_shape=(slices_shape,) * 2,
        in_specs=[SMEM, anywhere, VMEM, anywhere, anywhere, VMEM],
        out_specs=(VMEM, VMEM),
        scratch_shapes=[
            pltpu.VMEM((TOK, 1024), BF16), pltpu.VMEM((HEADS, TOK), F32), pltpu.VMEM((TOK, CH), BF16),
            pltpu.VMEM((TOK, STATE), BF16), pltpu.SemaphoreType.DMA((4,)),
        ],
        compiler_params=pltpu.CompilerParams(vmem_limit_bytes=24 << 20),
        name="end_state",
    )(*in_hbm(sample_length, prompt_step, decay, prompt_values, inject, s_read))
    sibling = other_core(send)
    joined = call(join_cores_kernel, "join_cores", slices_shape, (keep, sibling), 16)
    joined, step_1, s_step = lax.optimization_barrier((joined, prompt_step, sample_step.transpose(1, 0, 2)))
    slices = lax.all_to_all(joined, ("y", "x"), 0, 0, tiled=True)
    scaled_1, gain_1, *carry = local_outputs(
        0, step_1, decay, skip, prompt_values, prompt_gate, inject, read
    )
    scaled_1, s_values = lax.optimization_barrier((scaled_1, sample_values))
    sample = call(
        sample_kernel, "sample_outputs", (pltpu.HBM((16, CH), F32),) * 3,
        (sample_length, s_step, decay, skip, s_values, sample_gate, s_inject, s_read), 16, 1,
    )
    slices, scaled_1, sample = lax.optimization_barrier((slices, scaled_1, sample))
    prefix = call(prefix_kernel, "prefix", slices_shape, (slices,), 16)
    prefix, step_2 = lax.optimization_barrier((prefix, prompt_step))
    back = lax.all_to_all(prefix, ("y", "x"), 0, 0, tiled=True)
    scaled_2, gain_2 = local_outputs(
        1, step_2, decay, skip, prompt_values, prompt_gate, inject, read, carry
    )
    back, scaled_2, weight, read_2 = lax.optimization_barrier((back, scaled_2, out_weight, read))
    mine, send = call(
        split_cores_kernel, "split_cores", (shape((STATE + TAIL, 1024)), slices_shape), (back, keep, sibling), 16
    )
    theirs = other_core(send)

    near_columns, scaled_2, gain_2, read_2, norm, *sample = fetch(
        FIRST[:1], weight, scaled_2, gain_2, read_2, norm, *sample
    )
    scaled = (scaled_1, scaled_2)
    gain = (gain_1, gain_2)
    state = call(join_halves_kernel, "join_halves", shape((STATE + TAIL, CH)), (mine, theirs), 8)

    def chunk(place, far_columns, *sample):
        start, rows = CHUNKS[place]
        size = rows + (16 if sample else 0)
        leading = place == LEADING
        local = (scaled[start // HALF], gain[start // HALF])
        local = local if leading else in_hbm(*local)
        piece = shape((2, size, PIECE))
        held = pltpu.VMEM((3, CH, PIECE), BF16)
        first, second, normed, *held = pl.pallas_call(
            functools.partial(chunk_kernel, place, bool(sample)),
            out_shape=(piece, piece, shape((size, CH)), *([held] if leading else [])),
            in_specs=[VMEM] * 6 + [anywhere if leading else VMEM] + [VMEM] * len(sample),
            out_specs=(VMEM,) * (4 if leading else 3),
            scratch_shapes=[pltpu.SemaphoreType.DMA((3,))] if leading else [],
            compiler_params=pltpu.CompilerParams(vmem_limit_bytes=24 << 20),
            name="chunk",
        )(state, read_2, *local, norm, near_columns, far_columns, *sample)
        near = (swap(first, 1), swap(second, 3))
        return normed, near, *held

    normed_0, near_0, far_columns = chunk(0, *in_hbm(weight), *sample)
    (rest_columns,) = fetch(REST, weight)
    normed_1, near_1 = chunk(1, resident(far_columns))
    rest_0, rest_1 = (
        call(rest_kernel, "rest", shape((4, normed.shape[0], PIECE)), (normed, rest_columns), 24)
        for normed in (normed_0, normed_1)
    )

    def onward(near, rest):
        return [
            call(functools.partial(onward_kernel, piece), "onward", shape(x.shape[1:]), (x, rest), 8)
            for piece, x in zip((1, 3), near)
        ]

    def send_on(ons):
        return swap(ons[0], 3), swap(ons[1], 1)

    def own_sum(near, rest):
        return call(own_sum_kernel, "own_sum", shape((2, *near[0].shape[1:]), F32), (*near, rest), 8)

    ons_0, own_0, rest_1 = lax.optimization_barrier((onward(near_0, rest_0), own_sum(near_0, rest_0), rest_1))
    far_0 = send_on(ons_0)
    far_1 = send_on(onward(near_1, rest_1))
    parts = (own_0, *far_0, own_sum(near_1, rest_1), *far_1)
    prompt_mixed, sample_mixed = call(finish_kernel, "finish", (shape((1024, TOK)), shape((2, 1024))), parts, 16)
    return prompt_mixed, sample_mixed.T


def solution(mesh):
    split = Mesh(mesh.devices.reshape(4, 4, 2, mesh.shape["head"]), ("y", "x", "core", "head"))
    return jax.shard_map(
        per_device,
        mesh=split,
        in_specs=(
            P(CTX, "head"), P(CTX, "head"), P(CTX, "head", None), P(CTX, "head", None), P("head", CTX),
            P("head"), P("head"), P("head"), P("head", None),
            P(CTX, None, "head"), P(CTX, None, "head"), P(CTX, None, "head", None), P(CTX, None, "head", None),
            P("head", CTX, None), P(CTX),
        ),
        out_specs=(P("head", CTX), P("head", CTX)),
        check_vma=False,
    )
```

```python
import functools

import jax
import jax.numpy as jnp
from jax import lax
from jax.experimental import pallas as pl
from jax.experimental.pallas import tpu as pltpu
from jax.sharding import Mesh
from jax.sharding import PartitionSpec as P

HEADS = 32
HEAD_DIM = 64
STATE = 256
BLOCK = 128
SLEN = 16
TOK = 512
CH = HEADS * HEAD_DIM
PIECE = 512
HALF = TOK // 2
TAIL = 8
ROWS = 128 + TAIL
CTX = ("y", "x", "core")
F32 = jnp.float32
BF16 = jnp.bfloat16
EXACT = lax.Precision.HIGHEST
LOG2E = 1.4426950408889634
CHUNKS = ((256, 256), (0, 256))
LEADING = 0


def softplus(v):
    return jnp.maximum(v, 0.0) + jnp.log1p(jnp.exp(-jnp.abs(v)))


def iota(shape, dim):
    return lax.broadcasted_iota(jnp.int32, shape, dim)


def column(row):
    n = row.shape[1]
    square = jnp.broadcast_to(row, (n, n))
    return jnp.sum(jnp.where(iota((n, n), 0) == iota((n, n), 1), square, 0.0), axis=1, keepdims=True)


def tokens_first(x):
    pad = jnp.zeros((128 - x.shape[0], x.shape[1]), F32)
    return jnp.transpose(jnp.concatenate([x, pad], axis=0))


def per_pair(columns, pair, shape, low):
    first = jnp.broadcast_to(columns[:, 2 * pair : 2 * pair + 1], shape)
    second = jnp.broadcast_to(columns[:, 2 * pair + 1 : 2 * pair + 2], shape)
    return jnp.where(low, first, second)


def head_lanes(start, width):
    row, lane = iota((128, width), 0), iota((128, width), 1) + start
    return (((row & (HEADS - 1)) == (lane >> 6)) & (row < 3 * HEADS)).astype(BF16)


def three_parts(x):
    hi = x.astype(BF16).astype(F32)
    mid = (x - hi).astype(BF16).astype(F32)
    lo = (x - hi - mid).astype(BF16).astype(F32)
    return hi, mid, lo


def decay_of(tail):
    return tail[4:5] + tail[5:6] + tail[6:7]


def with_decay(tail, decay):
    row = iota((TAIL, 128), 0)
    for i, part in enumerate(three_parts(decay)):
        tail = jnp.where(row == 4 + i, part, tail)
    return tail


def end_state_kernel(
    length, step_any, decay_ref, values_any, inject_any, read_ref, keep_ref, send_ref,
    scaled, step_ref, values_ref, inject_ref, sems,
):
    copies = [
        pltpu.make_async_copy(step_any, step_ref, sems.at[0]),
        pltpu.make_async_copy(inject_any, inject_ref, sems.at[1]),
    ]
    for half in range(2):
        lanes = slice(half * 1024, (half + 1) * 1024)
        copies.append(pltpu.make_async_copy(values_any.at[:, lanes], values_ref.at[:, lanes], sems.at[2 + half]))
    for copy in copies:
        copy.start()
    copies[0].wait()
    core = lax.axis_index("core")
    step = softplus(step_ref[...])
    logs = step * -jnp.exp(column(decay_ref[...]))
    later = (iota((BLOCK, BLOCK), 0) > iota((BLOCK, BLOCK), 1)).astype(F32)
    after = jnp.zeros((HEADS, 1), F32)
    parts = []
    for b in reversed(range(TOK // BLOCK)):
        here = logs[:, b * BLOCK : (b + 1) * BLOCK]
        parts.append(jnp.dot(here, later, precision=EXACT, preferred_element_type=F32) + after)
        after = after + jnp.sum(here, axis=1, keepdims=True)
    weight = jnp.exp(jnp.concatenate(parts[::-1], axis=1)) * step
    weight = jnp.transpose(jnp.concatenate([*three_parts(weight), jnp.zeros((128 - 3 * HEADS, TOK), F32)], axis=0))
    weight = weight.astype(BF16)
    total = tokens_first(jnp.broadcast_to(jnp.exp(after), (HEADS, 128)))[0:8]
    copies[1].wait()
    inject_t = jnp.transpose(inject_ref[...].astype(F32)).astype(BF16)
    low_row = iota((8, 128), 1) < HEAD_DIM
    row = iota((TAIL, 128), 0)
    tails = []
    for half in range(2):
        lanes = slice(half * 128, (half + 1) * 128)
        tail = jnp.zeros((TAIL, 128), F32)
        for s in range(2):
            last = iota((SLEN, 128), 0) == length[s] - 1
            picked = jnp.sum(jnp.where(last, read_ref[s, :, lanes].astype(F32), 0.0), axis=0, keepdims=True)
            tail = jnp.where(row == 2 * core + s, picked, tail)
        tails.append(tail)
    for half in range(2):
        lanes = slice(half * 1024, (half + 1) * 1024)
        wide = jnp.dot(weight, head_lanes(half * 1024, 1024), preferred_element_type=F32)
        copies[2 + half].wait()
        scaled[...] = (values_ref[:, lanes].astype(F32) * wide).astype(BF16)
        state = jnp.dot(inject_t, scaled[...], preferred_element_type=F32).astype(BF16)

        def put(out_ref, half=half, state=state):
            for q in range(8):
                decay = per_pair(total, half * 8 + q, (8, 128), low_row)[0:1]
                for n in range(2):
                    out_ref[2 * q + n, 0:128, :] = state[n * 128 : (n + 1) * 128, q * 128 : (q + 1) * 128]
                    out_ref[2 * q + n, 128:ROWS, :] = with_decay(tails[n], decay).astype(BF16)

        @pl.when(core == half)
        def _(put=put):
            put(keep_ref)

        @pl.when(core != half)
        def _(put=put):
            put(send_ref)


def join_cores_kernel(own_ref, sib_ref, out_ref):
    first = lax.axis_index("core") == 0
    row = iota((TAIL, 128), 0)
    for k in range(16):
        own_tail = own_ref[k, 128:ROWS, :].astype(F32)
        sib_tail = sib_ref[k, 128:ROWS, :].astype(F32)
        own_decay, sib_decay = decay_of(own_tail), decay_of(sib_tail)
        own_weight = jnp.where(first, sib_decay, 1.0)
        sib_weight = jnp.where(first, 1.0, own_decay)
        out_ref[k, 0:128, :] = (
            own_ref[k, 0:128, :].astype(F32) * own_weight + sib_ref[k, 0:128, :].astype(F32) * sib_weight
        ).astype(BF16)
        tail = jnp.where(row < 4, own_tail + sib_tail, 0.0)
        out_ref[k, 128:ROWS, :] = with_decay(tail, own_decay * sib_decay).astype(BF16)


def prefix_kernel(in_ref, out_ref):
    state = jnp.zeros((128, 128), F32)
    for i in range(16):
        out_ref[i, 0:128, :] = state.astype(BF16)
        decay = decay_of(in_ref[i, 128:ROWS, :].astype(F32))
        state = state * decay + in_ref[i, 0:128, :].astype(F32)
    tails = jnp.concatenate([in_ref[i, 128:ROWS, :].astype(F32) for i in range(16)], axis=0).astype(BF16)
    readings = jnp.dot(tails, state.astype(BF16), preferred_element_type=F32)
    for i in range(16):
        out_ref[i, 128:ROWS, :] = readings[TAIL * i : TAIL * (i + 1)].astype(BF16)


def split_cores_kernel(back_ref, own_ref, sib_ref, mine_ref, send_ref):
    first = lax.axis_index("core") == 0
    for k in range(16):
        q, n = k // 2, k % 2
        arrived = back_ref[k, 0:128, :].astype(F32)
        own_decay = decay_of(own_ref[k, 128:ROWS, :].astype(F32))
        sib_decay = decay_of(sib_ref[k, 128:ROWS, :].astype(F32))
        decay = jnp.where(first, own_decay, sib_decay)
        state = jnp.where(first, own_ref[k, 0:128, :].astype(F32), sib_ref[k, 0:128, :].astype(F32))
        second = arrived * decay + state
        mine_ref[n * 128 : (n + 1) * 128, q * 128 : (q + 1) * 128] = jnp.where(first, arrived, second).astype(BF16)
        send_ref[k, 0:128, :] = jnp.where(first, second, arrived).astype(BF16)
        send_ref[k, 128:ROWS, :] = back_ref[k, 128:ROWS, :]
    for q in range(8):
        mine_ref[STATE : STATE + TAIL, q * 128 : (q + 1) * 128] = (
            back_ref[2 * q, 128:ROWS, :].astype(F32) + back_ref[2 * q + 1, 128:ROWS, :].astype(F32)
        ).astype(BF16)


def local_kernel(
    part, step_ref, decay_ref, skip_ref, values_ref, gate_ref, inject_ref, read_ref, *refs
):
    if part == 0:
        scaled_ref, gain_ref, carry, carry_before, ends, weighted, carried, state, before, stepped_all = refs
    else:
        start, start_before, scaled_ref, gain_ref, ends, weighted, carried, state, before, stepped_all = refs

    @pl.when(pl.program_id(0) == 0)
    def _():
        if part == 0:
            state[...] = jnp.zeros_like(state)
            before[...] = jnp.ones_like(before)
        else:
            state[...] = start[...].astype(F32)
            before[...] = start_before[...]

    step = softplus(step_ref[...])
    logs = step * -jnp.exp(column(decay_ref[...]))
    upto = (iota((BLOCK, BLOCK), 0) <= iota((BLOCK, BLOCK), 1)).astype(F32)
    running = jnp.dot(logs, upto, precision=EXACT, preferred_element_type=F32) * LOG2E
    running_t = tokens_first(running)
    parts = jnp.concatenate([*three_parts(step), jnp.zeros((128 - 3 * HEADS, BLOCK), F32)], axis=0)
    stepped_all[...] = values_ref[...].astype(F32) * jnp.dot(
        jnp.transpose(parts).astype(BF16), head_lanes(0, CH), preferred_element_type=F32
    )
    read = read_ref[...]
    inject = inject_ref[...]
    inject_t = jnp.transpose(inject.astype(F32)).astype(BF16)
    scores = jnp.dot(read, inject_t, preferred_element_type=F32)
    carried[...] = jnp.dot(read, state[...].astype(BF16), preferred_element_type=F32)
    causal = iota((BLOCK, BLOCK), 0) >= iota((BLOCK, BLOCK), 1)
    low = iota((BLOCK, 128), 1) < HEAD_DIM
    for pair in range(16):
        lanes = slice(pair * 128, (pair + 1) * 128)
        mixing = []
        spread = []
        for h in (2 * pair, 2 * pair + 1):
            mine = jnp.broadcast_to(running_t[:, h : h + 1], (BLOCK, BLOCK))
            gap = jnp.where(causal, mine - running[h : h + 1, :], -1e30)
            mixing.append((scores * jnp.exp2(gap)).astype(BF16))
            spread.append(mine)
        now = jnp.where(low, spread[0], spread[1])
        grown = jnp.exp2(now)
        values = values_ref[:, lanes].astype(F32)
        stepped = stepped_all[:, lanes]
        diagonal = jnp.concatenate([jnp.where(low, stepped, 0.0), jnp.where(low, 0.0, stepped)], axis=0)
        local = jnp.dot(
            jnp.concatenate(mixing, axis=1), diagonal.astype(BF16), preferred_element_type=F32
        )
        skip = per_pair(skip_ref[...], pair, (1, 128), low[0:1])
        out = local + carried[:, lanes] * grown + skip * values
        gate = gate_ref[:, lanes].astype(F32)
        gate = gate * jax.nn.sigmoid(gate)
        scaled_ref[:, lanes] = (out * gate).astype(BF16)
        gain_ref[:, lanes] = (gate * grown * before[0:1, lanes]).astype(BF16)
        end = now[BLOCK - 1 : BLOCK, :]
        weighted[:, lanes] = (stepped * jnp.exp2(end - now)).astype(BF16)
        ends[0:1, lanes] = jnp.exp2(end)
    state[...] = state[...] * ends[0:1, :] + jnp.dot(inject_t, weighted[...], preferred_element_type=F32)
    before[0:1, :] = before[0:1, :] * ends[0:1, :]
    if part == 0:

        @pl.when(pl.program_id(0) == pl.num_programs(0) - 1)
        def _():
            carry[...] = state[...].astype(BF16)
            carry_before[...] = before[...]


def sample_kernel(
    length, step_ref, decay_ref, skip_ref, values_ref, gate_ref, inject_ref, read_ref, local_ref, grown_ref, gate_out_ref
):
    rate = -jnp.exp(column(decay_ref[...]))
    row = iota((16, CH), 0)
    place = iota((SLEN, 128), 0)
    place_wide = iota((SLEN, STATE), 0)
    narrow = []
    for s in range(2):
        last = length[s] - 1
        step = softplus(step_ref[s])
        logs = step * rate
        pad = jnp.zeros((HEADS, 128 - SLEN), F32)
        step_t = tokens_first(jnp.concatenate([step, pad], axis=1))[0:SLEN]
        logs_t = tokens_first(jnp.concatenate([logs, pad], axis=1))[0:SLEN]
        logs_t = jnp.where(place <= last, logs_t, 0.0)
        gap = jnp.zeros((SLEN, 128), F32)
        for k in range(SLEN):
            gap = gap + jnp.where(place < k, logs_t[k : k + 1], 0.0)
        whole = jnp.sum(logs_t, axis=0, keepdims=True)
        read = jnp.sum(jnp.where(place_wide == last, read_ref[s].astype(F32), 0.0), axis=0, keepdims=True)
        scores = jnp.sum(inject_ref[s].astype(F32) * read, axis=1, keepdims=True)
        narrow.append(jnp.where(place <= last, scores * jnp.exp(gap) * step_t, 0.0))
        narrow.append(jnp.broadcast_to(jnp.exp(whole), (SLEN, 128)))
    skip = jnp.concatenate([skip_ref[...], jnp.zeros((1, 128 - HEADS), F32)], axis=1)
    narrow.append(jnp.broadcast_to(skip, (SLEN, 128)))
    spread = ((iota((128, CH), 1) >> 6) == iota((128, CH), 0)).astype(BF16)
    parts = jnp.concatenate(three_parts(jnp.concatenate(narrow, axis=0)), axis=0).astype(BF16)
    wide = jnp.dot(parts, spread, preferred_element_type=F32)
    wide = wide[0:80] + wide[80:160] + wide[160:240]
    local_all = jnp.zeros((16, CH), F32)
    grown_all = jnp.zeros((16, CH), F32)
    gate_all = jnp.zeros((16, CH), F32)
    for s in range(2):
        values = values_ref[s].astype(F32)
        at_last = iota((SLEN, CH), 0) == length[s] - 1
        picked = jnp.sum(jnp.where(at_last, values, 0.0), axis=0, keepdims=True)
        gate = jnp.sum(jnp.where(at_last, gate_ref[s].astype(F32), 0.0), axis=0, keepdims=True)
        local = jnp.sum(wide[32 * s : 32 * s + SLEN] * values, axis=0, keepdims=True) + wide[64:65] * picked
        local_all = jnp.where(row == s, local, local_all)
        grown_all = jnp.where(row == s, wide[32 * s + SLEN : 32 * s + SLEN + 1], grown_all)
        gate_all = jnp.where(row == s, gate / (1.0 + jnp.exp(-gate)), gate_all)
    local_ref[...] = local_all
    grown_ref[...] = grown_all
    gate_out_ref[...] = gate_all


def normalize(gated, weight):
    mean = jnp.sum(gated * gated, axis=1, keepdims=True) * (1.0 / CH)
    return (gated * lax.rsqrt(mean + 1e-05) * weight).astype(BF16)


FIRST = ((1, 0), (2, 0), (3, 1), (2, 1))
REST = ((3, 0), (1, 1), (0, 0), (0, 1))


def column_copies(pieces, weight_ref, held, sems):
    z = lax.axis_index("head")
    copies = []
    for i, (flip, half) in enumerate(pieces):
        at = pl.multiple_of(((z ^ flip) * 2 + half) * PIECE, PIECE)
        copies.append(pltpu.make_async_copy(weight_ref.at[:, pl.ds(at, PIECE)], held.at[i], sems.at[i]))
    return copies


def fetch_kernel(pieces, weight_ref, *refs):
    extra = (len(refs) - 2) // 2
    extra_refs, (out_ref, *extra_outs, sems) = refs[:extra], refs[extra:]
    copies = column_copies(pieces, weight_ref, out_ref, sems)
    for i, (src, dst) in enumerate(zip(extra_refs, extra_outs)):
        copies.append(pltpu.make_async_copy(src, dst, sems.at[len(pieces) + i]))
    for copy in copies:
        copy.start()
    for copy in copies:
        copy.wait()


def resident(x):
    return pltpu.with_memory_space_constraint(x, pltpu.VMEM)


def fetch(pieces, weight, *extra):
    held = pltpu.VMEM((len(pieces), CH, PIECE), BF16)
    out = pl.pallas_call(
        functools.partial(fetch_kernel, pieces),
        out_shape=(held, *(pltpu.VMEM(x.shape, x.dtype) for x in extra)),
        in_specs=[pl.BlockSpec(memory_space=pl.ANY)] * (1 + len(extra)),
        out_specs=(VMEM,) * (1 + len(extra)),
        scratch_shapes=[pltpu.SemaphoreType.DMA((len(pieces) + len(extra),))],
        compiler_params=pltpu.CompilerParams(vmem_limit_bytes=12 << 20),
        name="fetch_weight",
    )(*in_hbm(weight, *extra))
    return tuple(resident(x) for x in out)


def project(normed, columns, outs):
    for column, (ref, k) in zip(columns, outs):
        ref[k] = jnp.dot(normed[...], column[...], preferred_element_type=F32).astype(BF16)


HERE = tuple(slice(start % HALF, start % HALF + rows) for start, rows in CHUNKS)


def arriving(place, state_ref, read_ref):
    start, rows = CHUNKS[place]
    return jnp.dot(read_ref[start : start + rows, :], state_ref[0:STATE, :], preferred_element_type=F32)


def join_halves_kernel(mine_ref, theirs_ref, state_ref):
    core = lax.axis_index("core")
    state_ref[:, pl.ds(pl.multiple_of(core * 1024, 1024), 1024)] = mine_ref[...]
    for q in range(8):
        lanes = pl.ds(pl.multiple_of((1 - core) * 1024 + q * 128, 128), 128)
        for n in range(2):
            state_ref[n * 128 : (n + 1) * 128, lanes] = theirs_ref[2 * q + n, 0:128, :]
        state_ref[STATE : STATE + TAIL, lanes] = (
            theirs_ref[2 * q, 128:ROWS, :].astype(F32) + theirs_ref[2 * q + 1, 128:ROWS, :].astype(F32)
        ).astype(BF16)


def chunk_kernel(place, sampled, state_ref, read_ref, scaled_ref, gain_ref, norm_ref, near_ref, far_ref, *refs):
    if place == LEADING:
        *sample, first_ref, second_ref, normed_ref, held, sems = refs
        copies = column_copies(FIRST[1:], far_ref, held, sems)
        copies[0].start()
    else:
        *sample, first_ref, second_ref, normed_ref = refs
        held = far_ref
    arrived = arriving(place, state_ref, read_ref)
    if place == LEADING:
        copies[1].start()
    gated = scaled_ref[HERE[place], :].astype(F32) + arrived * gain_ref[HERE[place], :].astype(F32)
    normed_ref[0 : CHUNKS[place][1], :] = normalize(gated, norm_ref[...])
    if place == LEADING:
        copies[2].start()
    project(normed_ref, (near_ref.at[0],), ((first_ref, 0),))
    for i, out in enumerate(((first_ref, 1), (second_ref, 0), (second_ref, 1))):
        if place == LEADING:
            copies[i].wait()
        project(normed_ref, (held.at[i],), (out,))


def sample_rows_kernel(state_ref, norm_ref, local_ref, grown_ref, gate_ref, near_ref, far_ref, rest_ref, out_ref):
    readings = state_ref[STATE : STATE + TAIL, :].astype(F32)
    moved = jnp.concatenate([readings[2:TAIL], readings[0:2]], axis=0)
    readings = jnp.where(lax.axis_index("core") == 0, readings, moved)
    readings = jnp.concatenate([readings, jnp.zeros((16 - TAIL, CH), F32)], axis=0)
    sampled = (local_ref[...] + readings * grown_ref[...]) * gate_ref[...]
    normed = normalize(sampled, norm_ref[...])
    z = lax.axis_index("head")
    columns = [near_ref.at[0], *(far_ref.at[i] for i in range(3)), *(rest_ref.at[i] for i in range(4))]
    for column, (flip, half) in zip(columns, FIRST + REST):
        at = pl.multiple_of(((z ^ flip) * 2 + half) * PIECE, PIECE)
        out_ref[:, pl.ds(at, PIECE)] = jnp.dot(normed, column[...], preferred_element_type=F32).astype(BF16)


def rest_kernel(normed_ref, weight_ref, rest_ref):
    project(normed_ref, [weight_ref.at[i] for i in range(4)], ((rest_ref, 1), (rest_ref, 3), (rest_ref, 0), (rest_ref, 2)))


def onward_kernel(a_ref, b_ref, rest_ref, a_out, b_out):
    a_out[...] = (rest_ref[1].astype(F32) + a_ref[1].astype(F32)).astype(BF16)
    b_out[...] = (rest_ref[3].astype(F32) + b_ref[1].astype(F32)).astype(BF16)


def own_sum_kernel(a_ref, b_ref, rest_ref, out_ref):
    out_ref[0] = rest_ref[0].astype(F32) + a_ref[0].astype(F32)
    out_ref[1] = rest_ref[2].astype(F32) + b_ref[0].astype(F32)


def finish_kernel(*refs):
    ins, out_ref = refs[:-1], refs[-1]
    for place, (start, rows) in enumerate(CHUNKS):
        own, *far = ins[3 * place : 3 * place + 3]
        for half in range(2):
            total = own[half] + far[half][...].astype(F32)
            columns = slice(half * PIECE, (half + 1) * PIECE)
            out_ref[columns, start : start + rows] = jnp.transpose(total[0:rows]).astype(BF16)


def in_hbm(*arrays):
    return tuple(pltpu.with_memory_space_constraint(x, pltpu.HBM) for x in arrays)


def call(kernel, name, out_shape, inputs, limit, scalars=0, **more):
    return pl.pallas_call(
        kernel,
        out_shape=out_shape,
        in_specs=[SMEM] * scalars + [VMEM] * (len(inputs) - scalars),
        out_specs=jax.tree.map(lambda _: VMEM, out_shape, is_leaf=lambda x: not isinstance(x, tuple)),
        compiler_params=pltpu.CompilerParams(vmem_limit_bytes=limit << 20),
        cost_estimate=pl.CostEstimate(flops=1, bytes_accessed=1, transcendentals=0),
        name=name,
        **more,
    )(*inputs)


SMEM = pl.BlockSpec(memory_space=pltpu.SMEM)
VMEM = pl.BlockSpec(memory_space=pltpu.VMEM)


def shape(dims, dtype=BF16):
    return jax.ShapeDtypeStruct(dims, dtype)


def swap(x, step):
    return lax.ppermute(x, "head", [(i, i ^ step) for i in range(4)])


def other_core(x):
    return lax.ppermute(x, "core", [(0, 1), (1, 0)])


def local_outputs(part, step, decay, skip, values, gate, inject, read, start=()):
    blocks = TOK // BLOCK // 2
    row = lambda width: pl.BlockSpec((1, width), lambda b: (0, 0))
    tokens = lambda width: pl.BlockSpec((BLOCK, width), lambda b: (b + part * blocks, 0))
    out = pl.BlockSpec((BLOCK, CH), lambda b: (b, 0))
    whole = lambda rows: pl.BlockSpec((rows, CH), lambda b: (0, 0))
    carry = (pltpu.HBM((STATE, CH), BF16), pltpu.HBM((8, CH), F32))
    results = (pltpu.HBM((TOK // 2, CH), BF16),) * 2
    scratch = [
        pltpu.VMEM((8, CH), F32), pltpu.VMEM((BLOCK, CH), BF16), pltpu.VMEM((BLOCK, CH), F32),
        pltpu.VMEM((STATE, CH), F32), pltpu.VMEM((8, CH), F32), pltpu.VMEM((BLOCK, CH), F32),
    ]
    if start:
        start_specs = [whole(STATE), whole(8)]
        out_specs = (out, out)
    else:
        start_specs = []
        results += carry
        out_specs = (out, out, whole(STATE), whole(8))
    step, values, gate, inject, read, *start = in_hbm(step, values, gate, inject, read, *start)
    return pl.pallas_call(
        functools.partial(local_kernel, part),
        grid=(blocks,),
        out_shape=results,
        in_specs=[
            pl.BlockSpec((HEADS, BLOCK), lambda b: (0, b + part * blocks)), row(HEADS), row(HEADS),
            tokens(CH), tokens(CH), tokens(STATE), tokens(STATE), *start_specs,
        ],
        out_specs=out_specs,
        scratch_shapes=scratch,
        compiler_params=pltpu.CompilerParams(vmem_limit_bytes=20 << 20),
        cost_estimate=pl.CostEstimate(flops=3 << 30, bytes_accessed=20 << 20, transcendentals=2 << 20),
        name="local_outputs",
    )(step, decay, skip, values, gate, inject, read, *start)


def per_device(
    prompt_values, prompt_gate, prompt_inject, prompt_read, prompt_step, decay_log, skip_gain, norm_weight, out_weight,
    sample_values, sample_gate, sample_inject, sample_read, sample_step, sample_length,
):
    inject = prompt_inject.reshape(TOK, STATE)
    read = prompt_read.reshape(TOK, STATE)
    decay = decay_log.reshape(1, HEADS)
    skip = skip_gain.reshape(1, HEADS)
    norm = norm_weight.reshape(1, CH)
    s_read = sample_read.reshape(2, SLEN, STATE)
    s_inject = sample_inject.reshape(2, SLEN, STATE)
    slices_shape = shape((16, ROWS, 128))

    anywhere = pl.BlockSpec(memory_space=pl.ANY)
    keep, send = pl.pallas_call(
        end_state_kernel,
        out_shape=(slices_shape,) * 2,
        in_specs=[SMEM, anywhere, VMEM, anywhere, anywhere, VMEM],
        out_specs=(VMEM, VMEM),
        scratch_shapes=[
            pltpu.VMEM((TOK, 1024), BF16), pltpu.VMEM((HEADS, TOK), F32), pltpu.VMEM((TOK, CH), BF16),
            pltpu.VMEM((TOK, STATE), BF16), pltpu.SemaphoreType.DMA((4,)),
        ],
        compiler_params=pltpu.CompilerParams(vmem_limit_bytes=24 << 20),
        name="end_state",
    )(*in_hbm(sample_length, prompt_step, decay, prompt_values, inject, s_read))
    sibling = other_core(send)
    joined = call(join_cores_kernel, "join_cores", slices_shape, (keep, sibling), 16)
    joined, step_1, s_step = lax.optimization_barrier((joined, prompt_step, sample_step.transpose(1, 0, 2)))
    slices = lax.all_to_all(joined, ("y", "x"), 0, 0, tiled=True)
    scaled_1, gain_1, *carry = local_outputs(
        0, step_1, decay, skip, prompt_values, prompt_gate, inject, read
    )
    slices, scaled_1 = lax.optimization_barrier((slices, scaled_1))
    prefix = call(prefix_kernel, "prefix", slices_shape, (slices,), 16)
    prefix, step_2 = lax.optimization_barrier((prefix, prompt_step))
    back = lax.all_to_all(prefix, ("y", "x"), 0, 0, tiled=True)
    scaled_2, gain_2 = local_outputs(
        1, step_2, decay, skip, prompt_values, prompt_gate, inject, read, carry
    )
    back, scaled_2, weight, read_2 = lax.optimization_barrier((back, scaled_2, out_weight, read))
    mine, send = call(
        split_cores_kernel, "split_cores", (shape((STATE + TAIL, 1024)), slices_shape), (back, keep, sibling), 16
    )
    theirs = other_core(send)

    near_columns, scaled_2, gain_2, read_2, norm = fetch(
        FIRST[:1], weight, scaled_2, gain_2, read_2, norm
    )
    scaled = (scaled_1, scaled_2)
    gain = (gain_1, gain_2)
    state = call(join_halves_kernel, "join_halves", shape((STATE + TAIL, CH)), (mine, theirs), 8)

    def chunk(place, far_columns, *sample):
        start, rows = CHUNKS[place]
        size = rows + (16 if sample else 0)
        leading = place == LEADING
        local = (scaled[start // HALF], gain[start // HALF])
        local = local if leading else in_hbm(*local)
        piece = shape((2, size, PIECE))
        held = pltpu.VMEM((3, CH, PIECE), BF16)
        first, second, normed, *held = pl.pallas_call(
            functools.partial(chunk_kernel, place, bool(sample)),
            out_shape=(piece, piece, shape((size, CH)), *([held] if leading else [])),
            in_specs=[VMEM] * 6 + [anywhere if leading else VMEM] + [VMEM] * len(sample),
            out_specs=(VMEM,) * (4 if leading else 3),
            scratch_shapes=[pltpu.SemaphoreType.DMA((3,))] if leading else [],
            compiler_params=pltpu.CompilerParams(vmem_limit_bytes=24 << 20),
            name="chunk",
        )(state, read_2, *local, norm, near_columns, far_columns, *sample)
        near = lax.optimization_barrier((swap(first, 1), swap(second, 3)))
        return normed, near, *held

    normed_0, near_0, far_columns = chunk(0, *in_hbm(weight))
    (rest_columns,) = fetch(REST, weight)
    normed_0, s_values, s_step = lax.optimization_barrier((normed_0, sample_values, s_step))
    sample = call(
        sample_kernel, "sample_outputs", (shape((16, CH), F32),) * 3,
        (sample_length, s_step, decay, skip, s_values, sample_gate, s_inject, s_read), 16, 1,
    )
    normed_1, near_1 = chunk(1, resident(far_columns))
    rest_0, rest_1 = (
        call(rest_kernel, "rest", shape((4, normed.shape[0], PIECE)), (normed, rest_columns), 24)
        for normed in (normed_0, normed_1)
    )

    def onward(near, rest):
        return call(onward_kernel, "onward", (shape(near[0].shape[1:]),) * 2, (*near, rest), 8)

    def send_on(ons):
        return lax.optimization_barrier((swap(ons[0], 3), swap(ons[1], 1)))

    def own_sum(near, rest):
        return call(own_sum_kernel, "own_sum", shape((2, *near[0].shape[1:]), F32), (*near, rest), 8)

    sample_rows = call(
        sample_rows_kernel, "sample_rows", shape((16, 4 * 1024)),
        (state, norm, *sample, near_columns, resident(far_columns), rest_columns), 16,
    )
    sample_mixed = lax.psum_scatter(sample_rows, "head", scatter_dimension=1, tiled=True)[0:2].T
    ons_0, own_0, rest_1 = lax.optimization_barrier((onward(near_0, rest_0), own_sum(near_0, rest_0), rest_1))
    far_0 = send_on(ons_0)
    far_1 = send_on(onward(near_1, rest_1))
    parts = (own_0, *far_0, own_sum(near_1, rest_1), *far_1)
    prompt_mixed = call(finish_kernel, "finish", shape((1024, TOK)), parts, 16)
    return prompt_mixed, sample_mixed


def solution(mesh):
    split = Mesh(mesh.devices.reshape(4, 4, 2, mesh.shape["head"]), ("y", "x", "core", "head"))
    return jax.shard_map(
        per_device,
        mesh=split,
        in_specs=(
            P(CTX, "head"), P(CTX, "head"), P(CTX, "head", None), P(CTX, "head", None), P("head", CTX),
            P("head"), P("head"), P("head"), P("head", None),
            P(CTX, None, "head"), P(CTX, None, "head"), P(CTX, None, "head", None), P(CTX, None, "head", None),
            P("head", CTX, None), P(CTX),
        ),
        out_specs=(P("head", CTX), P("head", CTX)),
        check_vma=False,
    )
```
